256 devices in a mesh: seq: 64 (over x, z, core), batch: 4 (over y).
Axes of the slice: x: 4, y: 4, z: 8, core: 2. Of those that a mesh axis runs over, the one named last changes fastest.
Arguments:
- inputs: float32 [8, 16384, 256], P('batch', 'seq'), may hold values from -6 to 6
- guess_path: float32 [8, 16384, 128], P('batch', 'seq'), may hold values from -3 to 3
- recur_weight: float32 [128, 128], replicated, may hold values from -0.09 to 0.09
- damping: float32 [128], replicated, may hold values from 0.00024414062 to 2.5
- in_weight: float32 [256, 128], replicated, may hold values from -0.375 to 0.375
- bias_term: float32 [128], replicated, may hold values from -3 to 3
- targets: float32 [8, 128, 128], P('batch', 'seq'), may hold values from -6 to 6
- target_steps: int32 [8, 128], P('batch', 'seq'), may hold values from 0 to 127
Outputs:
- trajectory: float32 [8, 16384, 128], P('batch', 'seq')
- grad_recur: float32 [128, 128], replicated
- grad_in: float32 [256, 128], replicated
The draws below stay inside these ranges and needn't reach their ends.
All inputs are finite; a program needn't handle non-finite values.
Results may differ from the reference program's by a relative error of at most 0.0003.
Values sent between devices are 32-bit elements; how exact they have to be, the bound alone decides.
A program may use at most 64 MiB of HBM per device.

```python
import math
import jax
import jax.numpy as jnp
from jax import lax

H = 128
DIN = 256
TBLK = 128
SEQS = 8
SEQLEN = 16384
NTB = 128


def plant(drawn, own_key, least, high):
    spot = [jax.random.randint(jax.random.fold_in(own_key, axis), (), 0, length) for axis, length in enumerate(drawn.shape)]
    longest = drawn.shape.index(max(drawn.shape))
    next_to = spot[:longest] + [(spot[longest] + 1) % drawn.shape[longest]] + spot[longest + 1:]
    return drawn.at[tuple(spot)].set(least).at[tuple(next_to)].set(high)


def block_levels(stream_key, shape, split, smallest, high):
    loudness = 1.0
    for dim, shards_of in split:
        draws = jax.random.uniform(jax.random.fold_in(jax.random.fold_in(stream_key, 6), dim), (shards_of,), jnp.float32, smallest / len(split), high / len(split))
        loudness = loudness * jnp.repeat(jnp.exp(draws), shape[dim] // shards_of).reshape((-1,) + (1,) * (len(shape) - 1 - dim))
    return loudness


def noise(key, extent, scale, bound, shards=(), kind=jnp.bfloat16):
    factor_of = block_levels(key, extent, shards, -0.22, 0.18) if shards else 1.0
    result = jax.random.normal(key, extent, jnp.float32) * scale * factor_of
    return jnp.minimum(jnp.maximum(result, -bound), bound).astype(kind)


def setup_inputs(seed: int = 0) -> dict:
    key_of = jax.random.split(jax.random.key(seed), 9)
    inputs = noise(key_of[0], (SEQS, SEQLEN, DIN), 1.0, 6.0, ((0, 4), (1, 64)), jnp.float32)
    guess_path = noise(key_of[1], (SEQS, SEQLEN, H), 0.5, 3.0, ((0, 4), (1, 64)), jnp.float32)
    recur_weight = noise(key_of[2], (H, H), 0.015, 0.09, (), jnp.float32)
    damping = jnp.clip(jnp.exp(jax.random.uniform(key_of[3], (H,), jnp.float32, math.log(0.00024414062), math.log(2.5))), 0.00024414062, 2.5)
    in_weight = noise(key_of[4], (DIN, H), DIN ** -0.5, 0.375, (), jnp.float32)
    bias_term = noise(key_of[5], (H,), 0.5, 3.0, (), jnp.float32)
    targets = noise(key_of[6], (SEQS, NTB, H), 1.0, 6.0, ((0, 4), (1, 64)), jnp.float32)
    target_steps = plant(jax.random.randint(key_of[7], (SEQS, NTB), 0, TBLK), jax.random.fold_in(key_of[7], 1), 0, TBLK - 1).astype(jnp.int32)
    return {"inputs": inputs, "guess_path": guess_path, "recur_weight": recur_weight, "damping": damping, "in_weight": in_weight, "bias_term": bias_term, "targets": targets, "target_steps": target_steps}


euler_step = 0.02


def reference(inputs, guess_path, recur_weight, damping, in_weight, bias_term, targets, target_steps):
    highest = lax.Precision.HIGHEST
    skew = recur_weight - recur_weight.T
    seq_count, step_count, hidden = guess_path.shape
    prev = jnp.concatenate([jnp.zeros((seq_count, 1, hidden), jnp.float32), guess_path[:, :-1, :]], axis=1)
    drive = jnp.einsum('stc,ch->sth', inputs, in_weight, precision=highest)
    preact = jnp.einsum('stk,hk->sth', prev, skew, precision=highest) - damping * prev + drive + bias_term
    activation = jnp.tanh(preact)
    gain = euler_step * (1.0 - activation * activation)
    resid = prev + euler_step * activation - guess_path
    gain_steps = gain.transpose(1, 0, 2)

    def forward(state, inputs_now):
        gain_now, resid_now = inputs_now
        moved = jnp.dot(state, skew.T, precision=highest) - damping * state
        state = state + gain_now * moved + resid_now
        return state, state

    zero_state = jnp.zeros((seq_count, hidden), jnp.float32)
    _, deltas = lax.scan(forward, zero_state, (gain_steps, resid.transpose(1, 0, 2)))
    trajectory = guess_path + deltas.transpose(1, 0, 2)

    block_count = step_count // TBLK
    target_hit = (jnp.arange(TBLK)[None, None, :] == target_steps[:, :, None]).astype(jnp.float32)
    miss = trajectory.reshape(seq_count, block_count, TBLK, hidden) - targets[:, :, None, :]
    source = (target_hit[..., None] * miss / seq_count).reshape(seq_count, step_count, hidden)

    def backward(carry, inputs_now):
        gain_now, source_now = inputs_now
        adjoint = source_now + carry
        scaled = gain_now * adjoint
        carry = adjoint + jnp.dot(scaled, skew, precision=highest) - damping * scaled
        return carry, adjoint

    _, adjoints = lax.scan(backward, zero_state, (gain_steps, source.transpose(1, 0, 2)), reverse=True)
    grad_pre = gain * adjoints.transpose(1, 0, 2)
    recur_sum = jnp.einsum('sti,stj->ij', grad_pre, prev, precision=highest)
    grad_in = jnp.einsum('stc,sth->ch', inputs, grad_pre, precision=highest)
    return trajectory, recur_sum - recur_sum.T, grad_in
```

```python
import jax
import jax.numpy as jnp
from jax import lax
from jax.experimental import pallas as pl
from jax.experimental.pallas import tpu as pltpu
from jax.sharding import Mesh
from jax.sharding import PartitionSpec as P

H = 128
LEN = 16
TBLK = 128
AUG = 144
LANES = 12
GROUPS = 3
GROWS = LANES * H + 16
SEQ = ("x", "z", "core")
EULER = 0.02
F32 = jnp.float32
BF16 = jnp.bfloat16
MESH = pl.DeviceIdType.MESH
VM = pl.BlockSpec(memory_space=pltpu.VMEM)
SM = pl.BlockSpec(memory_space=pltpu.SMEM)


def split(value):
    high = value.astype(BF16)
    return high, (value - high.astype(F32)).astype(BF16)


def wide(value):
    return jnp.concatenate(split(value), axis=1)


def weights(matrix):
    row = wide(matrix)
    return jnp.concatenate([row, row], axis=0)


def times(rows, packed):
    both = jnp.dot(wide(rows), packed, preferred_element_type=F32)
    return both[:, :H] + both[:, H:]


def unit():
    line = lax.broadcasted_iota(jnp.int32, (H, H), 0)
    return jnp.where(line == lax.broadcasted_iota(jnp.int32, (H, H), 1), 1.0, 0.0).astype(F32)


def rate_matrix(weight, damping):
    return weight.T - weight - unit() * damping


def shift_down(block, first):
    line = lax.broadcasted_iota(jnp.int32, block.shape, 0)
    return jnp.where(line == 0, first, pltpu.roll(block, 1, 0))


def apply_rows(rows, packed_less_unit, offset):
    return rows + times(rows, packed_less_unit) + offset


def then(earlier, later, eye):
    tail = jnp.concatenate([jnp.zeros((H, H), F32), later[H:]], axis=0)
    return earlier + times(earlier, weights(later[:H] - eye)) + tail


def local_maps(
    x_ref, guess_ref, edge_ref, w_ref, damp_ref, u_ref, bias_ref, target_ref, steps_ref,
    gain_ref, resid_ref, maps_ref, prefix_ref, dev_ref, hit_ref,
):
    count = guess_ref.shape[0]
    steps = count // 2
    eye = unit()
    rate_t = rate_matrix(w_ref[...], damp_ref[...])
    packed = weights(rate_t)
    guess = guess_ref[...]
    prev = jnp.concatenate(
        [shift_down(guess[s * steps:(s + 1) * steps], edge_ref[s:s + 1, :]) for s in range(2)], axis=0
    )
    u_pair = wide(u_ref[...])
    x_high, x_low = split(x_ref[...])
    drive = jnp.dot(x_high, u_pair, preferred_element_type=F32)
    drive = drive + jnp.dot(x_low, u_pair, preferred_element_type=F32)
    preact = times(prev, packed) + drive[:, :H] + drive[:, H:] + bias_ref[...]
    activation = jnp.tanh(preact)
    gain_ref[0:count, :] = EULER * (1.0 - activation * activation)
    resid_ref[0:count, :] = prev + EULER * activation - guess
    line = lax.broadcasted_iota(jnp.int32, (LEN, H), 0)
    for s in range(2):
        for h in range(2):
            step = steps_ref[s, h]
            base = pl.multiple_of(s * steps + h * TBLK + (step // LEN) * LEN, LEN)
            kept = line <= lax.rem(step, LEN)
            to = pl.ds(count + (2 * s + h) * LEN, LEN)
            gain_ref[to, :] = jnp.where(kept, gain_ref[pl.ds(base, LEN), :], 0.0)
            resid_ref[to, :] = jnp.where(kept, resid_ref[pl.ds(base, LEN), :], 0.0)

    tail_pad = jnp.zeros((16 - LANES, H), F32)

    def group(g, carry):
        base = g * (LANES * LEN)

        def rows_at(ref, j):
            return [ref[pl.ds(base + i * LEN + j, 1), :] for i in range(LANES)]

        gains = rows_at(gain_ref, 0)
        for i in range(LANES):
            maps_ref[g, i * H:(i + 1) * H, :] = eye + rate_t * gains[i]
        maps_ref[g, LANES * H:, :] = jnp.concatenate(rows_at(resid_ref, 0) + [tail_pad], axis=0)

        def step(j, inner):
            gains = rows_at(gain_ref, j)
            for first in range(0, LANES, 4):
                last = first + 4
                end = last * H + (16 if last == LANES else 0)
                state = maps_ref[g, first * H:end, :]
                moved = times(state, packed)
                for i in range(4):
                    here = slice(i * H, (i + 1) * H)
                    maps_ref[g, (first + i) * H:(first + i + 1) * H, :] = (
                        state[here] + gains[first + i] * moved[here]
                    )
                if last == LANES:
                    more = jnp.concatenate(gains + [tail_pad], axis=0)
                    resid = jnp.concatenate(rows_at(resid_ref, j) + [tail_pad], axis=0)
                    maps_ref[g, LANES * H:, :] = state[4 * H:] + more * moved[4 * H:] + resid
            return inner

        return lax.fori_loop(1, LEN, step, carry)

    lax.fori_loop(0, GROUPS, group, 0)

    def lane_map(lane):
        g = lane // LANES
        i = lane - g * LANES
        begin = pl.multiple_of(i * H, H)
        return maps_ref[g, pl.ds(begin, H), :], maps_ref[g, pl.ds(LANES * H + i, 1), :]

    first_row = lax.broadcasted_iota(jnp.int32, (16, H), 0) == 0

    def chain(c, carry):
        out = []
        for s in range(2):
            run = carry[s]
            prefix_ref[s, c] = run
            main, offset = lane_map(s * (steps // LEN) + c)
            moved = run + times(run, weights(main - eye))
            last = moved[H:] + jnp.where(first_row, offset, 0.0)
            out.append(jnp.concatenate([moved[:H], last], axis=0))
        return tuple(out)

    start = jnp.concatenate([eye, jnp.zeros((16, H), F32)], axis=0)
    ends = lax.fori_loop(0, steps // LEN, chain, (start, start))
    for s in range(2):
        dev_ref[s] = ends[s]
        for h in range(2):
            step = steps_ref[s, h]
            c = h * (TBLK // LEN) + step // LEN
            main, offset = lane_map(2 * (steps // LEN) + 2 * s + h)
            run = prefix_ref[s, c]
            moved = run + times(run, weights(main - eye))
            here = guess_ref[pl.ds(s * steps + h * TBLK + step, 1), :]
            miss = offset + here - target_ref[2 * s + h:2 * s + h + 1, :]
            hit_ref[2 * s + h, 0:H, :] = moved[:H]
            hit_ref[2 * s + h, H:, :] = moved[H:] + jnp.where(first_row, miss, 0.0)


def shift_copy(src, dst, sends, recvs, target):
    return pltpu.make_async_remote_copy(
        src_ref=src, dst_ref=dst, send_sem=sends, recv_sem=recvs,
        device_id=target, device_id_type=MESH,
    )


def ring_gather(buf, axis, sends, recvs):
    n = lax.axis_size(axis)
    me = lax.axis_index(axis)
    half = AUG // 2
    sides = (lax.rem(me + 1, n), lax.rem(me + n - 1, n))
    started = []
    waiting = {}
    for k in range(1, n // 2 + 1):
        for side in range(2):
            slot = lax.rem(me + n - (k - 1), n) if side == 0 else lax.rem(me + k - 1, n)
            for piece in range(2) if k < n // 2 else (side,):
                if k > 1:
                    waiting[side, piece].wait_recv()
                part = buf.at[slot, pl.ds(piece * half, half)]
                copy = shift_copy(
                    part, part, sends.at[side, k - 1, piece], recvs.at[side, k - 1, piece], {axis: sides[side]}
                )
                copy.start()
                started.append(copy)
                waiting[side, piece] = copy
    for key in waiting:
        waiting[key].wait_recv()
    return started


def swap_all(buf, axis, sends, recvs):
    n = lax.axis_size(axis)
    me = lax.axis_index(axis)
    copies = [
        shift_copy(buf.at[me], buf.at[me], sends.at[d - 1], recvs.at[d - 1], {axis: lax.rem(me + d, n)})
        for d in range(1, n)
    ]
    for copy in copies:
        copy.start()
    for copy in copies:
        copy.wait_recv()
    return copies


def lane_sum(matrix):
    ones = jnp.ones((16, 2 * H), BF16)
    return lax.dot_general(ones, wide(matrix), (((1,), (1,)), ((), ())), preferred_element_type=F32)


def bridge(
    dev_ref, hit_ref, out_ref,
    pair, hits, zbuf, ubuf, xbuf, qz, qx, tiles, result,
    core_send, core_recv, zs, zr, xs, xr, vzs, vzr, vxs, vxr,
):
    x = lax.axis_index("x")
    z = lax.axis_index("z")
    c = lax.axis_index("core")
    nx = lax.axis_size("x")
    nz = lax.axis_size("z")
    other = 1 - c
    sibling = {"core": other}
    barrier = pltpu.get_barrier_semaphore()
    pl.semaphore_signal(barrier, inc=1, device_id=sibling, device_id_type=MESH)
    for d in range(1, nz):
        pl.semaphore_signal(barrier, inc=1, device_id={"z": lax.rem(z + d, nz)}, device_id_type=MESH)
    for d in range(1, nx):
        pl.semaphore_signal(barrier, inc=1, device_id={"x": lax.rem(x + d, nx)}, device_id_type=MESH)
    pl.semaphore_wait(barrier, nz + nx - 1)

    eye = unit()
    done = []
    first = shift_copy(dev_ref.at[other], pair.at[c], core_send.at[0], core_recv.at[0], sibling)
    first.start()
    second = shift_copy(
        hit_ref.at[pl.ds(2 * other, 2)], hits.at[c], core_send.at[1], core_recv.at[1], sibling
    )
    second.start()
    pair[c] = dev_ref[c]
    hits[c] = hit_ref[pl.ds(2 * c, 2)]
    first.wait_recv()
    zbuf[z] = then(pair[0], pair[1], eye)
    done += [first, second]
    done += ring_gather(zbuf, "z", zs, zr)
    second.wait_recv()

    start = jnp.concatenate([eye, jnp.zeros((16, H), F32)], axis=0)
    run = zbuf[0]
    ahead = start
    after = eye
    for k in range(1, nz):
        ahead = jnp.where(k == z, run, ahead)
        ubuf[k] = after
        element = zbuf[k]
        moved = times(jnp.concatenate([run, after], axis=0), weights(element[:H] - eye))
        run = run + moved[:AUG] + jnp.concatenate([jnp.zeros((H, H), F32), element[H:]], axis=0)
        after = jnp.where(k > z, after + moved[AUG:], after)
    xbuf[x] = run
    done += ring_gather(xbuf, "x", xs, xr)

    late = [then(pair[0], hits[1, h], eye) for h in range(2)]
    v = jnp.where(x > 0, xbuf[0, H:], 0.0)
    for k in range(1, nx - 1):
        v = jnp.where(k < x, apply_rows(v, weights(xbuf[k, :H] - eye), xbuf[k, H:]), v)
    v = apply_rows(v, weights(ahead[:H] - eye), ahead[H:])
    v_late = apply_rows(v, weights(pair[0, :H] - eye), pair[0, H:])
    q_late = jnp.zeros((16, H), F32)
    q = jnp.zeros((16, H), F32)
    scale = 0.125
    for h in range(2):
        miss = apply_rows(v, weights(hits[0, h, :H] - eye), hits[0, h, H:]) * scale
        q = q + times(miss, weights(hits[0, h, :H].T))
        miss = apply_rows(v, weights(late[h][:H] - eye), late[h][H:]) * scale
        q = q + times(miss, weights(late[h][:H].T))
        q_late = q_late + times(miss, weights(hits[1, h, :H].T))
    q_far = times(q, weights(ahead[:H].T))
    line = lax.broadcasted_iota(jnp.int32, (8, H), 0)
    qz[z] = jnp.where(line == 0, q[0:1], q_far[0:1])
    done += swap_all(qz, "z", vzs, vzr)
    total = jnp.zeros((H, H), F32)
    q_row = jnp.zeros((8, H), F32)
    for k in range(nz):
        if k > 0:
            total = total + jnp.where(k > z, ubuf[k] * qz[k, 0:1], 0.0)
        q_row = q_row + qz[k]
    near = lane_sum(total)
    qx[x] = q_row
    done += swap_all(qx, "x", vxs, vxr)
    t = jnp.where(nx - 1 > x, jnp.broadcast_to(qx[nx - 1, 1:2], (16, H)), 0.0)
    for k in range(nx - 2, 0, -1):
        moved = t + times(t, weights((xbuf[k, :H] - eye).T)) + qx[k, 1:2]
        t = jnp.where(k > x, moved, t)
    lam_late = near + t + times(t, weights((after - eye).T))
    lam = lam_late + times(lam_late, weights((pair[1, :H] - eye).T)) + q_late[0:1]
    early_tile = jnp.where(line == 0, v[0:1], lam[0:1])
    late_tile = jnp.where(line == 0, v_late[0:1], lam_late[0:1])
    result[c] = jnp.where(c == 0, early_tile, late_tile)
    tiles[...] = jnp.where(c == 0, late_tile, early_tile)
    final = shift_copy(tiles, result.at[c], core_send.at[2], core_recv.at[2], sibling)
    final.start()
    final.wait_recv()
    done.append(final)
    out_ref[...] = result[...]
    for copy in done:
        copy.wait_send()


def sweeps(
    x_ref, guess_ref, edge_ref, w_ref, damp_ref, target_ref, steps_ref, gain_ref, resid_ref,
    maps_ref, prefix_ref, hit_ref, ends_ref,
    traj_ref, grad_ref, start_ref, carry_ref, push_ref, source_ref, pre_ref,
):
    count = guess_ref.shape[0]
    steps = count // 2
    chunks = steps // LEN
    eye = unit()
    rate_t = rate_matrix(w_ref[...], damp_ref[...])
    packed = weights(rate_t)
    packed_t = weights(rate_t.T)
    push_ref[...] = jnp.zeros(push_ref.shape, F32)
    source_ref[...] = jnp.zeros(source_ref.shape, F32)

    def lane_map(lane):
        g = lane // LANES
        i = lane - g * LANES
        return maps_ref[g, pl.ds(pl.multiple_of(i * H, H), H), :]

    for s in range(2):
        column = jnp.broadcast_to(ends_ref[s, 0:1, :], (H, H)).T
        for k in range(chunks):
            start_ref[s * chunks + k:s * chunks + k + 1, :] = (
                jnp.sum(prefix_ref[s, k, :H, :] * column, axis=0, keepdims=True) + prefix_ref[s, k, H:H + 1, :]
            )
        for h in range(2):
            n = 2 * s + h
            step = steps_ref[s, h]
            miss = jnp.sum(hit_ref[n, :H, :] * column, axis=0, keepdims=True) + hit_ref[n, H:H + 1, :]
            miss = miss * 0.125
            source_ref[pl.ds(s * steps + h * TBLK + step, 1), :] = miss
            spread = jnp.broadcast_to(miss, (16, H))
            pushed = times(spread, weights(lane_map(2 * chunks + n).T))
            push_ref[pl.ds(s * chunks + h * (TBLK // LEN) + step // LEN, 1), :] = pushed[0:1]

    def back(i, carry):
        k = chunks - 1 - i
        out = []
        for s in range(2):
            t = carry[s]
            lane = s * chunks + k
            carry_ref[pl.ds(lane, 1), :] = t[0:1]
            moved = t + times(t, weights((lane_map(lane) - eye).T))
            out.append(moved + push_ref[pl.ds(lane, 1), :])
        return tuple(out)

    ends = tuple(jnp.broadcast_to(ends_ref[s, 1:2, :], (16, H)) for s in range(2))
    lax.fori_loop(0, chunks, back, ends)

    def sweep(j, carry):
        state, adjoint = carry
        ahead = pl.ds(j, 2 * chunks, stride=LEN)
        behind = pl.ds(LEN - 1 - j, 2 * chunks, stride=LEN)
        state = state + gain_ref[ahead, :] * times(state, packed) + resid_ref[ahead, :]
        traj_ref[ahead, :] = state + guess_ref[ahead, :]
        adjoint = adjoint + source_ref[behind, :]
        scaled = gain_ref[behind, :] * adjoint
        pre_ref[behind, :] = scaled
        return state, adjoint + times(scaled, packed_t)

    lax.fori_loop(0, LEN, sweep, (start_ref[...], carry_ref[...]))
    guess = guess_ref[...]
    prev = jnp.concatenate(
        [shift_down(guess[s * steps:(s + 1) * steps], edge_ref[s:s + 1, :]) for s in range(2)], axis=0
    )
    left_high, left_low = split(jnp.concatenate([prev, x_ref[...]], axis=1))
    right = wide(pre_ref[...])
    dims = (((0,), (0,)), ((), ()))
    both = lax.dot_general(left_high, right, dims, preferred_element_type=F32)
    both = both + lax.dot_general(left_low, right, dims, preferred_element_type=F32)
    grads = both[:, :H] + both[:, H:]
    grad_ref[0:H, :] = grads[:H].T - grads[:H]
    grad_ref[H:, :] = grads[H:]


def grad_sum(in_ref, out_ref, parts, shares, whole, send1, recv1, send2, recv2, send3, recv3):
    x = lax.axis_index("x")
    y = lax.axis_index("batch")
    z = lax.axis_index("z")
    c = lax.axis_index("core")
    nx, ny, nz, nc = (lax.axis_size(name) for name in ("x", "batch", "z", "core"))
    plane, column = nx * ny, nz * nc
    tiles = in_ref.shape[0] // plane
    p = x * ny + y
    q = z * nc + c
    planes = [lax.rem(p + d, plane) for d in range(1, plane)]
    columns = [lax.rem(q + d, column) for d in range(1, column)]
    plane_ids = [{"x": other // ny, "batch": lax.rem(other, ny)} for other in planes]
    column_ids = [{"z": other // nc, "core": lax.rem(other, nc)} for other in columns]
    barrier = pltpu.get_barrier_semaphore()
    for target in plane_ids + column_ids:
        pl.semaphore_signal(barrier, inc=1, device_id=target, device_id_type=MESH)
    pl.semaphore_wait(barrier, plane + column - 2)
    done = []
    for i in range(plane - 1):
        done.append(shift_copy(
            in_ref.at[pl.ds(planes[i] * tiles, tiles)], parts.at[p], send1.at[i], recv1.at[i], plane_ids[i]
        ))
        done[-1].start()
    parts[p] = in_ref[pl.ds(p * tiles, tiles)]
    for copy in done:
        copy.wait_recv()
    shares[q] = jnp.sum(parts[...], axis=0)
    exchange = [
        shift_copy(shares.at[q], shares.at[q], send2.at[i], recv2.at[i], column_ids[i])
        for i in range(column - 1)
    ]
    for copy in exchange:
        copy.start()
    for copy in exchange:
        copy.wait_recv()
    mine = pl.ds(p * tiles, tiles)
    whole[mine] = jnp.sum(shares[...], axis=0)
    last = [
        shift_copy(whole.at[mine], whole.at[mine], send3.at[i], recv3.at[i], plane_ids[i])
        for i in range(plane - 1)
    ]
    for copy in last:
        copy.start()
    for copy in last:
        copy.wait_recv()
    out_ref[...] = whole[...]
    for copy in done + exchange + last:
        copy.wait_send()


def vmem(*dims):
    return pltpu.VMEM(dims, F32)


def out(*dims):
    return jax.ShapeDtypeStruct(dims, F32)


def on_device(inputs, guess_path, recur_weight, damping, in_weight, bias_term, targets, target_steps):
    seqs, steps, hidden = guess_path.shape
    count = seqs * steps
    chunks = steps // LEN
    nx, nz, nc, ny = (lax.axis_size(name) for name in ("x", "z", "core", "batch"))
    devices = nx * nz * nc
    edge = lax.ppermute(guess_path[:, steps - 1, :], SEQ, [(i, i + 1) for i in range(devices - 1)])
    x = inputs.reshape(count, -1)
    guess = guess_path.reshape(count, hidden)
    damp = damping.reshape(1, hidden)
    target = targets.reshape(-1, hidden)
    extra = count + 4 * LEN
    big = pltpu.CompilerParams(vmem_limit_bytes=48 * 1024 * 1024)
    gain, resid, maps, prefix, dev, hit = pl.pallas_call(
        local_maps,
        out_shape=(
            out(extra, hidden), out(extra, hidden), out(GROUPS, GROWS, hidden),
            out(seqs, chunks, AUG, hidden), out(seqs, AUG, hidden), out(2 * seqs, AUG, hidden),
        ),
        in_specs=[VM] * 8 + [SM],
        out_specs=[VM] * 6,
        compiler_params=big,
        name="local_maps",
    )(x, guess, edge, recur_weight, damp, in_weight, bias_term.reshape(1, hidden), target, target_steps)
    dma = pltpu.SemaphoreType.DMA
    ends = pl.pallas_call(
        bridge,
        out_shape=out(seqs, 8, hidden),
        in_specs=[VM] * 2,
        out_specs=VM,
        scratch_shapes=[
            vmem(2, AUG, hidden), vmem(2, 2, AUG, hidden), vmem(nz, AUG, hidden), vmem(nz, hidden, hidden),
            vmem(nx, AUG, hidden), vmem(nz, 8, hidden), vmem(nx, 8, hidden), vmem(8, hidden), vmem(2, 8, hidden),
            dma((3,)), dma((3,)), dma((2, nz // 2, 2)), dma((2, nz // 2, 2)), dma((2, nx // 2, 2)),
            dma((2, nx // 2, 2)), dma((nz - 1,)), dma((nz - 1,)), dma((nx - 1,)), dma((nx - 1,)),
        ],
        compiler_params=pltpu.CompilerParams(
            collective_id=0, has_side_effects=True, vmem_limit_bytes=32 * 1024 * 1024
        ),
        name="bridge",
    )(dev, hit)
    traj, grads = pl.pallas_call(
        sweeps,
        out_shape=(out(count, hidden), out(3 * hidden, hidden)),
        in_specs=[VM] * 6 + [SM] + [VM] * 6,
        out_specs=[VM] * 2,
        scratch_shapes=[
            vmem(2 * chunks, hidden), vmem(2 * chunks, hidden), vmem(2 * chunks, hidden),
            vmem(count, hidden), vmem(count, hidden),
        ],
        compiler_params=big,
        name="sweeps",
    )(x, guess, edge, recur_weight, damp, target, target_steps, gain, resid, maps, prefix, hit, ends)
    plane, column = nx * ny, nz * nc
    tiles = 3 * hidden // 8 // plane
    whole = pl.pallas_call(
        grad_sum,
        out_shape=out(3 * hidden // 8, 8, hidden),
        in_specs=[VM],
        out_specs=VM,
        scratch_shapes=[
            vmem(plane, tiles, 8, hidden), vmem(column, tiles, 8, hidden), vmem(3 * hidden // 8, 8, hidden),
            dma((plane - 1,)), dma((plane - 1,)), dma((column - 1,)), dma((column - 1,)),
            dma((plane - 1,)), dma((plane - 1,)),
        ],
        compiler_params=pltpu.CompilerParams(
            collective_id=1, has_side_effects=True, vmem_limit_bytes=16 * 1024 * 1024
        ),
        name="grad_sum",
    )(grads.reshape(-1, 8, hidden))
    whole = whole.reshape(3 * hidden, hidden)
    return traj.reshape(guess_path.shape), whole[:hidden], whole[hidden:]


def solution(mesh):
    torus = Mesh(mesh.devices.reshape(4, 8, 2, mesh.shape["batch"]), (*SEQ, "batch"))
    return jax.shard_map(
        on_device,
        mesh=torus,
        in_specs=(
            P("batch", SEQ, None), P("batch", SEQ, None), P(), P(), P(), P(), P("batch", SEQ, None), P("batch", SEQ),
        ),
        out_specs=(P("batch", SEQ, None), P(), P()),
        check_vma=False,
    )
```

```python
import jax
import jax.numpy as jnp
from jax import lax
from jax.experimental import pallas as pl
from jax.experimental.pallas import tpu as pltpu
from jax.sharding import Mesh
from jax.sharding import PartitionSpec as P

H = 128
LEN = 16
TBLK = 128
AUG = 144
SENT = 136
SEQ = ("x", "z", "core")
EULER = 0.02
F32 = jnp.float32
BF16 = jnp.bfloat16
MESH = pl.DeviceIdType.MESH
VM = pl.BlockSpec(memory_space=pltpu.VMEM)
HBM = pl.BlockSpec(memory_space=pl.ANY)


def split(value):
    high = value.astype(BF16)
    return high, (value - high.astype(F32)).astype(BF16)


def wide(value):
    return jnp.concatenate(split(value), axis=1)


def weights(matrix):
    row = wide(matrix)
    return jnp.concatenate([row, row], axis=0)


def times(rows, packed):
    both = jnp.dot(wide(rows), packed, preferred_element_type=F32)
    return both[:, :H] + both[:, H:]


def unit():
    line = lax.broadcasted_iota(jnp.int32, (H, H), 0)
    return jnp.where(line == lax.broadcasted_iota(jnp.int32, (H, H), 1), 1.0, 0.0).astype(F32)


def rate_matrix(weight, damping):
    return weight.T - weight - unit() * damping


def shift_down(block, first):
    line = lax.broadcasted_iota(jnp.int32, block.shape, 0)
    return jnp.where(line == 0, first, pltpu.roll(block, 1, 0))


def tail_of(rows):
    return jnp.concatenate([rows, jnp.zeros((8, H), F32)], axis=0)


def then(earlier, later, offset, eye):
    moved = earlier + times(earlier, weights(later - eye))
    return jnp.concatenate([moved[:H], moved[H:] + offset], axis=0)


def remote(src, dst, sends, recvs, target):
    return pltpu.make_async_remote_copy(
        src_ref=src, dst_ref=dst, send_sem=sends, recv_sem=recvs,
        device_id=target, device_id_type=MESH,
    )


def swap_copies(buf, axis, sends, recvs, rows):
    n = lax.axis_size(axis)
    me = lax.axis_index(axis)
    part = buf.at[me, pl.ds(0, rows)]
    return [
        remote(part, part, sends.at[d - 1], recvs.at[d - 1], {axis: lax.rem(me + d, n)}) for d in range(1, n)
    ]


def lane_sum(matrix):
    ones = jnp.ones((16, 2 * H), BF16)
    return lax.dot_general(ones, wide(matrix), (((1,), (1,)), ((), ())), preferred_element_type=F32)


def newton(
    x_hbm, guess_hbm, w_hbm, damp_hbm, u_hbm, bias_hbm, target_hbm, steps_hbm,
    traj_hbm, recur_ref, gin_ref,
    x_ref, guess_ref, w_ref, damp_ref, u_ref, bias_ref, target_ref, steps_ref, load_sem,
    edge, gain_ref, resid_ref, offs_ref, maps_ref, tree, totals, prefix, suffix, turned,
    pair, hit_ref, hits, zbuf, ubuf, xbuf, qz, qx, tiles, ends,
    start_ref, carry_ref, push_ref, source_ref, pre_ref, traj_ref,
    grads, parts, shares, whole,
    edge_send, edge_recv, core_send, core_recv, zs, zr, xs, xr, vzs, vzr, vxs, vxr,
    send1, recv1, send2, recv2, send3, recv3,
):
    x, y, z, c = (lax.axis_index(name) for name in ("x", "batch", "z", "core"))
    nx, ny, nz, nc = (lax.axis_size(name) for name in ("x", "batch", "z", "core"))
    count = guess_ref.shape[0]
    steps = count // 2
    chunks = steps // LEN
    lanes = 2 * chunks
    blocks = TBLK // LEN

    loads = [
        pltpu.make_async_copy(src, dst, load_sem.at[i])
        for i, (src, dst) in enumerate((
            (w_hbm, w_ref), (damp_hbm, damp_ref), (guess_hbm, guess_ref), (u_hbm, u_ref), (x_hbm, x_ref),
            (bias_hbm, bias_ref), (target_hbm, target_ref), (steps_hbm, steps_ref),
        ))
    ]
    for load in loads:
        load.start()

    other = 1 - c
    sibling = {"core": other}
    plane, column = nx * ny, nz * nc
    p = x * ny + y
    q = z * nc + c
    planes = [lax.rem(p + d, plane) for d in range(1, plane)]
    columns = [lax.rem(q + d, column) for d in range(1, column)]
    plane_ids = [{"x": mate // ny, "batch": lax.rem(mate, ny)} for mate in planes]
    column_ids = [{"z": mate // nc, "core": lax.rem(mate, nc)} for mate in columns]
    place = x * column + q

    def along(where):
        return {"x": where // column, "z": lax.rem(where // nc, nz), "core": lax.rem(where, nc)}

    following = along(lax.rem(place + 1, nx * column))
    preceding = along(lax.rem(place + nx * column - 1, nx * column))
    barrier = pltpu.get_barrier_semaphore()
    greeted = plane_ids + column_ids + [following, preceding]
    for target in greeted:
        pl.semaphore_signal(barrier, inc=1, device_id=target, device_id_type=MESH)

    eye = unit()
    loads[0].wait()
    loads[1].wait()
    rate_t = rate_matrix(w_ref[...], damp_ref[...])
    packed = weights(rate_t)
    for load in loads[2:]:
        load.wait()
    guess = guess_ref[...]

    def prev_rows(firsts):
        return jnp.concatenate(
            [shift_down(guess_ref[s * steps:(s + 1) * steps, :], firsts[s]) for s in range(2)], axis=0
        )

    zero_row = jnp.zeros((1, H), F32)
    u_pair = wide(u_ref[...])
    x_high, x_low = split(x_ref[...])
    drive = jnp.dot(x_high, u_pair, preferred_element_type=F32)
    drive = drive + jnp.dot(x_low, u_pair, preferred_element_type=F32)
    prev = prev_rows([zero_row, zero_row])
    preact = times(prev, packed) + drive[:, :H] + drive[:, H:] + bias_ref[...]
    activation = jnp.tanh(preact)
    gain_ref[0:count, :] = EULER * (1.0 - activation * activation)
    resid_ref[0:count, :] = prev + EULER * activation - guess
    early_preact = [preact[s * steps:s * steps + 1] for s in range(2)]

    pl.semaphore_wait(barrier, len(greeted))
    edge_copies = [
        remote(guess_ref.at[pl.ds((s + 1) * steps - 8, 8)], edge.at[s], edge_send.at[s], edge_recv.at[s], following)
        for s in range(2)
    ]
    for copy in edge_copies:
        copy.start()

    chunk_line = lax.broadcasted_iota(jnp.int32, (LEN, H), 0)

    def begin(s):
        gains = jnp.where(chunk_line == 0, 0.0, gain_ref[pl.ds(s * steps, chunks, stride=LEN), :])
        for k in range(chunks):
            maps_ref[s * chunks + k] = eye + rate_t * gains[k:k + 1]
        offs_ref[s * chunks:(s + 1) * chunks, :] = jnp.where(
            chunk_line == 0, 0.0, resid_ref[pl.ds(s * steps, chunks, stride=LEN), :]
        )

    def step_maps(base, size, gains, resid):
        for first in range(0, size, 4):
            state = maps_ref[base + first:base + first + 4].reshape(4 * H, H)
            if first + 4 == size:
                state = jnp.concatenate([state, offs_ref[base:base + 16, :]], axis=0)
            moved = times(state, packed)
            for i in range(4):
                here = slice(i * H, (i + 1) * H)
                maps_ref[base + first + i] = state[here] + gains[first + i:first + i + 1] * moved[here]
            if first + 4 == size:
                offs_ref[base:base + 16, :] = state[4 * H:] + gains * moved[4 * H:] + resid

    def compose(s, begin_at, end_at):
        def body(i, carry):
            for u in range(3):
                j = 1 + 3 * i + u
                rows = pl.ds(s * steps + j, chunks, stride=LEN)
                step_maps(s * chunks, chunks, gain_ref[rows, :], resid_ref[rows, :])
            return carry

        lax.fori_loop(begin_at, end_at, body, 0)

    first_row = chunk_line == 0

    def offset_of(lane):
        return jnp.where(first_row, offs_ref[pl.ds(lane, 1), :], 0.0)

    def lane_rows(lane):
        return jnp.concatenate([maps_ref[lane], offset_of(lane)], axis=0)

    def finish(s):
        lane = s * chunks
        gain = gain_ref[s * steps:s * steps + 1, :]
        resid = jnp.where(first_row, resid_ref[s * steps:s * steps + 1, :], 0.0)
        step = jnp.concatenate([eye + rate_t * gain, resid], axis=0)
        whole_chunk = then(step, maps_ref[lane], offset_of(lane), eye)
        maps_ref[lane] = whole_chunk[:H]
        offs_ref[lane:lane + 1, :] = whole_chunk[H:H + 1]
        for k in range(chunks // 2):
            tree[k] = then(lane_rows(lane + 2 * k), maps_ref[lane + 2 * k + 1], offset_of(lane + 2 * k + 1), eye)
        size = chunks // 2
        while size > 1:
            for k in range(size // 2):
                joined = then(tree[2 * k], tree[2 * k + 1, :H, :], tree[2 * k + 1, H:, :], eye)
                if size == 2:
                    totals[s] = joined
                else:
                    tree[k] = joined
            size //= 2

    core_copy = remote(
        totals.at[other, pl.ds(0, SENT)], pair.at[c, pl.ds(0, SENT)], core_send.at[0], core_recv.at[0], sibling
    )
    z_copies = swap_copies(zbuf, "z", zs, zr, SENT)

    def leave():
        core_copy.wait_recv()
        pair[c] = totals[c]
        zbuf[z] = then(
            jnp.concatenate([pair[0, :H, :], tail_of(pair[0, H:SENT, :])], axis=0),
            pair[1, :H, :], tail_of(pair[1, H:SENT, :]), eye,
        )
        for copy in z_copies:
            copy.start()

    begin(0)
    begin(1)
    compose(0, 0, (LEN - 1) // 3)
    for copy in edge_copies:
        copy.wait_recv()
    at_start = jnp.where(place > 0, 1.0, 0.0)
    firsts = [edge[s, 7:8, :] * at_start for s in range(2)]
    added = times(jnp.concatenate(firsts + [jnp.zeros((14, H), F32)], axis=0), packed)
    for s in range(2):
        row = slice(s * steps, s * steps + 1)
        activation = jnp.tanh(early_preact[s] + added[s:s + 1])
        gain_ref[row, :] = EULER * (1.0 - activation * activation)
        resid_ref[row, :] = firsts[s] + EULER * activation - guess_ref[row, :]
    finish(0)

    @pl.when(c == 1)
    def _():
        core_copy.start()

    compose(1, 0, 2)

    @pl.when(c == 0)
    def _():
        leave()

    compose(1, 2, (LEN - 1) // 3)
    finish(1)

    @pl.when(c == 0)
    def _():
        core_copy.start()

    for s in range(2):
        for h in range(2):
            n = 2 * s + h
            step = steps_ref[s, h]
            kept = chunk_line <= lax.rem(step, LEN)
            to = slice(count + n * LEN, count + (n + 1) * LEN)
            for ref in (gain_ref, resid_ref):
                rows = jnp.zeros((LEN, H), F32)
                for k in range(blocks):
                    base = s * steps + h * TBLK + k * LEN
                    rows = jnp.where(chunk_line * 0 + step // LEN == k, ref[base:base + LEN, :], rows)
                ref[to, :] = jnp.where(kept, rows, 0.0)
    hit_pad = jnp.zeros((12, H), F32)

    def hit_rows(ref, j):
        return jnp.concatenate([ref[pl.ds(count + j, 4, stride=LEN), :], hit_pad], axis=0)

    gains = hit_rows(gain_ref, 0)
    for n in range(4):
        maps_ref[lanes + n] = eye + rate_t * gains[n:n + 1]
    offs_ref[lanes:lanes + 16, :] = hit_rows(resid_ref, 0)

    def compose_hits(begin_at, end_at):
        def body(i, carry):
            for u in range(3):
                j = 1 + 3 * i + u
                step_maps(lanes, 4, hit_rows(gain_ref, j), hit_rows(resid_ref, j))
            return carry

        lax.fori_loop(begin_at, end_at, body, 0)

    compose_hits(0, 2)

    @pl.when(c == 1)
    def _():
        leave()

    compose_hits(2, (LEN - 1) // 3)

    start = jnp.concatenate([eye, jnp.zeros((16, H), F32)], axis=0)

    def chain(k, carry):
        out = []
        for s in range(2):
            lane = s * chunks + k
            prefix[lane] = carry[s]
            out.append(then(carry[s], maps_ref[lane], offset_of(lane), eye))
        return tuple(out)

    lax.fori_loop(0, chunks, chain, (start, start))
    block_line = lax.broadcasted_iota(jnp.int32, (TBLK, H), 0)
    map_line = jnp.zeros((AUG, H), jnp.int32)
    for s in range(2):
        for h in range(2):
            n = 2 * s + h
            step = steps_ref[s, h]
            run = jnp.zeros((AUG, H), F32)
            for k in range(blocks):
                run = jnp.where(map_line + step // LEN == k, prefix[s * chunks + h * blocks + k], run)
            base = s * steps + h * TBLK
            here = jnp.where(block_line == step, guess_ref[base:base + TBLK, :], 0.0)
            miss = offs_ref[lanes + n:lanes + n + 1, :] + jnp.sum(here, axis=0, keepdims=True)
            miss = miss - target_ref[n:n + 1, :]
            hit_ref[n] = then(run, maps_ref[lanes + n], jnp.where(first_row, miss, 0.0), eye)
    hit_copy = remote(
        hit_ref.at[pl.ds(2 * other, 2)], hits.at[c], core_send.at[1], core_recv.at[1], sibling
    )
    hit_copy.start()
    hits[c] = hit_ref[pl.ds(2 * c, 2)]

    def back_chain(i, carry):
        k = chunks - 1 - i
        out = []
        for s in range(2):
            lane = s * chunks + k
            suffix[lane] = carry[s]
            turn = weights((maps_ref[lane] - eye).T)
            turned[lane] = turn
            out.append(carry[s] + times(carry[s], turn))
        return tuple(out)

    lax.fori_loop(0, chunks, back_chain, (eye, eye))

    for copy in z_copies:
        copy.wait_recv()
    run = jnp.concatenate([zbuf[0, :H, :], tail_of(zbuf[0, H:SENT, :])], axis=0)
    ahead = start
    after = eye
    for k in range(1, nz):
        ahead = jnp.where(k == z, run, ahead)
        ubuf[k] = after
        moved = times(jnp.concatenate([run, after], axis=0), weights(zbuf[k, :H, :] - eye))
        offset = tail_of(zbuf[k, H:SENT, :])
        run = run + moved[:AUG] + jnp.concatenate([jnp.zeros((H, H), F32), offset], axis=0)
        after = jnp.where(k > z, after + moved[AUG:], after)
    xbuf[x] = run
    inner = jnp.logical_and(x > 0, x < nx - 1)

    def x_copy(slot, full, d):
        part = xbuf.at[slot, pl.ds(0, SENT) if full else pl.ds(H, 8)]
        return remote(part, part, xs.at[d - 1], xr.at[d - 1], {"x": lax.rem(x + d, nx)})

    def x_copies(slot, full):
        return [x_copy(slot, full, d) for d in range(1, nx)]

    @pl.when(inner)
    def _():
        for copy in x_copies(x, True):
            copy.start()

    @pl.when(jnp.logical_not(inner))
    def _():
        for copy in x_copies(x, False):
            copy.start()

    hit_copy.wait_recv()
    first_map = jnp.concatenate([pair[0, :H, :], tail_of(pair[0, H:SENT, :])], axis=0)
    late = [then(first_map, hits[1, h, :H, :], hits[1, h, H:, :], eye) for h in range(2)]
    w_ahead = weights(ahead[:H] - eye)
    w_first = weights(pair[0, :H, :] - eye)
    w_hits = [weights(hits[0, h, :H, :] - eye) for h in range(2)] + [weights(late[h][:H] - eye) for h in range(2)]
    t_hits = [weights(hits[0, h, :H, :].T) for h in range(2)] + [weights(late[h][:H].T) for h in range(2)]
    t_late = [weights(hits[1, h, :H, :].T) for h in range(2)]
    t_ahead = weights(ahead[:H].T)
    miss_rows = [hits[0, h, H:, :] for h in range(2)] + [late[h][H:] for h in range(2)]

    for d in range(1, nx):
        source = lax.rem(x + nx - d, nx)
        source_inner = jnp.logical_and(source > 0, source < nx - 1)

        @pl.when(source_inner)
        def _():
            x_copy(source, True, d).wait_recv()

        @pl.when(jnp.logical_not(source_inner))
        def _():
            x_copy(source, False, d).wait_recv()

    v = jnp.where(x > 0, tail_of(xbuf[0, H:SENT, :]), 0.0)
    for k in range(1, nx - 1):
        moved = v + times(v, weights(xbuf[k, :H, :] - eye)) + tail_of(xbuf[k, H:SENT, :])
        v = jnp.where(k < x, moved, v)
    v = v + times(v, w_ahead) + ahead[H:]
    scale = 0.125
    misses = [(v + times(v, w_hits[i]) + miss_rows[i]) * scale for i in range(4)]
    pull = jnp.zeros((16, H), F32)
    for i in range(4):
        pull = pull + times(misses[i], t_hits[i])
    far = times(pull, t_ahead)
    line = lax.broadcasted_iota(jnp.int32, (8, H), 0)
    qz[z] = jnp.where(line == 0, pull[0:1], far[0:1])
    vz_copies = swap_copies(qz, "z", vzs, vzr, 8)
    for copy in vz_copies:
        copy.start()
    v_late = v + times(v, w_first) + tail_of(pair[0, H:SENT, :])
    ends[0, c] = jnp.where(c == 0, v[:8], v_late[:8])
    tiles[0] = jnp.where(c == 0, v_late[:8], v[:8])
    delta_copy = remote(tiles.at[0], ends.at[0, c], core_send.at[2], core_recv.at[2], sibling)
    delta_copy.start()
    pull_late = times(misses[2], t_late[0]) + times(misses[3], t_late[1])
    delta_copy.wait_recv()

    lane_line = lax.broadcasted_iota(jnp.int32, (lanes, H), 0)
    pushes = jnp.zeros((lanes, H), F32)
    columns_d = [jnp.broadcast_to(ends[0, s, 0:1, :], (H, H)).T for s in range(2)]
    for s in range(2):
        for h in range(2):
            n = 2 * s + h
            step = steps_ref[s, h]
            miss = jnp.sum(hit_ref[n, :H, :] * columns_d[s], axis=0, keepdims=True) + hit_ref[n, H:H + 1, :]
            miss = miss * scale
            source_ref[s * steps + h * TBLK:s * steps + (h + 1) * TBLK, :] = jnp.where(block_line == step, miss, 0.0)
            pushed = times(jnp.broadcast_to(miss, (16, H)), weights(maps_ref[lanes + n].T))
            pushes = pushes + jnp.where(lane_line == s * chunks + h * blocks + step // LEN, pushed[0:1], 0.0)
    push_ref[...] = pushes

    def spread(table, columns, k, s):
        lane = s * chunks + k
        return jnp.sum(table[lane, :H, :] * columns[s], axis=0, keepdims=True)

    def starts(k, carry):
        for s in range(2):
            lane = s * chunks + k
            start_ref[pl.ds(lane, 1), :] = spread(prefix, columns_d, k, s) + prefix[lane, H:H + 1, :]
        return carry

    lax.fori_loop(0, chunks, starts, 0)

    def forward(j, carry):
        state, back0, back1 = carry
        rows = pl.ds(j, lanes, stride=LEN)
        k = chunks - 1 - j
        out = []
        for s, t in enumerate((back0, back1)):
            lane = s * chunks + k
            carry_ref[pl.ds(lane, 1), :] = t[0:1]
            out.append(t + times(t, turned[lane]) + push_ref[pl.ds(lane, 1), :])
        state = state + gain_ref[rows, :] * times(state, packed) + resid_ref[rows, :]
        traj_ref[rows, :] = state + guess_ref[rows, :]
        return state, out[0], out[1]

    nothing = jnp.zeros((16, H), F32)
    lax.fori_loop(0, LEN, forward, (start_ref[...], nothing, nothing))
    traj_copy = pltpu.make_async_copy(traj_ref, traj_hbm, load_sem.at[0])
    traj_copy.start()
    t_first = weights((pair[1, :H, :] - eye).T)
    t_after = weights((after - eye).T)
    t_rows = {k: weights((xbuf[k, :H, :] - eye).T) for k in range(1, nx - 1)}

    for copy in vz_copies:
        copy.wait_recv()
    total = jnp.zeros((H, H), F32)
    q_row = jnp.zeros((8, H), F32)
    for k in range(nz):
        if k > 0:
            total = total + jnp.where(k > z, ubuf[k] * qz[k, 0:1, :], 0.0)
        q_row = q_row + qz[k]
    qx[x] = q_row
    vx_copies = swap_copies(qx, "x", vxs, vxr, 8)
    for copy in vx_copies:
        copy.start()
    summed = lane_sum(total)
    near = summed[:, :H]
    for copy in vx_copies:
        copy.wait_recv()
    t = jnp.where(nx - 1 > x, jnp.broadcast_to(qx[nx - 1, 1:2, :], (16, H)), 0.0)
    for k in range(nx - 2, 0, -1):
        t = jnp.where(k > x, t + times(t, t_rows[k]) + qx[k, 1:2, :], t)
    lam_late = near + t + times(t, t_after)
    lam = lam_late + times(lam_late, t_first) + pull_late
    ends[1, c] = jnp.where(c == 0, lam[:8], lam_late[:8])
    tiles[1] = jnp.where(c == 0, lam_late[:8], lam[:8])
    lam_copy = remote(tiles.at[1], ends.at[1, c], core_send.at[3], core_recv.at[3], sibling)
    lam_copy.start()
    packed_t = weights(rate_t.T)
    lam_copy.wait_recv()
    columns_l = [jnp.broadcast_to(ends[1, s, 0:1, :], (H, H)).T for s in range(2)]

    def carries(k, carry):
        for s in range(2):
            lane = pl.ds(s * chunks + k, 1)
            carry_ref[lane, :] = carry_ref[lane, :] + spread(suffix, columns_l, k, s)
        return carry

    lax.fori_loop(0, chunks, carries, 0)

    def backward(j, adjoint):
        rows = pl.ds(LEN - 1 - j, lanes, stride=LEN)
        adjoint = adjoint + source_ref[rows, :]
        scaled = gain_ref[rows, :] * adjoint
        pre_ref[rows, :] = scaled
        return adjoint + times(scaled, packed_t)

    lax.fori_loop(0, LEN, backward, carry_ref[...])
    left_high, left_low = split(jnp.concatenate([prev_rows([edge[s, 7:8, :] * at_start for s in range(2)]), x_ref[...]], axis=1))
    right = wide(pre_ref[...])
    dims = (((0,), (0,)), ((), ()))
    both = lax.dot_general(left_high, right, dims, preferred_element_type=F32)
    both = both + lax.dot_general(left_low, right, dims, preferred_element_type=F32)
    sums = both[:, :H] + both[:, H:]
    grads[0:H // 8] = (sums[:H].T - sums[:H]).reshape(H // 8, 8, H)
    grads[H // 8:] = sums[H:].reshape(2 * H // 8, 8, H)

    share = grads.shape[0] // plane
    done = []
    for i in range(plane - 1):
        done.append(remote(
            grads.at[pl.ds(planes[i] * share, share)], parts.at[p], send1.at[i], recv1.at[i], plane_ids[i]
        ))
        done[-1].start()
    parts[p] = grads[pl.ds(p * share, share)]
    for copy in done:
        copy.wait_recv()
    shares[q] = jnp.sum(parts[...], axis=0)
    exchange = [
        remote(shares.at[q], shares.at[q], send2.at[i], recv2.at[i], column_ids[i]) for i in range(column - 1)
    ]
    for copy in exchange:
        copy.start()
    for copy in exchange:
        copy.wait_recv()
    mine = pl.ds(p * share, share)
    whole[mine] = jnp.sum(shares[...], axis=0)
    last = [
        remote(whole.at[mine], whole.at[mine], send3.at[i], recv3.at[i], plane_ids[i]) for i in range(plane - 1)
    ]
    for copy in last:
        copy.start()

    @pl.when(inner)
    def _():
        for copy in x_copies(x, True):
            copy.wait_send()

    @pl.when(jnp.logical_not(inner))
    def _():
        for copy in x_copies(x, False):
            copy.wait_send()

    traj_copy.wait()
    early = edge_copies + [core_copy, hit_copy, delta_copy, lam_copy] + z_copies + vz_copies + vx_copies
    for copy in early + done + exchange:
        copy.wait_send()
    for copy in last:
        copy.wait_recv()
    recur_ref[...] = whole[0:H // 8].reshape(H, H)
    gin_ref[...] = whole[H // 8:].reshape(2 * H, H)
    for copy in last:
        copy.wait_send()


def vmem(*dims):
    return pltpu.VMEM(dims, F32)


def out(*dims):
    return jax.ShapeDtypeStruct(dims, F32)


def on_device(inputs, guess_path, recur_weight, damping, in_weight, bias_term, targets, target_steps):
    seqs, steps, hidden = guess_path.shape
    features = inputs.shape[2]
    count = seqs * steps
    chunks = steps // LEN
    lanes = seqs * chunks
    nx, nz, nc, ny = (lax.axis_size(name) for name in ("x", "z", "core", "batch"))
    plane, column = nx * ny, nz * nc
    tiles = 3 * hidden // 8
    share = tiles // plane
    extra = count + 4 * LEN
    dma = pltpu.SemaphoreType.DMA
    traj, grad_recur, grad_in = pl.pallas_call(
        newton,
        out_shape=(out(count, hidden), out(hidden, hidden), out(features, hidden)),
        in_specs=[HBM] * 8,
        out_specs=[HBM, VM, VM],
        scratch_shapes=[
            vmem(count, features), vmem(count, hidden), vmem(hidden, hidden), vmem(1, hidden),
            vmem(features, hidden), vmem(1, hidden), vmem(4, hidden), pltpu.SMEM((seqs, 2), jnp.int32), dma((8,)),
            vmem(seqs, 8, hidden), vmem(extra, hidden), vmem(extra, hidden), vmem(lanes + 16, hidden),
            vmem(lanes + 4, hidden, hidden), vmem(chunks // 2, AUG, hidden), vmem(seqs, AUG, hidden),
            vmem(lanes, AUG, hidden), vmem(lanes, hidden, hidden), pltpu.VMEM((lanes, 2 * hidden, 2 * hidden), BF16),
            vmem(2, AUG, hidden), vmem(4, AUG, hidden), vmem(2, 2, AUG, hidden), vmem(nz, AUG, hidden),
            vmem(nz, hidden, hidden), vmem(nx, AUG, hidden), vmem(nz, 8, hidden), vmem(nx, 8, hidden),
            vmem(2, 8, hidden), vmem(2, seqs, 8, hidden),
            vmem(lanes, hidden), vmem(lanes, hidden), vmem(lanes, hidden), vmem(count, hidden), vmem(count, hidden),
            vmem(count, hidden),
            vmem(tiles, 8, hidden), vmem(plane, share, 8, hidden), vmem(column, share, 8, hidden), vmem(tiles, 8, hidden),
            dma((2,)), dma((2,)), dma((4,)), dma((4,)), dma((nz - 1,)), dma((nz - 1,)), dma((nx - 1,)), dma((nx - 1,)),
            dma((nz - 1,)), dma((nz - 1,)), dma((nx - 1,)), dma((nx - 1,)),
            dma((plane - 1,)), dma((plane - 1,)), dma((column - 1,)), dma((column - 1,)), dma((plane - 1,)),
            dma((plane - 1,)),
        ],
        compiler_params=pltpu.CompilerParams(
            collective_id=0, has_side_effects=True, vmem_limit_bytes=63 * 1024 * 1024
        ),
        name="newton",
    )(
        inputs.reshape(count, features), guess_path.reshape(count, hidden), recur_weight, damping.reshape(1, hidden),
        in_weight, bias_term.reshape(1, hidden), targets.reshape(-1, hidden), target_steps,
    )
    return traj.reshape(guess_path.shape), grad_recur, grad_in


def solution(mesh):
    torus = Mesh(mesh.devices.reshape(4, 8, 2, mesh.shape["batch"]), (*SEQ, "batch"))
    return jax.shard_map(
        on_device,
        mesh=torus,
        in_specs=(
            P("batch", SEQ, None), P("batch", SEQ, None), P(), P(), P(), P(), P("batch", SEQ, None), P("batch", SEQ),
        ),
        out_specs=(P("batch", SEQ, None), P(), P()),
        check_vma=False,
    )
```

```python
import jax
import jax.numpy as jnp
from jax import lax
from jax.experimental import pallas as pl
from jax.experimental.pallas import tpu as pltpu
from jax.sharding import Mesh
from jax.sharding import PartitionSpec as P

H = 128
LEN = 16
TBLK = 128
AUG = 144
SENT = 136
DEPTH = 5
SEQ = ("x", "z", "core")
EULER = 0.02
F32 = jnp.float32
BF16 = jnp.bfloat16
MESH = pl.DeviceIdType.MESH
VM = pl.BlockSpec(memory_space=pltpu.VMEM)
HBM = pl.BlockSpec(memory_space=pl.ANY)


def split(value):
    high = value.astype(BF16)
    return high, (value - high.astype(F32)).astype(BF16)


def wide(value):
    return jnp.concatenate(split(value), axis=1)


def weights(matrix):
    row = wide(matrix)
    return jnp.concatenate([row, row], axis=0)


def times(rows, packed):
    both = jnp.dot(wide(rows), packed, preferred_element_type=F32)
    return both[:, :H] + both[:, H:]


def unit():
    line = lax.broadcasted_iota(jnp.int32, (H, H), 0)
    return jnp.where(line == lax.broadcasted_iota(jnp.int32, (H, H), 1), 1.0, 0.0).astype(F32)


def rate_matrix(weight, damping):
    return weight.T - weight - unit() * damping


def shift_down(block, first):
    line = lax.broadcasted_iota(jnp.int32, block.shape, 0)
    return jnp.where(line == 0, first, pltpu.roll(block, 1, 0))


def tail_of(rows):
    return jnp.concatenate([rows, jnp.zeros((8, H), F32)], axis=0)


def then(earlier, later, offset, eye):
    moved = earlier + times(earlier, weights(later - eye))
    return jnp.concatenate([moved[:H], moved[H:] + offset], axis=0)


def remote(src, dst, sends, recvs, target):
    return pltpu.make_async_remote_copy(
        src_ref=src, dst_ref=dst, send_sem=sends, recv_sem=recvs,
        device_id=target, device_id_type=MESH,
    )


def swap_copies(buf, axis, sends, recvs, rows):
    n = lax.axis_size(axis)
    me = lax.axis_index(axis)
    part = buf.at[me, pl.ds(0, rows)]
    farthest_first = sorted(range(1, n), key=lambda d: -min(d, n - d))
    return [
        remote(part, part, sends.at[d - 1], recvs.at[d - 1], {axis: lax.rem(me + d, n)}) for d in farthest_first
    ]


def lane_sum(matrix):
    ones = jnp.ones((16, 2 * H), BF16)
    return lax.dot_general(ones, wide(matrix), (((1,), (1,)), ((), ())), preferred_element_type=F32)


def newton(
    x_hbm, guess_hbm, w_hbm, damp_hbm, u_hbm, bias_hbm, target_hbm, steps_hbm,
    traj_hbm, recur_ref, gin_ref,
    x_ref, guess_ref, w_ref, damp_ref, u_ref, bias_ref, target_ref, steps_ref, load_sem,
    edge, gain_ref, resid_ref, offs_ref, maps_ref, tree, totals, prefix, suffix, turned,
    pair, hit_ref, hits, zbuf, ubuf, xbuf, pulls, tiles, ends,
    start_ref, carry_ref, push_ref, source_ref, pre_ref, traj_ref,
    grads, parts, shares, whole,
    edge_send, edge_recv, core_send, core_recv, zs, zr, xs, xr, pull_send, pull_recv,
    send1, recv1, send2, recv2, send3, recv3,
):
    x, y, z, c = (lax.axis_index(name) for name in ("x", "batch", "z", "core"))
    nx, ny, nz, nc = (lax.axis_size(name) for name in ("x", "batch", "z", "core"))
    count = guess_ref.shape[0]
    steps = count // 2
    chunks = steps // LEN
    lanes = 2 * chunks
    blocks = TBLK // LEN

    loads = [
        pltpu.make_async_copy(src, dst, load_sem.at[i])
        for i, (src, dst) in enumerate((
            (w_hbm, w_ref), (damp_hbm, damp_ref), (guess_hbm, guess_ref), (u_hbm, u_ref), (x_hbm, x_ref),
            (bias_hbm, bias_ref), (target_hbm, target_ref), (steps_hbm, steps_ref),
        ))
    ]
    for load in loads:
        load.start()

    other = 1 - c
    sibling = {"core": other}
    plane, column = nx * ny, nz * nc
    p = x * ny + y
    q = z * nc + c
    planes = [lax.rem(p + d, plane) for d in range(1, plane)]
    columns = [lax.rem(q + d, column) for d in range(1, column)]
    plane_ids = [{"x": mate // ny, "batch": lax.rem(mate, ny)} for mate in planes]
    column_ids = [{"z": mate // nc, "core": lax.rem(mate, nc)} for mate in columns]
    place = x * column + q

    def along(where):
        return {"x": where // column, "z": lax.rem(where // nc, nz), "core": lax.rem(where, nc)}

    following = along(lax.rem(place + 1, nx * column))
    preceding = along(lax.rem(place + nx * column - 1, nx * column))
    barrier = pltpu.get_barrier_semaphore()
    chips = nx * nz
    chip = x * nz + z
    chip_ids = []
    for d in range(1, chips):
        mate = lax.rem(chip + d, chips)
        chip_ids.append({"x": mate // nz, "z": lax.rem(mate, nz)})
    across = [
        {"x": lax.rem(x + dx, nx), "z": lax.rem(z + dz, nz)} for dx in range(1, nx) for dz in range(1, nz)
    ]
    greeted = plane_ids + column_ids + across + [following, preceding]
    for target in greeted:
        pl.semaphore_signal(barrier, inc=1, device_id=target, device_id_type=MESH)

    eye = unit()
    loads[0].wait()
    loads[1].wait()
    rate_t = rate_matrix(w_ref[...], damp_ref[...])
    packed = weights(rate_t)
    for load in loads[2:]:
        load.wait()
    guess = guess_ref[...]

    def prev_rows(firsts):
        return jnp.concatenate(
            [shift_down(guess_ref[s * steps:(s + 1) * steps, :], firsts[s]) for s in range(2)], axis=0
        )

    zero_row = jnp.zeros((1, H), F32)
    u_pair = wide(u_ref[...])
    x_high, x_low = split(x_ref[...])
    drive = jnp.dot(x_high, u_pair, preferred_element_type=F32)
    drive = drive + jnp.dot(x_low, u_pair, preferred_element_type=F32)
    prev = prev_rows([zero_row, zero_row])
    preact = times(prev, packed) + drive[:, :H] + drive[:, H:] + bias_ref[...]
    activation = jnp.tanh(preact)
    gain_ref[0:count, :] = EULER * (1.0 - activation * activation)
    resid_ref[0:count, :] = prev + EULER * activation - guess
    early_preact = [preact[s * steps:s * steps + 1] for s in range(2)]

    edge_copies = [
        remote(guess_ref.at[pl.ds((s + 1) * steps - 8, 8)], edge.at[s], edge_send.at[s], edge_recv.at[s], following)
        for s in range(2)
    ]
    chunk_line = lax.broadcasted_iota(jnp.int32, (LEN, H), 0)

    def begin(s):
        gains = jnp.where(chunk_line == 0, 0.0, gain_ref[pl.ds(s * steps, chunks, stride=LEN), :])
        for k in range(chunks):
            maps_ref[s * chunks + k] = eye + rate_t * gains[k:k + 1]
        offs_ref[s * chunks:(s + 1) * chunks, :] = jnp.where(
            chunk_line == 0, 0.0, resid_ref[pl.ds(s * steps, chunks, stride=LEN), :]
        )

    def step_maps(base, size, gains, resid):
        for first in range(0, size, 4):
            state = maps_ref[base + first:base + first + 4].reshape(4 * H, H)
            if first + 4 == size:
                state = jnp.concatenate([state, offs_ref[base:base + 16, :]], axis=0)
            moved = times(state, packed)
            for i in range(4):
                here = slice(i * H, (i + 1) * H)
                maps_ref[base + first + i] = state[here] + gains[first + i:first + i + 1] * moved[here]
            if first + 4 == size:
                offs_ref[base:base + 16, :] = state[4 * H:] + gains * moved[4 * H:] + resid

    def compose(s, begin_at, end_at):
        def body(i, carry):
            for u in range(DEPTH):
                j = 1 + DEPTH * i + u
                rows = pl.ds(s * steps + j, chunks, stride=LEN)
                step_maps(s * chunks, chunks, gain_ref[rows, :], resid_ref[rows, :])
            return carry

        lax.fori_loop(begin_at, end_at, body, 0)

    first_row = chunk_line == 0

    def offset_of(lane):
        return jnp.where(first_row, offs_ref[pl.ds(lane, 1), :], 0.0)

    def lane_rows(lane):
        return jnp.concatenate([maps_ref[lane], offset_of(lane)], axis=0)

    def finish(s):
        lane = s * chunks
        gain = gain_ref[s * steps:s * steps + 1, :]
        resid = jnp.where(first_row, resid_ref[s * steps:s * steps + 1, :], 0.0)
        step = jnp.concatenate([eye + rate_t * gain, resid], axis=0)
        whole_chunk = then(step, maps_ref[lane], offset_of(lane), eye)
        maps_ref[lane] = whole_chunk[:H]
        offs_ref[lane:lane + 1, :] = whole_chunk[H:H + 1]
        for k in range(chunks // 2):
            tree[k] = then(lane_rows(lane + 2 * k), maps_ref[lane + 2 * k + 1], offset_of(lane + 2 * k + 1), eye)
        size = chunks // 2
        while size > 1:
            for k in range(size // 2):
                joined = then(tree[2 * k], tree[2 * k + 1, :H, :], tree[2 * k + 1, H:, :], eye)
                if size == 2:
                    totals[s] = joined
                else:
                    tree[k] = joined
            size //= 2

    core_copy = remote(
        totals.at[other, pl.ds(0, SENT)], pair.at[c, pl.ds(0, SENT)], core_send.at[0], core_recv.at[0], sibling
    )
    z_copies = swap_copies(zbuf, "z", zs, zr, SENT)

    def leave():
        core_copy.wait_recv()
        pair[c] = totals[c]
        zbuf[z] = then(
            jnp.concatenate([pair[0, :H, :], tail_of(pair[0, H:SENT, :])], axis=0),
            pair[1, :H, :], tail_of(pair[1, H:SENT, :]), eye,
        )
        for copy in z_copies:
            copy.start()

    begin(0)
    compose(0, 0, 1)
    pl.semaphore_wait(barrier, len(greeted))
    for copy in edge_copies:
        copy.start()
    compose(0, 1, (LEN - 1) // DEPTH)
    begin(1)
    for copy in edge_copies:
        copy.wait_recv()
    at_start = jnp.where(place > 0, 1.0, 0.0)
    firsts = [edge[s, 7:8, :] * at_start for s in range(2)]
    added = times(jnp.concatenate(firsts + [jnp.zeros((14, H), F32)], axis=0), packed)
    for s in range(2):
        row = slice(s * steps, s * steps + 1)
        activation = jnp.tanh(early_preact[s] + added[s:s + 1])
        gain_ref[row, :] = EULER * (1.0 - activation * activation)
        resid_ref[row, :] = firsts[s] + EULER * activation - guess_ref[row, :]
    finish(0)

    @pl.when(c == 1)
    def _():
        core_copy.start()

    compose(1, 0, 1)

    @pl.when(c == 0)
    def _():
        leave()

    compose(1, 1, (LEN - 1) // DEPTH)
    finish(1)

    @pl.when(c == 0)
    def _():
        core_copy.start()

    for s in range(2):
        for h in range(2):
            n = 2 * s + h
            step = steps_ref[s, h]
            kept = chunk_line <= lax.rem(step, LEN)
            to = slice(count + n * LEN, count + (n + 1) * LEN)
            for ref in (gain_ref, resid_ref):
                rows = jnp.zeros((LEN, H), F32)
                for k in range(blocks):
                    base = s * steps + h * TBLK + k * LEN
                    rows = jnp.where(chunk_line * 0 + step // LEN == k, ref[base:base + LEN, :], rows)
                ref[to, :] = jnp.where(kept, rows, 0.0)
    hit_pad = jnp.zeros((12, H), F32)

    def hit_rows(ref, j):
        return jnp.concatenate([ref[pl.ds(count + j, 4, stride=LEN), :], hit_pad], axis=0)

    gains = hit_rows(gain_ref, 0)
    for n in range(4):
        maps_ref[lanes + n] = eye + rate_t * gains[n:n + 1]
    offs_ref[lanes:lanes + 16, :] = hit_rows(resid_ref, 0)

    def compose_hits(begin_at, end_at):
        def body(i, carry):
            for u in range(DEPTH):
                j = 1 + DEPTH * i + u
                step_maps(lanes, 4, hit_rows(gain_ref, j), hit_rows(resid_ref, j))
            return carry

        lax.fori_loop(begin_at, end_at, body, 0)

    compose_hits(0, 2)

    @pl.when(c == 1)
    def _():
        leave()

    compose_hits(2, (LEN - 1) // DEPTH)

    start = jnp.concatenate([eye, jnp.zeros((16, H), F32)], axis=0)

    def chain(k, carry):
        out = []
        for s in range(2):
            lane = s * chunks + k
            prefix[lane] = carry[s]
            out.append(then(carry[s], maps_ref[lane], offset_of(lane), eye))
        return tuple(out)

    lax.fori_loop(0, chunks, chain, (start, start))
    block_line = lax.broadcasted_iota(jnp.int32, (TBLK, H), 0)
    map_line = jnp.zeros((AUG, H), jnp.int32)
    for s in range(2):
        for h in range(2):
            n = 2 * s + h
            step = steps_ref[s, h]
            run = jnp.zeros((AUG, H), F32)
            for k in range(blocks):
                run = jnp.where(map_line + step // LEN == k, prefix[s * chunks + h * blocks + k], run)
            base = s * steps + h * TBLK
            here = jnp.where(block_line == step, guess_ref[base:base + TBLK, :], 0.0)
            miss = offs_ref[lanes + n:lanes + n + 1, :] + jnp.sum(here, axis=0, keepdims=True)
            miss = miss - target_ref[n:n + 1, :]
            hit_ref[n] = then(run, maps_ref[lanes + n], jnp.where(first_row, miss, 0.0), eye)
    hit_copy = remote(
        hit_ref.at[pl.ds(2 * other, 2)], hits.at[c], core_send.at[1], core_recv.at[1], sibling
    )
    hit_copy.start()
    hits[c] = hit_ref[pl.ds(2 * c, 2)]

    def back_chain(i, carry):
        k = chunks - 1 - i
        out = []
        for s in range(2):
            lane = s * chunks + k
            suffix[lane] = carry[s]
            turn = weights((maps_ref[lane] - eye).T)
            turned[lane] = turn
            out.append(carry[s] + times(carry[s], turn))
        return tuple(out)

    lax.fori_loop(0, chunks, back_chain, (eye, eye))

    for copy in z_copies:
        copy.wait_recv()
    run = jnp.concatenate([zbuf[0, :H, :], tail_of(zbuf[0, H:SENT, :])], axis=0)
    ahead = start
    after = eye
    for k in range(1, nz):
        ahead = jnp.where(k == z, run, ahead)
        ubuf[k] = after
        moved = times(jnp.concatenate([run, after], axis=0), weights(zbuf[k, :H, :] - eye))
        offset = tail_of(zbuf[k, H:SENT, :])
        run = run + moved[:AUG] + jnp.concatenate([jnp.zeros((H, H), F32), offset], axis=0)
        after = jnp.where(k > z, after + moved[AUG:], after)
    xbuf[x] = run
    inner = jnp.logical_and(x > 0, x < nx - 1)

    def x_copy(slot, full, d):
        part = xbuf.at[slot, pl.ds(0, SENT) if full else pl.ds(H, 8)]
        return remote(part, part, xs.at[d - 1], xr.at[d - 1], {"x": lax.rem(x + d, nx)})

    def x_copies(slot, full):
        return [x_copy(slot, full, d) for d in range(1, nx)]

    @pl.when(inner)
    def _():
        for copy in x_copies(x, True):
            copy.start()

    @pl.when(jnp.logical_not(inner))
    def _():
        for copy in x_copies(x, False):
            copy.start()

    hit_copy.wait_recv()
    first_map = jnp.concatenate([pair[0, :H, :], tail_of(pair[0, H:SENT, :])], axis=0)
    late = [then(first_map, hits[1, h, :H, :], hits[1, h, H:, :], eye) for h in range(2)]
    w_ahead = weights(ahead[:H] - eye)
    w_first = weights(pair[0, :H, :] - eye)
    w_hits = [weights(hits[0, h, :H, :] - eye) for h in range(2)] + [weights(late[h][:H] - eye) for h in range(2)]
    t_hits = [weights(hits[0, h, :H, :].T) for h in range(2)] + [weights(late[h][:H].T) for h in range(2)]
    t_late = [weights(hits[1, h, :H, :].T) for h in range(2)]
    t_ahead = weights(ahead[:H].T)
    miss_rows = [hits[0, h, H:, :] for h in range(2)] + [late[h][H:] for h in range(2)]

    for d in range(1, nx):
        source = lax.rem(x + nx - d, nx)
        source_inner = jnp.logical_and(source > 0, source < nx - 1)

        @pl.when(source_inner)
        def _():
            x_copy(source, True, d).wait_recv()

        @pl.when(jnp.logical_not(source_inner))
        def _():
            x_copy(source, False, d).wait_recv()

    v = jnp.where(x > 0, tail_of(xbuf[0, H:SENT, :]), 0.0)
    for k in range(1, nx - 1):
        moved = v + times(v, weights(xbuf[k, :H, :] - eye)) + tail_of(xbuf[k, H:SENT, :])
        v = jnp.where(k < x, moved, v)
    v = v + times(v, w_ahead) + ahead[H:]
    scale = 0.125
    misses = [(v + times(v, w_hits[i]) + miss_rows[i]) * scale for i in range(4)]
    pull = jnp.zeros((16, H), F32)
    for i in range(4):
        pull = pull + times(misses[i], t_hits[i])
    far = times(pull, t_ahead)
    line = lax.broadcasted_iota(jnp.int32, (8, H), 0)
    pulls[chip] = jnp.where(line == 0, pull[0:1], far[0:1])
    pull_copies = [
        remote(pulls.at[chip], pulls.at[chip], pull_send.at[i], pull_recv.at[i], chip_ids[i]) for i in range(chips - 1)
    ]
    for copy in pull_copies:
        copy.start()
    v_late = v + times(v, w_first) + tail_of(pair[0, H:SENT, :])
    ends[0, c] = jnp.where(c == 0, v[:8], v_late[:8])
    tiles[0] = jnp.where(c == 0, v_late[:8], v[:8])
    delta_copy = remote(tiles.at[0], ends.at[0, c], core_send.at[2], core_recv.at[2], sibling)
    delta_copy.start()
    pull_late = times(misses[2], t_late[0]) + times(misses[3], t_late[1])
    delta_copy.wait_recv()

    lane_line = lax.broadcasted_iota(jnp.int32, (lanes, H), 0)
    pushes = jnp.zeros((lanes, H), F32)
    columns_d = [jnp.broadcast_to(ends[0, s, 0:1, :], (H, H)).T for s in range(2)]
    for s in range(2):
        for h in range(2):
            n = 2 * s + h
            step = steps_ref[s, h]
            miss = jnp.sum(hit_ref[n, :H, :] * columns_d[s], axis=0, keepdims=True) + hit_ref[n, H:H + 1, :]
            miss = miss * scale
            source_ref[s * steps + h * TBLK:s * steps + (h + 1) * TBLK, :] = jnp.where(block_line == step, miss, 0.0)
            pushed = times(jnp.broadcast_to(miss, (16, H)), weights(maps_ref[lanes + n].T))
            pushes = pushes + jnp.where(lane_line == s * chunks + h * blocks + step // LEN, pushed[0:1], 0.0)
    push_ref[...] = pushes

    def spread(table, columns, k, s):
        lane = s * chunks + k
        return jnp.sum(table[lane, :H, :] * columns[s], axis=0, keepdims=True)

    def local_back(j, carry):
        k = chunks - 1 - j
        out = []
        for s, t in enumerate(carry):
            lane = s * chunks + k
            carry_ref[pl.ds(lane, 1), :] = t[0:1]
            out.append(t + times(t, turned[lane]) + push_ref[pl.ds(lane, 1), :])
        return tuple(out)

    nothing = jnp.zeros((16, H), F32)
    lax.fori_loop(0, chunks, local_back, (nothing, nothing), unroll=True)
    t_first = weights((pair[1, :H, :] - eye).T)
    t_after = weights((after - eye).T)
    t_rows = {k: weights((xbuf[k, :H, :] - eye).T) for k in range(1, nx - 1)}

    for copy in pull_copies:
        copy.wait_recv()
    total = jnp.zeros((H, H), F32)
    for k in range(1, nz):
        total = total + jnp.where(k > z, ubuf[k] * pulls[x * nz + k, 0:1, :], 0.0)
    near = lane_sum(total)
    row_pulls = []
    for k in range(nx):
        row = pulls[k * nz]
        for i in range(1, nz):
            row = row + pulls[k * nz + i]
        row_pulls.append(row)
    t = jnp.where(nx - 1 > x, jnp.broadcast_to(row_pulls[nx - 1][1:2], (16, H)), 0.0)
    for k in range(nx - 2, 0, -1):
        t = jnp.where(k > x, t + times(t, t_rows[k]) + row_pulls[k][1:2], t)
    lam_late = near + t + times(t, t_after)
    lam = lam_late + times(lam_late, t_first) + pull_late
    ends[1, c] = jnp.where(c == 0, lam[:8], lam_late[:8])
    tiles[1] = jnp.where(c == 0, lam_late[:8], lam[:8])
    lam_copy = remote(tiles.at[1], ends.at[1, c], core_send.at[3], core_recv.at[3], sibling)
    lam_copy.start()
    packed_t = weights(rate_t.T)
    lam_copy.wait_recv()
    columns_l = [jnp.broadcast_to(ends[1, s, 0:1, :], (H, H)).T for s in range(2)]

    def carries(k, carry):
        for s in range(2):
            lane = pl.ds(s * chunks + k, 1)
            carry_ref[lane, :] = carry_ref[lane, :] + spread(suffix, columns_l, k, s)
        return carry

    lax.fori_loop(0, chunks, carries, 0)

    def backward(j, adjoint):
        rows = pl.ds(LEN - 1 - j, lanes, stride=LEN)
        adjoint = adjoint + source_ref[rows, :]
        scaled = gain_ref[rows, :] * adjoint
        pre_ref[rows, :] = scaled
        return adjoint + times(scaled, packed_t)

    lax.fori_loop(0, LEN, backward, carry_ref[...], unroll=True)
    left_high, left_low = split(jnp.concatenate([prev_rows([edge[s, 7:8, :] * at_start for s in range(2)]), x_ref[...]], axis=1))
    right = wide(pre_ref[...])
    dims = (((0,), (0,)), ((), ()))
    both = lax.dot_general(left_high, right, dims, preferred_element_type=F32)
    both = both + lax.dot_general(left_low, right, dims, preferred_element_type=F32)
    sums = both[:, :H] + both[:, H:]
    grads[0:H // 8] = (sums[:H].T - sums[:H]).reshape(H // 8, 8, H)
    grads[H // 8:] = sums[H:].reshape(2 * H // 8, 8, H)

    share = grads.shape[0] // plane
    done = []
    for i in range(plane - 1):
        done.append(remote(
            grads.at[pl.ds(planes[i] * share, share)], parts.at[p], send1.at[i], recv1.at[i], plane_ids[i]
        ))
        done[-1].start()
    parts[p] = grads[pl.ds(p * share, share)]

    def starts(k, carry):
        for s in range(2):
            lane = s * chunks + k
            start_ref[pl.ds(lane, 1), :] = spread(prefix, columns_d, k, s) + prefix[lane, H:H + 1, :]
        return carry

    def forward(j, state):
        rows = pl.ds(j, lanes, stride=LEN)
        state = state + gain_ref[rows, :] * times(state, packed) + resid_ref[rows, :]
        traj_ref[rows, :] = state + guess_ref[rows, :]
        return state

    lax.fori_loop(0, chunks, starts, 0)
    lax.fori_loop(0, LEN, forward, start_ref[...], unroll=True)
    traj_copy = pltpu.make_async_copy(traj_ref, traj_hbm, load_sem.at[0])
    traj_copy.start()
    for copy in done:
        copy.wait_recv()
    shares[q] = jnp.sum(parts[...], axis=0)
    exchange = [
        remote(shares.at[q], shares.at[q], send2.at[i], recv2.at[i], column_ids[i]) for i in range(column - 1)
    ]
    for copy in exchange:
        copy.start()
    for copy in exchange:
        copy.wait_recv()
    mine = pl.ds(p * share, share)
    whole[mine] = jnp.sum(shares[...], axis=0)
    last = [
        remote(whole.at[mine], whole.at[mine], send3.at[i], recv3.at[i], plane_ids[i]) for i in range(plane - 1)
    ]
    for copy in last:
        copy.start()

    @pl.when(inner)
    def _():
        for copy in x_copies(x, True):
            copy.wait_send()

    @pl.when(jnp.logical_not(inner))
    def _():
        for copy in x_copies(x, False):
            copy.wait_send()

    traj_copy.wait()
    early = edge_copies + [core_copy, hit_copy, delta_copy, lam_copy] + z_copies + pull_copies
    for copy in early + done + exchange:
        copy.wait_send()
    for copy in last:
        copy.wait_recv()
    recur_ref[...] = whole[0:H // 8].reshape(H, H)
    gin_ref[...] = whole[H // 8:].reshape(2 * H, H)
    for copy in last:
        copy.wait_send()


def vmem(*dims):
    return pltpu.VMEM(dims, F32)


def out(*dims):
    return jax.ShapeDtypeStruct(dims, F32)


def on_device(inputs, guess_path, recur_weight, damping, in_weight, bias_term, targets, target_steps):
    seqs, steps, hidden = guess_path.shape
    features = inputs.shape[2]
    count = seqs * steps
    chunks = steps // LEN
    lanes = seqs * chunks
    nx, nz, nc, ny = (lax.axis_size(name) for name in ("x", "z", "core", "batch"))
    plane, column = nx * ny, nz * nc
    tiles = 3 * hidden // 8
    share = tiles // plane
    extra = count + 4 * LEN
    dma = pltpu.SemaphoreType.DMA
    traj, grad_recur, grad_in = pl.pallas_call(
        newton,
        out_shape=(out(count, hidden), out(hidden, hidden), out(features, hidden)),
        in_specs=[HBM] * 8,
        out_specs=[HBM, VM, VM],
        scratch_shapes=[
            vmem(count, features), vmem(count, hidden), vmem(hidden, hidden), vmem(1, hidden),
            vmem(features, hidden), vmem(1, hidden), vmem(4, hidden), pltpu.SMEM((seqs, 2), jnp.int32), dma((8,)),
            vmem(seqs, 8, hidden), vmem(extra, hidden), vmem(extra, hidden), vmem(lanes + 16, hidden),
            vmem(lanes + 4, hidden, hidden), vmem(chunks // 2, AUG, hidden), vmem(seqs, AUG, hidden),
            vmem(lanes, AUG, hidden), vmem(lanes, hidden, hidden), pltpu.VMEM((lanes, 2 * hidden, 2 * hidden), BF16),
            vmem(2, AUG, hidden), vmem(4, AUG, hidden), vmem(2, 2, AUG, hidden), vmem(nz, AUG, hidden),
            vmem(nz, hidden, hidden), vmem(nx, AUG, hidden), vmem(nx * nz, 8, hidden),
            vmem(2, 8, hidden), vmem(2, seqs, 8, hidden),
            vmem(lanes, hidden), vmem(lanes, hidden), vmem(lanes, hidden), vmem(count, hidden), vmem(count, hidden),
            vmem(count, hidden),
            vmem(tiles, 8, hidden), vmem(plane, share, 8, hidden), vmem(column, share, 8, hidden), vmem(tiles, 8, hidden),
            dma((2,)), dma((2,)), dma((4,)), dma((4,)), dma((nz - 1,)), dma((nz - 1,)), dma((nx - 1,)), dma((nx - 1,)),
            dma((nx * nz - 1,)), dma((nx * nz - 1,)),
            dma((plane - 1,)), dma((plane - 1,)), dma((column - 1,)), dma((column - 1,)), dma((plane - 1,)),
            dma((plane - 1,)),
        ],
        compiler_params=pltpu.CompilerParams(
            collective_id=0, has_side_effects=True, vmem_limit_bytes=63 * 1024 * 1024
        ),
        name="newton",
    )(
        inputs.reshape(count, features), guess_path.reshape(count, hidden), recur_weight, damping.reshape(1, hidden),
        in_weight, bias_term.reshape(1, hidden), targets.reshape(-1, hidden), target_steps,
    )
    return traj.reshape(guess_path.shape), grad_recur, grad_in


def solution(mesh):
    torus = Mesh(mesh.devices.reshape(4, 8, 2, mesh.shape["batch"]), (*SEQ, "batch"))
    return jax.shard_map(
        on_device,
        mesh=torus,
        in_specs=(
            P("batch", SEQ, None), P("batch", SEQ, None), P(), P(), P(), P(), P("batch", SEQ, None), P("batch", SEQ),
        ),
        out_specs=(P("batch", SEQ, None), P(), P()),
        check_vma=False,
    )
```

```python
import jax
import jax.numpy as jnp
from jax import lax
from jax.experimental import pallas as pl
from jax.experimental.pallas import tpu as pltpu
from jax.sharding import Mesh
from jax.sharding import PartitionSpec as P

H = 128
LEN = 16
TBLK = 128
AUG = 144
SENT = 136
DEPTH = 5
SEQ = ("x", "z", "core")
EULER = 0.02
F32 = jnp.float32
BF16 = jnp.bfloat16
MESH = pl.DeviceIdType.MESH
VM = pl.BlockSpec(memory_space=pltpu.VMEM)
HBM = pl.BlockSpec(memory_space=pltpu.HBM)


def split(value):
    high = value.astype(BF16)
    return high, (value - high.astype(F32)).astype(BF16)


def wide(value):
    return jnp.concatenate(split(value), axis=1)


def weights(matrix):
    row = wide(matrix)
    return jnp.concatenate([row, row], axis=0)


def times(rows, packed):
    both = jnp.dot(wide(rows), packed, preferred_element_type=F32)
    return both[:, :H] + both[:, H:]


def unit():
    line = lax.broadcasted_iota(jnp.int32, (H, H), 0)
    return jnp.where(line == lax.broadcasted_iota(jnp.int32, (H, H), 1), 1.0, 0.0).astype(F32)


def rate_matrix(weight, damping):
    return weight.T - weight - unit() * damping


def shift_down(block, first):
    line = lax.broadcasted_iota(jnp.int32, block.shape, 0)
    return jnp.where(line == 0, first, pltpu.roll(block, 1, 0))


def tail_of(rows):
    return jnp.concatenate([rows, jnp.zeros((8, H), F32)], axis=0)


def then(earlier, later, offset, eye):
    moved = earlier + times(earlier, weights(later - eye))
    return jnp.concatenate([moved[:H], moved[H:] + offset], axis=0)


def remote(src, dst, sends, recvs, target):
    return pltpu.make_async_remote_copy(
        src_ref=src, dst_ref=dst, send_sem=sends, recv_sem=recvs,
        device_id=target, device_id_type=MESH,
    )


def swap_copies(buf, axis, sends, recvs, rows):
    n = lax.axis_size(axis)
    me = lax.axis_index(axis)
    part = buf.at[me, pl.ds(0, rows)]
    farthest_first = sorted(range(1, n), key=lambda d: -min(d, n - d))
    return [
        remote(part, part, sends.at[d - 1], recvs.at[d - 1], {axis: lax.rem(me + d, n)}) for d in farthest_first
    ]


def lane_sum(matrix):
    ones = jnp.ones((16, 2 * H), BF16)
    return lax.dot_general(ones, wide(matrix), (((1,), (1,)), ((), ())), preferred_element_type=F32)


def newton(
    x_hbm, guess_hbm, w_hbm, damp_hbm, u_hbm, bias_hbm, target_hbm, steps_hbm,
    traj_ref, whole,
    x_ref, guess_ref, w_ref, damp_ref, u_ref, bias_ref, target_ref, steps_ref, load_sem,
    edge, gain_ref, resid_ref, offs_ref, maps_ref, tree, totals, prefix, suffix, turned,
    pair, hit_ref, hits, zbuf, ubuf, xbuf, pulls, tiles, ends,
    start_ref, carry_ref, push_ref, source_ref, pre_ref,
    grads, parts, shares,
    edge_send, edge_recv, core_send, core_recv, zs, zr, xs, xr, pull_send, pull_recv,
    send1, recv1, send2, recv2, send3, recv3,
):
    x, y, z, c = (lax.axis_index(name) for name in ("x", "batch", "z", "core"))
    nx, ny, nz, nc = (lax.axis_size(name) for name in ("x", "batch", "z", "core"))
    count = guess_ref.shape[0]
    steps = count // 2
    chunks = steps // LEN
    lanes = 2 * chunks
    blocks = TBLK // LEN

    loads = [
        pltpu.make_async_copy(src, dst, load_sem.at[i])
        for i, (src, dst) in enumerate((
            (w_hbm, w_ref), (damp_hbm, damp_ref), (guess_hbm, guess_ref), (u_hbm, u_ref), (x_hbm, x_ref),
            (bias_hbm, bias_ref), (target_hbm, target_ref), (steps_hbm, steps_ref),
        ))
    ]
    for load in loads:
        load.start()

    other = 1 - c
    sibling = {"core": other}
    plane, column = nx * ny, nz * nc
    p = x * ny + y
    q = z * nc + c
    planes = [lax.rem(p + d, plane) for d in range(1, plane)]
    columns = [lax.rem(q + d, column) for d in range(1, column)]
    plane_ids = [{"x": mate // ny, "batch": lax.rem(mate, ny)} for mate in planes]
    column_ids = [{"z": mate // nc, "core": lax.rem(mate, nc)} for mate in columns]
    place = x * column + q

    def along(where):
        return {"x": where // column, "z": lax.rem(where // nc, nz), "core": lax.rem(where, nc)}

    following = along(lax.rem(place + 1, nx * column))
    preceding = along(lax.rem(place + nx * column - 1, nx * column))
    barrier = pltpu.get_barrier_semaphore()
    chips = nx * nz
    chip = x * nz + z
    chip_ids = []
    for d in range(1, chips):
        mate = lax.rem(chip + d, chips)
        chip_ids.append({"x": mate // nz, "z": lax.rem(mate, nz)})
    z_ids = [{"z": lax.rem(z + d, nz)} for d in range(1, nz)]
    greeted = plane_ids + z_ids + [sibling, following, preceding]

    eye = unit()
    loads[0].wait()
    loads[1].wait()
    rate_t = rate_matrix(w_ref[...], damp_ref[...])
    packed = weights(rate_t)
    for load in loads[2:]:
        load.wait()
    for target in greeted:
        pl.semaphore_signal(barrier, inc=1, device_id=target, device_id_type=MESH)
    guess = guess_ref[...]

    def prev_rows(firsts):
        return jnp.concatenate(
            [shift_down(guess_ref[s * steps:(s + 1) * steps, :], firsts[s]) for s in range(2)], axis=0
        )

    zero_row = jnp.zeros((1, H), F32)
    u_pair = wide(u_ref[...])
    x_high, x_low = split(x_ref[...])
    drive = jnp.dot(x_high, u_pair, preferred_element_type=F32)
    drive = drive + jnp.dot(x_low, u_pair, preferred_element_type=F32)
    prev = prev_rows([zero_row, zero_row])
    preact = times(prev, packed) + drive[:, :H] + drive[:, H:] + bias_ref[...]
    activation = jnp.tanh(preact)
    gain_ref[0:count, :] = EULER * (1.0 - activation * activation)
    resid_ref[0:count, :] = prev + EULER * activation - guess
    early_preact = [preact[s * steps:s * steps + 1] for s in range(2)]

    edge_copies = [
        remote(guess_ref.at[pl.ds((s + 1) * steps - 8, 8)], edge.at[s], edge_send.at[s], edge_recv.at[s], following)
        for s in range(2)
    ]
    chunk_line = lax.broadcasted_iota(jnp.int32, (LEN, H), 0)

    def begin(s):
        gains = jnp.where(chunk_line == 0, 0.0, gain_ref[pl.ds(s * steps, chunks, stride=LEN), :])
        for k in range(chunks):
            maps_ref[s * chunks + k] = eye + rate_t * gains[k:k + 1]
        offs_ref[s * chunks:(s + 1) * chunks, :] = jnp.where(
            chunk_line == 0, 0.0, resid_ref[pl.ds(s * steps, chunks, stride=LEN), :]
        )

    def step_maps(base, size, gains, resid):
        for first in range(0, size, 4):
            state = maps_ref[base + first:base + first + 4].reshape(4 * H, H)
            if first + 4 == size:
                state = jnp.concatenate([state, offs_ref[base:base + 16, :]], axis=0)
            moved = times(state, packed)
            for i in range(4):
                here = slice(i * H, (i + 1) * H)
                maps_ref[base + first + i] = state[here] + gains[first + i:first + i + 1] * moved[here]
            if first + 4 == size:
                offs_ref[base:base + 16, :] = state[4 * H:] + gains * moved[4 * H:] + resid

    def compose(s, begin_at, end_at):
        def body(i, carry):
            for u in range(DEPTH):
                j = 1 + DEPTH * i + u
                rows = pl.ds(s * steps + j, chunks, stride=LEN)
                step_maps(s * chunks, chunks, gain_ref[rows, :], resid_ref[rows, :])
            return carry

        lax.fori_loop(begin_at, end_at, body, 0)

    first_row = chunk_line == 0

    def offset_of(lane):
        return jnp.where(first_row, offs_ref[pl.ds(lane, 1), :], 0.0)

    def lane_rows(lane):
        return jnp.concatenate([maps_ref[lane], offset_of(lane)], axis=0)

    def finish(s):
        lane = s * chunks
        gain = gain_ref[s * steps:s * steps + 1, :]
        resid = jnp.where(first_row, resid_ref[s * steps:s * steps + 1, :], 0.0)
        step = jnp.concatenate([eye + rate_t * gain, resid], axis=0)
        whole_chunk = then(step, maps_ref[lane], offset_of(lane), eye)
        maps_ref[lane] = whole_chunk[:H]
        offs_ref[lane:lane + 1, :] = whole_chunk[H:H + 1]
        for k in range(chunks // 2):
            tree[k] = then(lane_rows(lane + 2 * k), maps_ref[lane + 2 * k + 1], offset_of(lane + 2 * k + 1), eye)
        size = chunks // 2
        while size > 1:
            for k in range(size // 2):
                joined = then(tree[2 * k], tree[2 * k + 1, :H, :], tree[2 * k + 1, H:, :], eye)
                if size == 2:
                    totals[s] = joined
                else:
                    tree[k] = joined
            size //= 2

    core_copy = remote(
        totals.at[other, pl.ds(0, SENT)], pair.at[c, pl.ds(0, SENT)], core_send.at[0], core_recv.at[0], sibling
    )
    z_copies = swap_copies(zbuf, "z", zs, zr, SENT)

    def leave():
        core_copy.wait_recv()
        pair[c] = totals[c]
        zbuf[z] = then(
            jnp.concatenate([pair[0, :H, :], tail_of(pair[0, H:SENT, :])], axis=0),
            pair[1, :H, :], tail_of(pair[1, H:SENT, :]), eye,
        )
        for copy in z_copies:
            copy.start()

    begin(0)
    compose(0, 0, 2)
    pl.semaphore_wait(barrier, len(greeted))
    for copy in edge_copies:
        copy.start()
    compose(0, 2, (LEN - 1) // DEPTH)
    begin(1)
    for copy in edge_copies:
        copy.wait_recv()
    at_start = jnp.where(place > 0, 1.0, 0.0)
    firsts = [edge[s, 7:8, :] * at_start for s in range(2)]
    added = times(jnp.concatenate(firsts + [jnp.zeros((14, H), F32)], axis=0), packed)
    for s in range(2):
        row = slice(s * steps, s * steps + 1)
        activation = jnp.tanh(early_preact[s] + added[s:s + 1])
        gain_ref[row, :] = EULER * (1.0 - activation * activation)
        resid_ref[row, :] = firsts[s] + EULER * activation - guess_ref[row, :]
    finish(0)

    @pl.when(c == 1)
    def _():
        core_copy.start()

    compose(1, 0, 1)

    @pl.when(c == 0)
    def _():
        leave()

    compose(1, 1, (LEN - 1) // DEPTH)
    finish(1)

    @pl.when(c == 0)
    def _():
        core_copy.start()

    for s in range(2):
        for h in range(2):
            n = 2 * s + h
            step = steps_ref[s, h]
            kept = chunk_line <= lax.rem(step, LEN)
            to = slice(count + n * LEN, count + (n + 1) * LEN)
            for ref in (gain_ref, resid_ref):
                rows = jnp.zeros((LEN, H), F32)
                for k in range(blocks):
                    base = s * steps + h * TBLK + k * LEN
                    rows = jnp.where(chunk_line * 0 + step // LEN == k, ref[base:base + LEN, :], rows)
                ref[to, :] = jnp.where(kept, rows, 0.0)
    hit_pad = jnp.zeros((12, H), F32)

    def hit_rows(ref, j):
        return jnp.concatenate([ref[pl.ds(count + j, 4, stride=LEN), :], hit_pad], axis=0)

    gains = hit_rows(gain_ref, 0)
    for n in range(4):
        maps_ref[lanes + n] = eye + rate_t * gains[n:n + 1]
    offs_ref[lanes:lanes + 16, :] = hit_rows(resid_ref, 0)

    def compose_hits(begin_at, end_at):
        def body(i, carry):
            for u in range(DEPTH):
                j = 1 + DEPTH * i + u
                step_maps(lanes, 4, hit_rows(gain_ref, j), hit_rows(resid_ref, j))
            return carry

        lax.fori_loop(begin_at, end_at, body, 0)

    compose_hits(0, 2)

    @pl.when(c == 1)
    def _():
        leave()

    compose_hits(2, (LEN - 1) // DEPTH)

    start = jnp.concatenate([eye, jnp.zeros((16, H), F32)], axis=0)

    def chain(k, carry):
        out = []
        for s in range(2):
            lane = s * chunks + k
            prefix[lane] = carry[s]
            out.append(then(carry[s], maps_ref[lane], offset_of(lane), eye))
        return tuple(out)

    lax.fori_loop(0, chunks, chain, (start, start))
    block_line = lax.broadcasted_iota(jnp.int32, (TBLK, H), 0)
    map_line = jnp.zeros((AUG, H), jnp.int32)
    for s in range(2):
        for h in range(2):
            n = 2 * s + h
            step = steps_ref[s, h]
            run = jnp.zeros((AUG, H), F32)
            for k in range(blocks):
                run = jnp.where(map_line + step // LEN == k, prefix[s * chunks + h * blocks + k], run)
            base = s * steps + h * TBLK
            here = jnp.where(block_line == step, guess_ref[base:base + TBLK, :], 0.0)
            miss = offs_ref[lanes + n:lanes + n + 1, :] + jnp.sum(here, axis=0, keepdims=True)
            miss = miss - target_ref[n:n + 1, :]
            hit_ref[n] = then(run, maps_ref[lanes + n], jnp.where(first_row, miss, 0.0), eye)
    hit_copy = remote(
        hit_ref.at[pl.ds(2 * other, 2)], hits.at[c], core_send.at[1], core_recv.at[1], sibling
    )
    hit_copy.start()
    hits[c] = hit_ref[pl.ds(2 * c, 2)]

    def back_chain(i, carry):
        k = chunks - 1 - i
        out = []
        for s in range(2):
            lane = s * chunks + k
            suffix[lane] = carry[s]
            turn = weights((maps_ref[lane] - eye).T)
            turned[lane] = turn
            out.append(carry[s] + times(carry[s], turn))
        return tuple(out)

    lax.fori_loop(0, chunks, back_chain, (eye, eye))

    for copy in z_copies:
        copy.wait_recv()
    run = jnp.concatenate([zbuf[0, :H, :], tail_of(zbuf[0, H:SENT, :])], axis=0)
    ahead = start
    after = eye
    for k in range(1, nz):
        ahead = jnp.where(k == z, run, ahead)
        ubuf[k] = after
        moved = times(jnp.concatenate([run, after], axis=0), weights(zbuf[k, :H, :] - eye))
        offset = tail_of(zbuf[k, H:SENT, :])
        run = run + moved[:AUG] + jnp.concatenate([jnp.zeros((H, H), F32), offset], axis=0)
        after = jnp.where(k > z, after + moved[AUG:], after)
    xbuf[x] = run
    inner = jnp.logical_and(x > 0, x < nx - 1)

    def x_copy(slot, full, d):
        part = xbuf.at[slot, pl.ds(0, SENT) if full else pl.ds(H, 8)]
        return remote(part, part, xs.at[d - 1], xr.at[d - 1], {"x": lax.rem(x + d, nx)})

    def x_copies(slot, full):
        return [x_copy(slot, full, d) for d in range(1, nx)]

    @pl.when(inner)
    def _():
        for copy in x_copies(x, True):
            copy.start()

    @pl.when(jnp.logical_not(inner))
    def _():
        for copy in x_copies(x, False):
            copy.start()

    hit_copy.wait_recv()
    first_map = jnp.concatenate([pair[0, :H, :], tail_of(pair[0, H:SENT, :])], axis=0)
    late = [then(first_map, hits[1, h, :H, :], hits[1, h, H:, :], eye) for h in range(2)]
    w_ahead = weights(ahead[:H] - eye)
    w_first = weights(pair[0, :H, :] - eye)
    w_hits = [weights(hits[0, h, :H, :] - eye) for h in range(2)] + [weights(late[h][:H] - eye) for h in range(2)]
    t_hits = [weights(hits[0, h, :H, :].T) for h in range(2)] + [weights(late[h][:H].T) for h in range(2)]
    t_late = [weights(hits[1, h, :H, :].T) for h in range(2)]
    t_ahead = weights(ahead[:H].T)
    miss_rows = [hits[0, h, H:, :] for h in range(2)] + [late[h][H:] for h in range(2)]

    for d in range(1, nx):
        source = lax.rem(x + nx - d, nx)
        source_inner = jnp.logical_and(source > 0, source < nx - 1)

        @pl.when(source_inner)
        def _():
            x_copy(source, True, d).wait_recv()

        @pl.when(jnp.logical_not(source_inner))
        def _():
            x_copy(source, False, d).wait_recv()

    v = jnp.where(x > 0, tail_of(xbuf[0, H:SENT, :]), 0.0)
    for k in range(1, nx - 1):
        moved = v + times(v, weights(xbuf[k, :H, :] - eye)) + tail_of(xbuf[k, H:SENT, :])
        v = jnp.where(k < x, moved, v)
    v = v + times(v, w_ahead) + ahead[H:]
    scale = 0.125
    misses = [(v + times(v, w_hits[i]) + miss_rows[i]) * scale for i in range(4)]
    pull = jnp.zeros((16, H), F32)
    for i in range(4):
        pull = pull + times(misses[i], t_hits[i])
    far = times(pull, t_ahead)
    line = lax.broadcasted_iota(jnp.int32, (8, H), 0)
    pulls[chip] = jnp.concatenate([pull[0:1], far[0:1]], axis=0)
    pull_copies = [
        remote(pulls.at[chip], pulls.at[chip], pull_send.at[i], pull_recv.at[i], chip_ids[i]) for i in range(chips - 1)
    ]
    for copy in pull_copies:
        copy.start()
    v_late = v + times(v, w_first) + tail_of(pair[0, H:SENT, :])
    ends[0, c] = jnp.where(c == 0, v[:8], v_late[:8])
    tiles[0] = jnp.where(c == 0, v_late[:8], v[:8])
    delta_copy = remote(tiles.at[0], ends.at[0, c], core_send.at[2], core_recv.at[2], sibling)
    delta_copy.start()
    pull_late = times(misses[2], t_late[0]) + times(misses[3], t_late[1])
    delta_copy.wait_recv()

    lane_line = lax.broadcasted_iota(jnp.int32, (lanes, H), 0)
    pushes = jnp.zeros((lanes, H), F32)
    columns_d = [jnp.broadcast_to(ends[0, s, 0:1, :], (H, H)).T for s in range(2)]
    for s in range(2):
        for h in range(2):
            n = 2 * s + h
            step = steps_ref[s, h]
            miss = jnp.sum(hit_ref[n, :H, :] * columns_d[s], axis=0, keepdims=True) + hit_ref[n, H:H + 1, :]
            miss = miss * scale
            source_ref[s * steps + h * TBLK:s * steps + (h + 1) * TBLK, :] = jnp.where(block_line == step, miss, 0.0)
            pushed = times(jnp.broadcast_to(miss, (16, H)), weights(maps_ref[lanes + n].T))
            pushes = pushes + jnp.where(lane_line == s * chunks + h * blocks + step // LEN, pushed[0:1], 0.0)
    push_ref[...] = pushes

    def spread(table, columns, k, s):
        lane = s * chunks + k
        return jnp.sum(table[lane, :H, :] * columns[s], axis=0, keepdims=True)

    def local_back(j, carry):
        k = chunks - 1 - j
        out = []
        for s, t in enumerate(carry):
            lane = s * chunks + k
            carry_ref[pl.ds(lane, 1), :] = t[0:1]
            out.append(t + times(t, turned[lane]) + push_ref[pl.ds(lane, 1), :])
        return tuple(out)

    nothing = jnp.zeros((16, H), F32)
    lax.fori_loop(0, chunks, local_back, (nothing, nothing), unroll=True)
    t_first = weights((pair[1, :H, :] - eye).T)
    t_after = weights((after - eye).T)
    t_rows = {k: weights((xbuf[k, :H, :] - eye).T) for k in range(1, nx - 1)}

    for copy in pull_copies:
        copy.wait_recv()
    total = jnp.zeros((H, H), F32)
    for k in range(1, nz):
        total = total + jnp.where(k > z, ubuf[k] * pulls[x * nz + k, 0:1, :], 0.0)
    near = lane_sum(total)
    row_pulls = []
    for k in range(nx):
        row = pulls[k * nz]
        for i in range(1, nz):
            row = row + pulls[k * nz + i]
        row_pulls.append(row)
    t = jnp.where(nx - 1 > x, jnp.broadcast_to(row_pulls[nx - 1][1:2], (16, H)), 0.0)
    for k in range(nx - 2, 0, -1):
        t = jnp.where(k > x, t + times(t, t_rows[k]) + row_pulls[k][1:2], t)
    lam_late = near + t + times(t, t_after)
    lam = lam_late + times(lam_late, t_first) + pull_late
    ends[1, c] = jnp.where(c == 0, lam[:8], lam_late[:8])
    tiles[1] = jnp.where(c == 0, lam_late[:8], lam[:8])
    lam_copy = remote(tiles.at[1], ends.at[1, c], core_send.at[3], core_recv.at[3], sibling)
    lam_copy.start()
    packed_t = weights(rate_t.T)
    lam_copy.wait_recv()
    columns_l = [jnp.broadcast_to(ends[1, s, 0:1, :], (H, H)).T for s in range(2)]

    def carries(k, carry):
        for s in range(2):
            lane = pl.ds(s * chunks + k, 1)
            carry_ref[lane, :] = carry_ref[lane, :] + spread(suffix, columns_l, k, s)
        return carry

    lax.fori_loop(0, chunks, carries, 0)

    def backward(j, adjoint):
        rows = pl.ds(LEN - 1 - j, lanes, stride=LEN)
        adjoint = adjoint + source_ref[rows, :]
        scaled = gain_ref[rows, :] * adjoint
        pre_ref[rows, :] = scaled
        return adjoint + times(scaled, packed_t)

    lax.fori_loop(0, LEN, backward, carry_ref[...], unroll=True)
    left_high, left_low = split(jnp.concatenate([prev_rows([edge[s, 7:8, :] * at_start for s in range(2)]), x_ref[...]], axis=1))
    right = wide(pre_ref[...])
    dims = (((0,), (0,)), ((), ()))
    both = lax.dot_general(left_high, right, dims, preferred_element_type=F32)
    both = both + lax.dot_general(left_low, right, dims, preferred_element_type=F32)
    sums = both[:, :H] + both[:, H:]
    grads[0:H // 8] = (sums[:H].T - sums[:H]).reshape(H // 8, 8, H)
    grads[H // 8:] = sums[H:].reshape(2 * H // 8, 8, H)

    share = grads.shape[0] // plane
    done = []
    for i in range(plane - 1):
        done.append(remote(
            grads.at[pl.ds(planes[i] * share, share)], parts.at[p], send1.at[i], recv1.at[i], plane_ids[i]
        ))
        done[-1].start()
    parts[p] = grads[pl.ds(p * share, share)]

    def starts(k, carry):
        for s in range(2):
            lane = s * chunks + k
            start_ref[pl.ds(lane, 1), :] = spread(prefix, columns_d, k, s) + prefix[lane, H:H + 1, :]
        return carry

    def forward(j, state):
        rows = pl.ds(j, lanes, stride=LEN)
        state = state + gain_ref[rows, :] * times(state, packed) + resid_ref[rows, :]
        traj_ref[rows, :] = state + guess_ref[rows, :]
        return state

    lax.fori_loop(0, chunks, starts, 0)
    lax.fori_loop(0, LEN, forward, start_ref[...], unroll=True)
    for copy in done:
        copy.wait_recv()
    shares[q] = jnp.sum(parts[...], axis=0)
    exchange = [
        remote(shares.at[q], shares.at[q], send2.at[i], recv2.at[i], column_ids[i]) for i in range(column - 1)
    ]
    for copy in exchange:
        copy.start()
    for copy in exchange:
        copy.wait_recv()
    mine = pl.ds(p * share, share)
    whole[mine] = jnp.sum(shares[...], axis=0)
    last = [
        remote(whole.at[mine], whole.at[mine], send3.at[i], recv3.at[i], plane_ids[i]) for i in range(plane - 1)
    ]
    for copy in last:
        copy.start()

    @pl.when(inner)
    def _():
        for copy in x_copies(x, True):
            copy.wait_send()

    @pl.when(jnp.logical_not(inner))
    def _():
        for copy in x_copies(x, False):
            copy.wait_send()

    early = edge_copies + [core_copy, hit_copy, delta_copy, lam_copy] + z_copies + pull_copies
    for copy in early + done + exchange:
        copy.wait_send()
    for copy in last:
        copy.wait_recv()
    for copy in last:
        copy.wait_send()


def deliver(traj_ref, whole_ref, traj_hbm, recur_hbm, gin_hbm, sems):
    rows = recur_hbm.shape[0]
    copies = [
        pltpu.make_async_copy(src, dst, sems.at[i])
        for i, (src, dst) in enumerate((
            (traj_ref, traj_hbm), (whole_ref.at[pl.ds(0, rows)], recur_hbm),
            (whole_ref.at[pl.ds(rows, gin_hbm.shape[0])], gin_hbm),
        ))
    ]
    for copy in copies:
        copy.start()
    for copy in copies:
        copy.wait()


def vmem(*dims):
    return pltpu.VMEM(dims, F32)


def out(*dims):
    return jax.ShapeDtypeStruct(dims, F32)


def on_device(inputs, guess_path, recur_weight, damping, in_weight, bias_term, targets, target_steps):
    seqs, steps, hidden = guess_path.shape
    features = inputs.shape[2]
    count = seqs * steps
    chunks = steps // LEN
    lanes = seqs * chunks
    nx, nz, nc, ny = (lax.axis_size(name) for name in ("x", "z", "core", "batch"))
    plane, column = nx * ny, nz * nc
    tiles = 3 * hidden // 8
    share = tiles // plane
    extra = count + 4 * LEN
    dma = pltpu.SemaphoreType.DMA
    traj, whole = pl.pallas_call(
        newton,
        out_shape=(out(count, hidden), out(tiles, 8, hidden)),
        in_specs=[HBM] * 8,
        out_specs=[VM, VM],
        scratch_shapes=[
            vmem(count, features), vmem(count, hidden), vmem(hidden, hidden), vmem(1, hidden),
            vmem(features, hidden), vmem(1, hidden), vmem(4, hidden), pltpu.SMEM((seqs, 2), jnp.int32), dma((8,)),
            vmem(seqs, 8, hidden), vmem(extra, hidden), vmem(extra, hidden), vmem(lanes + 16, hidden),
            vmem(lanes + 4, hidden, hidden), vmem(chunks // 2, AUG, hidden), vmem(seqs, AUG, hidden),
            vmem(lanes, AUG, hidden), vmem(lanes, hidden, hidden), pltpu.VMEM((lanes, 2 * hidden, 2 * hidden), BF16),
            vmem(2, AUG, hidden), vmem(4, AUG, hidden), vmem(2, 2, AUG, hidden), vmem(nz, AUG, hidden),
            vmem(nz, hidden, hidden), vmem(nx, AUG, hidden), vmem(nx * nz, 2, hidden),
            vmem(2, 8, hidden), vmem(2, seqs, 8, hidden),
            vmem(lanes, hidden), vmem(lanes, hidden), vmem(lanes, hidden), vmem(count, hidden), vmem(count, hidden),
            vmem(tiles, 8, hidden), vmem(plane, share, 8, hidden), vmem(column, share, 8, hidden),
            dma((2,)), dma((2,)), dma((4,)), dma((4,)), dma((nz - 1,)), dma((nz - 1,)), dma((nx - 1,)), dma((nx - 1,)),
            dma((nx * nz - 1,)), dma((nx * nz - 1,)),
            dma((plane - 1,)), dma((plane - 1,)), dma((column - 1,)), dma((column - 1,)), dma((plane - 1,)),
            dma((plane - 1,)),
        ],
        compiler_params=pltpu.CompilerParams(
            collective_id=0, has_side_effects=True, vmem_limit_bytes=40 * 1024 * 1024
        ),
        name="newton",
    )(
        *(pltpu.with_memory_space_constraint(value, pltpu.HBM) for value in (
            inputs.reshape(count, features), guess_path.reshape(count, hidden), recur_weight, damping.reshape(1, hidden),
            in_weight, bias_term.reshape(1, hidden), targets.reshape(-1, hidden), target_steps,
        ))
    )
    any_space = pl.BlockSpec(memory_space=pl.ANY)
    traj, grad_recur, grad_in = pl.pallas_call(
        deliver,
        out_shape=(out(count, hidden), out(hidden, hidden), out(features, hidden)),
        in_specs=[VM, VM],
        out_specs=[any_space] * 3,
        scratch_shapes=[dma((3,))],
        compiler_params=pltpu.CompilerParams(vmem_limit_bytes=4 * 1024 * 1024),
        name="deliver",
    )(traj, whole.reshape(3 * hidden, hidden))
    return traj.reshape(guess_path.shape), grad_recur, grad_in


def solution(mesh):
    torus = Mesh(mesh.devices.reshape(4, 8, 2, mesh.shape["batch"]), (*SEQ, "batch"))
    return jax.shard_map(
        on_device,
        mesh=torus,
        in_specs=(
            P("batch", SEQ, None), P("batch", SEQ, None), P(), P(), P(), P(), P("batch", SEQ, None), P("batch", SEQ),
        ),
        out_specs=(P("batch", SEQ, None), P(), P()),
        check_vma=False,
    )
```

```python
import jax
import jax.numpy as jnp
from jax import lax
from jax.experimental import pallas as pl
from jax.experimental.pallas import tpu as pltpu
from jax.sharding import Mesh
from jax.sharding import PartitionSpec as P

H = 128
LEN = 16
TBLK = 128
AUG = 144
SENT = 136
DEPTH = 5
SEQ = ("x", "z", "core")
EULER = 0.02
F32 = jnp.float32
BF16 = jnp.bfloat16
MESH = pl.DeviceIdType.MESH
VM = pl.BlockSpec(memory_space=pltpu.VMEM)
HBM = pl.BlockSpec(memory_space=pltpu.HBM)


def split(value):
    high = value.astype(BF16)
    return high, (value - high.astype(F32)).astype(BF16)


def wide(value):
    return jnp.concatenate(split(value), axis=1)


def weights(matrix):
    row = wide(matrix)
    return jnp.concatenate([row, row], axis=0)


def times(rows, packed):
    both = jnp.dot(wide(rows), packed, preferred_element_type=F32)
    return both[:, :H] + both[:, H:]


def unit():
    line = lax.broadcasted_iota(jnp.int32, (H, H), 0)
    return jnp.where(line == lax.broadcasted_iota(jnp.int32, (H, H), 1), 1.0, 0.0).astype(F32)


def rate_matrix(weight, damping):
    return weight.T - weight - unit() * damping


def shift_down(block, first):
    line = lax.broadcasted_iota(jnp.int32, block.shape, 0)
    return jnp.where(line == 0, first, pltpu.roll(block, 1, 0))


def tail_of(rows):
    return jnp.concatenate([rows, jnp.zeros((8, H), F32)], axis=0)


def then(earlier, later, offset, eye):
    moved = earlier + times(earlier, weights(later - eye))
    return jnp.concatenate([moved[:H], moved[H:] + offset], axis=0)


def remote(src, dst, sends, recvs, target):
    return pltpu.make_async_remote_copy(
        src_ref=src, dst_ref=dst, send_sem=sends, recv_sem=recvs,
        device_id=target, device_id_type=MESH,
    )


def swap_copies(buf, axis, sends, recvs, rows):
    n = lax.axis_size(axis)
    me = lax.axis_index(axis)
    part = buf.at[me, pl.ds(0, rows)]
    farthest_first = sorted(range(1, n), key=lambda d: -min(d, n - d))
    return [
        (d, remote(part, part, sends.at[d - 1], recvs.at[d - 1], {axis: lax.rem(me + d, n)})) for d in farthest_first
    ]


def lane_sum(matrix):
    ones = jnp.ones((16, 2 * H), BF16)
    return lax.dot_general(ones, wide(matrix), (((1,), (1,)), ((), ())), preferred_element_type=F32)


def newton(
    x_hbm, guess_hbm, w_hbm, damp_hbm, u_hbm, bias_hbm, target_hbm, steps_hbm,
    traj_ref, whole,
    x_ref, guess_ref, w_ref, damp_ref, u_ref, bias_ref, target_ref, steps_ref, load_sem,
    edge, gain_ref, resid_ref, offs_ref, maps_ref, tree, totals, prefix, suffix, turned,
    pair, hit_ref, hits, zbuf, ubuf, xbuf, pulls, tiles, ends,
    start_ref, carry_ref, push_ref, source_ref, pre_ref,
    grads, parts, shares,
    edge_send, edge_recv, core_send, core_recv, zs, zr, relay_send, relay_recv, xs, xr, pull_send, pull_recv,
    send1, recv1, send2, recv2, send3, recv3,
):
    x, y, z, c = (lax.axis_index(name) for name in ("x", "batch", "z", "core"))
    nx, ny, nz, nc = (lax.axis_size(name) for name in ("x", "batch", "z", "core"))
    count = guess_ref.shape[0]
    steps = count // 2
    chunks = steps // LEN
    lanes = 2 * chunks
    blocks = TBLK // LEN

    loads = [
        pltpu.make_async_copy(src, dst, load_sem.at[i])
        for i, (src, dst) in enumerate((
            (w_hbm, w_ref), (damp_hbm, damp_ref), (guess_hbm, guess_ref), (u_hbm, u_ref), (x_hbm, x_ref),
            (bias_hbm, bias_ref), (target_hbm, target_ref), (steps_hbm, steps_ref),
        ))
    ]
    for load in loads:
        load.start()

    other = 1 - c
    sibling = {"core": other}
    plane, column = nx * ny, nz * nc
    p = x * ny + y
    q = z * nc + c
    planes = [lax.rem(p + d, plane) for d in range(1, plane)]
    columns = [lax.rem(q + d, column) for d in range(1, column)]
    plane_ids = [{"x": mate // ny, "batch": lax.rem(mate, ny)} for mate in planes]
    column_ids = [{"z": mate // nc, "core": lax.rem(mate, nc)} for mate in columns]
    place = x * column + q

    def along(where):
        return {"x": where // column, "z": lax.rem(where // nc, nz), "core": lax.rem(where, nc)}

    following = along(lax.rem(place + 1, nx * column))
    preceding = along(lax.rem(place + nx * column - 1, nx * column))
    barrier = pltpu.get_barrier_semaphore()
    chips = nx * nz
    chip = x * nz + z
    chip_ids = []
    for d in range(1, chips):
        mate = lax.rem(chip + d, chips)
        chip_ids.append({"x": mate // nz, "z": lax.rem(mate, nz)})
    z_ids = [{"z": lax.rem(z + d, nz)} for d in range(1, nz)]
    greeted = plane_ids + z_ids + [sibling, following, preceding]

    eye = unit()
    loads[0].wait()
    loads[1].wait()
    rate_t = rate_matrix(w_ref[...], damp_ref[...])
    packed = weights(rate_t)
    for load in loads[2:]:
        load.wait()
    for target in greeted:
        pl.semaphore_signal(barrier, inc=1, device_id=target, device_id_type=MESH)
    guess = guess_ref[...]

    def prev_rows(firsts):
        return jnp.concatenate(
            [shift_down(guess_ref[s * steps:(s + 1) * steps, :], firsts[s]) for s in range(2)], axis=0
        )

    zero_row = jnp.zeros((1, H), F32)
    u_pair = wide(u_ref[...])
    x_high, x_low = split(x_ref[...])
    drive = jnp.dot(x_high, u_pair, preferred_element_type=F32)
    drive = drive + jnp.dot(x_low, u_pair, preferred_element_type=F32)
    prev = prev_rows([zero_row, zero_row])
    preact = times(prev, packed) + drive[:, :H] + drive[:, H:] + bias_ref[...]
    activation = jnp.tanh(preact)
    gain_ref[0:count, :] = EULER * (1.0 - activation * activation)
    resid_ref[0:count, :] = prev + EULER * activation - guess
    early_preact = [preact[s * steps:s * steps + 1] for s in range(2)]

    edge_copies = [
        remote(guess_ref.at[pl.ds((s + 1) * steps - 8, 8)], edge.at[s], edge_send.at[s], edge_recv.at[s], following)
        for s in range(2)
    ]
    chunk_line = lax.broadcasted_iota(jnp.int32, (LEN, H), 0)

    def begin(s):
        gains = jnp.where(chunk_line == 0, 0.0, gain_ref[pl.ds(s * steps, chunks, stride=LEN), :])
        for k in range(chunks):
            maps_ref[s * chunks + k] = eye + rate_t * gains[k:k + 1]
        offs_ref[s * chunks:(s + 1) * chunks, :] = jnp.where(
            chunk_line == 0, 0.0, resid_ref[pl.ds(s * steps, chunks, stride=LEN), :]
        )

    def step_maps(base, size, gains, resid):
        for first in range(0, size, 4):
            state = maps_ref[base + first:base + first + 4].reshape(4 * H, H)
            if first + 4 == size:
                state = jnp.concatenate([state, offs_ref[base:base + 16, :]], axis=0)
            moved = times(state, packed)
            for i in range(4):
                here = slice(i * H, (i + 1) * H)
                maps_ref[base + first + i] = state[here] + gains[first + i:first + i + 1] * moved[here]
            if first + 4 == size:
                offs_ref[base:base + 16, :] = state[4 * H:] + gains * moved[4 * H:] + resid

    def compose(s, begin_at, end_at):
        def body(i, carry):
            for u in range(DEPTH):
                j = 1 + DEPTH * i + u
                rows = pl.ds(s * steps + j, chunks, stride=LEN)
                step_maps(s * chunks, chunks, gain_ref[rows, :], resid_ref[rows, :])
            return carry

        lax.fori_loop(begin_at, end_at, body, 0)

    first_row = chunk_line == 0

    def offset_of(lane):
        return jnp.where(first_row, offs_ref[pl.ds(lane, 1), :], 0.0)

    def lane_rows(lane):
        return jnp.concatenate([maps_ref[lane], offset_of(lane)], axis=0)

    def finish(s):
        lane = s * chunks
        gain = gain_ref[s * steps:s * steps + 1, :]
        resid = jnp.where(first_row, resid_ref[s * steps:s * steps + 1, :], 0.0)
        step = jnp.concatenate([eye + rate_t * gain, resid], axis=0)
        whole_chunk = then(step, maps_ref[lane], offset_of(lane), eye)
        maps_ref[lane] = whole_chunk[:H]
        offs_ref[lane:lane + 1, :] = whole_chunk[H:H + 1]
        for k in range(chunks // 2):
            tree[k] = then(lane_rows(lane + 2 * k), maps_ref[lane + 2 * k + 1], offset_of(lane + 2 * k + 1), eye)
        size = chunks // 2
        while size > 1:
            for k in range(size // 2):
                joined = then(tree[2 * k], tree[2 * k + 1, :H, :], tree[2 * k + 1, H:, :], eye)
                if size == 2:
                    totals[s] = joined
                else:
                    tree[k] = joined
            size //= 2

    core_copy = remote(
        totals.at[other, pl.ds(0, SENT)], pair.at[c, pl.ds(0, SENT)], core_send.at[0], core_recv.at[0], sibling
    )
    quarter = nz // 4
    pieces = (pl.ds(0, 72), pl.ds(72, SENT - 72))
    relays = []
    for i, (toward, piece) in enumerate(zip((quarter, nz - quarter), pieces)):
        part = zbuf.at[lax.rem(z + nz - toward, nz), piece]
        relays.append(remote(part, part, relay_send.at[i], relay_recv.at[i], {"z": lax.rem(z + toward, nz)}))
    first_legs = [copy for d, copy in swap_copies(zbuf, "z", zs, zr, SENT) if d in (quarter, nz - quarter)]
    other_legs = [copy for d, copy in swap_copies(zbuf, "z", zs, zr, SENT) if d not in (quarter, nz // 2, nz - quarter)]

    def pass_on():
        for copy in first_legs:
            copy.wait_recv()
        for copy in relays:
            copy.start()

    def leave():
        core_copy.wait_recv()
        pair[c] = totals[c]
        zbuf[z] = then(
            jnp.concatenate([pair[0, :H, :], tail_of(pair[0, H:SENT, :])], axis=0),
            pair[1, :H, :], tail_of(pair[1, H:SENT, :]), eye,
        )
        for copy in first_legs + other_legs:
            copy.start()

    begin(0)
    compose(0, 0, 2)
    pl.semaphore_wait(barrier, len(greeted))
    for copy in edge_copies:
        copy.start()
    compose(0, 2, (LEN - 1) // DEPTH)
    begin(1)
    for copy in edge_copies:
        copy.wait_recv()
    at_start = jnp.where(place > 0, 1.0, 0.0)
    firsts = [edge[s, 7:8, :] * at_start for s in range(2)]
    added = times(jnp.concatenate(firsts + [jnp.zeros((14, H), F32)], axis=0), packed)
    for s in range(2):
        row = slice(s * steps, s * steps + 1)
        activation = jnp.tanh(early_preact[s] + added[s:s + 1])
        gain_ref[row, :] = EULER * (1.0 - activation * activation)
        resid_ref[row, :] = firsts[s] + EULER * activation - guess_ref[row, :]
    finish(0)

    @pl.when(c == 1)
    def _():
        core_copy.start()

    compose(1, 0, 1)

    @pl.when(c == 0)
    def _():
        leave()

    compose(1, 1, (LEN - 1) // DEPTH)
    finish(1)

    @pl.when(c == 0)
    def _():
        core_copy.start()
        pass_on()

    for s in range(2):
        for h in range(2):
            n = 2 * s + h
            step = steps_ref[s, h]
            kept = chunk_line <= lax.rem(step, LEN)
            to = slice(count + n * LEN, count + (n + 1) * LEN)
            for ref in (gain_ref, resid_ref):
                rows = jnp.zeros((LEN, H), F32)
                for k in range(blocks):
                    base = s * steps + h * TBLK + k * LEN
                    rows = jnp.where(chunk_line * 0 + step // LEN == k, ref[base:base + LEN, :], rows)
                ref[to, :] = jnp.where(kept, rows, 0.0)
    hit_pad = jnp.zeros((12, H), F32)

    def hit_rows(ref, j):
        return jnp.concatenate([ref[pl.ds(count + j, 4, stride=LEN), :], hit_pad], axis=0)

    gains = hit_rows(gain_ref, 0)
    for n in range(4):
        maps_ref[lanes + n] = eye + rate_t * gains[n:n + 1]
    offs_ref[lanes:lanes + 16, :] = hit_rows(resid_ref, 0)

    def compose_hits(begin_at, end_at):
        def body(i, carry):
            for u in range(DEPTH):
                j = 1 + DEPTH * i + u
                step_maps(lanes, 4, hit_rows(gain_ref, j), hit_rows(resid_ref, j))
            return carry

        lax.fori_loop(begin_at, end_at, body, 0)

    compose_hits(0, 2)

    @pl.when(c == 1)
    def _():
        leave()

    compose_hits(2, (LEN - 1) // DEPTH)

    start = jnp.concatenate([eye, jnp.zeros((16, H), F32)], axis=0)

    def chain(k, carry):
        out = []
        for s in range(2):
            lane = s * chunks + k
            prefix[lane] = carry[s]
            out.append(then(carry[s], maps_ref[lane], offset_of(lane), eye))
        return tuple(out)

    lax.fori_loop(0, chunks, chain, (start, start))

    @pl.when(c == 1)
    def _():
        pass_on()

    block_line = lax.broadcasted_iota(jnp.int32, (TBLK, H), 0)
    map_line = jnp.zeros((AUG, H), jnp.int32)
    for s in range(2):
        for h in range(2):
            n = 2 * s + h
            step = steps_ref[s, h]
            run = jnp.zeros((AUG, H), F32)
            for k in range(blocks):
                run = jnp.where(map_line + step // LEN == k, prefix[s * chunks + h * blocks + k], run)
            base = s * steps + h * TBLK
            here = jnp.where(block_line == step, guess_ref[base:base + TBLK, :], 0.0)
            miss = offs_ref[lanes + n:lanes + n + 1, :] + jnp.sum(here, axis=0, keepdims=True)
            miss = miss - target_ref[n:n + 1, :]
            hit_ref[n] = then(run, maps_ref[lanes + n], jnp.where(first_row, miss, 0.0), eye)
    hit_copy = remote(
        hit_ref.at[pl.ds(2 * other, 2)], hits.at[c], core_send.at[1], core_recv.at[1], sibling
    )
    hit_copy.start()
    hits[c] = hit_ref[pl.ds(2 * c, 2)]

    def back_chain(i, carry):
        k = chunks - 1 - i
        out = []
        for s in range(2):
            lane = s * chunks + k
            suffix[lane] = carry[s]
            turn = weights((maps_ref[lane] - eye).T)
            turned[lane] = turn
            out.append(carry[s] + times(carry[s], turn))
        return tuple(out)

    lax.fori_loop(0, chunks, back_chain, (eye, eye))

    for copy in other_legs + relays:
        copy.wait_recv()
    size = nz
    while size > 1:
        for k in range(size // 2):
            table = zbuf if size == nz else tree
            ends_at = [tail_of(table[2 * k + i, H:SENT, :]) for i in range(2)]
            left = jnp.concatenate([table[2 * k, :H, :], ends_at[0]], axis=0)
            joined = then(left, table[2 * k + 1, :H, :], ends_at[1], eye)
            if size == 2:
                xbuf[x] = joined
            else:
                tree[k] = joined
        size //= 2
    inner = jnp.logical_and(x > 0, x < nx - 1)

    def x_copy(slot, full, d):
        part = xbuf.at[slot, pl.ds(0, SENT) if full else pl.ds(H, 8)]
        return remote(part, part, xs.at[d - 1], xr.at[d - 1], {"x": lax.rem(x + d, nx)})

    def x_copies(slot, full):
        return [x_copy(slot, full, d) for d in range(1, nx)]

    @pl.when(inner)
    def _():
        for copy in x_copies(x, True):
            copy.start()

    @pl.when(jnp.logical_not(inner))
    def _():
        for copy in x_copies(x, False):
            copy.start()

    run = jnp.concatenate([zbuf[0, :H, :], tail_of(zbuf[0, H:SENT, :])], axis=0)
    ahead = start
    after = eye
    for k in range(1, nz):
        ahead = jnp.where(k == z, run, ahead)
        ubuf[k] = after
        moved = times(jnp.concatenate([run, after], axis=0), weights(zbuf[k, :H, :] - eye))
        offset = tail_of(zbuf[k, H:SENT, :])
        run = run + moved[:AUG] + jnp.concatenate([jnp.zeros((H, H), F32), offset], axis=0)
        after = jnp.where(k > z, after + moved[AUG:], after)
    hit_copy.wait_recv()
    first_map = jnp.concatenate([pair[0, :H, :], tail_of(pair[0, H:SENT, :])], axis=0)
    late = [then(first_map, hits[1, h, :H, :], hits[1, h, H:, :], eye) for h in range(2)]
    w_ahead = weights(ahead[:H] - eye)
    w_first = weights(pair[0, :H, :] - eye)
    w_hits = [weights(hits[0, h, :H, :] - eye) for h in range(2)] + [weights(late[h][:H] - eye) for h in range(2)]
    t_hits = [weights(hits[0, h, :H, :].T) for h in range(2)] + [weights(late[h][:H].T) for h in range(2)]
    t_late = [weights(hits[1, h, :H, :].T) for h in range(2)]
    t_ahead = weights(ahead[:H].T)
    miss_rows = [hits[0, h, H:, :] for h in range(2)] + [late[h][H:] for h in range(2)]

    for d in range(1, nx):
        source = lax.rem(x + nx - d, nx)
        source_inner = jnp.logical_and(source > 0, source < nx - 1)

        @pl.when(source_inner)
        def _():
            x_copy(source, True, d).wait_recv()

        @pl.when(jnp.logical_not(source_inner))
        def _():
            x_copy(source, False, d).wait_recv()

    v = jnp.where(x > 0, tail_of(xbuf[0, H:SENT, :]), 0.0)
    for k in range(1, nx - 1):
        moved = v + times(v, weights(xbuf[k, :H, :] - eye)) + tail_of(xbuf[k, H:SENT, :])
        v = jnp.where(k < x, moved, v)
    v = v + times(v, w_ahead) + ahead[H:]
    scale = 0.125
    misses = [(v + times(v, w_hits[i]) + miss_rows[i]) * scale for i in range(4)]
    pull = jnp.zeros((16, H), F32)
    for i in range(4):
        pull = pull + times(misses[i], t_hits[i])
    far = times(pull, t_ahead)
    line = lax.broadcasted_iota(jnp.int32, (8, H), 0)
    pulls[chip] = jnp.concatenate([pull[0:1], far[0:1]], axis=0)
    pull_copies = [
        remote(pulls.at[chip], pulls.at[chip], pull_send.at[i], pull_recv.at[i], chip_ids[i]) for i in range(chips - 1)
    ]
    for copy in pull_copies:
        copy.start()
    v_late = v + times(v, w_first) + tail_of(pair[0, H:SENT, :])
    ends[0, c] = jnp.where(c == 0, v[:8], v_late[:8])
    tiles[0] = jnp.where(c == 0, v_late[:8], v[:8])
    delta_copy = remote(tiles.at[0], ends.at[0, c], core_send.at[2], core_recv.at[2], sibling)
    delta_copy.start()
    pull_late = times(misses[2], t_late[0]) + times(misses[3], t_late[1])
    delta_copy.wait_recv()

    lane_line = lax.broadcasted_iota(jnp.int32, (lanes, H), 0)
    pushes = jnp.zeros((lanes, H), F32)
    columns_d = [jnp.broadcast_to(ends[0, s, 0:1, :], (H, H)).T for s in range(2)]
    for s in range(2):
        for h in range(2):
            n = 2 * s + h
            step = steps_ref[s, h]
            miss = jnp.sum(hit_ref[n, :H, :] * columns_d[s], axis=0, keepdims=True) + hit_ref[n, H:H + 1, :]
            miss = miss * scale
            source_ref[s * steps + h * TBLK:s * steps + (h + 1) * TBLK, :] = jnp.where(block_line == step, miss, 0.0)
            pushed = times(jnp.broadcast_to(miss, (16, H)), weights(maps_ref[lanes + n].T))
            pushes = pushes + jnp.where(lane_line == s * chunks + h * blocks + step // LEN, pushed[0:1], 0.0)
    push_ref[...] = pushes

    def spread(table, columns, k, s):
        lane = s * chunks + k
        return jnp.sum(table[lane, :H, :] * columns[s], axis=0, keepdims=True)

    def local_back(j, carry):
        k = chunks - 1 - j
        out = []
        for s, t in enumerate(carry):
            lane = s * chunks + k
            carry_ref[pl.ds(lane, 1), :] = t[0:1]
            out.append(t + times(t, turned[lane]) + push_ref[pl.ds(lane, 1), :])
        return tuple(out)

    nothing = jnp.zeros((16, H), F32)
    lax.fori_loop(0, chunks, local_back, (nothing, nothing), unroll=True)
    t_first = weights((pair[1, :H, :] - eye).T)
    t_after = weights((after - eye).T)
    t_rows = {k: weights((xbuf[k, :H, :] - eye).T) for k in range(1, nx - 1)}

    for copy in pull_copies:
        copy.wait_recv()
    total = jnp.zeros((H, H), F32)
    for k in range(1, nz):
        total = total + jnp.where(k > z, ubuf[k] * pulls[x * nz + k, 0:1, :], 0.0)
    near = lane_sum(total)
    row_pulls = []
    for k in range(nx):
        row = pulls[k * nz]
        for i in range(1, nz):
            row = row + pulls[k * nz + i]
        row_pulls.append(row)
    t = jnp.where(nx - 1 > x, jnp.broadcast_to(row_pulls[nx - 1][1:2], (16, H)), 0.0)
    for k in range(nx - 2, 0, -1):
        t = jnp.where(k > x, t + times(t, t_rows[k]) + row_pulls[k][1:2], t)
    lam_late = near + t + times(t, t_after)
    lam = lam_late + times(lam_late, t_first) + pull_late
    ends[1, c] = jnp.where(c == 0, lam[:8], lam_late[:8])
    tiles[1] = jnp.where(c == 0, lam_late[:8], lam[:8])
    lam_copy = remote(tiles.at[1], ends.at[1, c], core_send.at[3], core_recv.at[3], sibling)
    lam_copy.start()
    packed_t = weights(rate_t.T)

    def add_carries(s):
        spread_row = jnp.broadcast_to(ends[1, s, 0:1, :], (H, H)).T

        def body(i, carry):
            for u in range(4):
                lane = s * chunks + 4 * i + u
                rows = pl.ds(lane, 1)
                moved = jnp.sum(suffix[lane] * spread_row, axis=0, keepdims=True)
                carry_ref[rows, :] = carry_ref[rows, :] + moved
            return carry

        lax.fori_loop(0, chunks // 4, body, 0)

    add_carries(c)
    lam_copy.wait_recv()
    add_carries(other)
    def backward(j, adjoint):
        rows = pl.ds(LEN - 1 - j, lanes, stride=LEN)
        adjoint = adjoint + source_ref[rows, :]
        scaled = gain_ref[rows, :] * adjoint
        pre_ref[rows, :] = scaled
        return adjoint + times(scaled, packed_t)

    lax.fori_loop(0, LEN, backward, carry_ref[...], unroll=True)
    left_high, left_low = split(jnp.concatenate([prev_rows([edge[s, 7:8, :] * at_start for s in range(2)]), x_ref[...]], axis=1))
    right = wide(pre_ref[...])
    dims = (((0,), (0,)), ((), ()))
    both = lax.dot_general(left_high, right, dims, preferred_element_type=F32)
    both = both + lax.dot_general(left_low, right, dims, preferred_element_type=F32)
    sums = both[:, :H] + both[:, H:]
    grads[0:H // 8] = (sums[:H].T - sums[:H]).reshape(H // 8, 8, H)
    grads[H // 8:] = sums[H:].reshape(2 * H // 8, 8, H)

    share = grads.shape[0] // plane
    done = []
    for i in range(plane - 1):
        done.append(remote(
            grads.at[pl.ds(planes[i] * share, share)], parts.at[p], send1.at[i], recv1.at[i], plane_ids[i]
        ))
        done[-1].start()
    parts[p] = grads[pl.ds(p * share, share)]

    def starts(k, carry):
        for s in range(2):
            lane = s * chunks + k
            start_ref[pl.ds(lane, 1), :] = spread(prefix, columns_d, k, s) + prefix[lane, H:H + 1, :]
        return carry

    def forward(j, state):
        rows = pl.ds(j, lanes, stride=LEN)
        state = state + gain_ref[rows, :] * times(state, packed) + resid_ref[rows, :]
        traj_ref[rows, :] = state + guess_ref[rows, :]
        return state

    lax.fori_loop(0, chunks, starts, 0)
    lax.fori_loop(0, LEN, forward, start_ref[...], unroll=True)
    for copy in done:
        copy.wait_recv()
    shares[q] = jnp.sum(parts[...], axis=0)
    exchange = [
        remote(shares.at[q], shares.at[q], send2.at[i], recv2.at[i], column_ids[i]) for i in range(column - 1)
    ]
    for copy in exchange:
        copy.start()
    for copy in exchange:
        copy.wait_recv()
    mine = pl.ds(p * share, share)
    whole[mine] = jnp.sum(shares[...], axis=0)
    last = [
        remote(whole.at[mine], whole.at[mine], send3.at[i], recv3.at[i], plane_ids[i]) for i in range(plane - 1)
    ]
    for copy in last:
        copy.start()

    @pl.when(inner)
    def _():
        for copy in x_copies(x, True):
            copy.wait_send()

    @pl.when(jnp.logical_not(inner))
    def _():
        for copy in x_copies(x, False):
            copy.wait_send()

    early = edge_copies + [core_copy, hit_copy, delta_copy, lam_copy] + first_legs + other_legs + relays + pull_copies
    for copy in early + done + exchange:
        copy.wait_send()
    for copy in last:
        copy.wait_recv()
    for copy in last:
        copy.wait_send()


def deliver(traj_ref, whole_ref, traj_hbm, recur_hbm, gin_hbm, sems):
    rows = recur_hbm.shape[0]
    copies = [
        pltpu.make_async_copy(src, dst, sems.at[i])
        for i, (src, dst) in enumerate((
            (traj_ref, traj_hbm), (whole_ref.at[pl.ds(0, rows)], recur_hbm),
            (whole_ref.at[pl.ds(rows, gin_hbm.shape[0])], gin_hbm),
        ))
    ]
    for copy in copies:
        copy.start()
    for copy in copies:
        copy.wait()


def vmem(*dims):
    return pltpu.VMEM(dims, F32)


def out(*dims):
    return jax.ShapeDtypeStruct(dims, F32)


def on_device(inputs, guess_path, recur_weight, damping, in_weight, bias_term, targets, target_steps):
    seqs, steps, hidden = guess_path.shape
    features = inputs.shape[2]
    count = seqs * steps
    chunks = steps // LEN
    lanes = seqs * chunks
    nx, nz, nc, ny = (lax.axis_size(name) for name in ("x", "z", "core", "batch"))
    plane, column = nx * ny, nz * nc
    tiles = 3 * hidden // 8
    share = tiles // plane
    extra = count + 4 * LEN
    dma = pltpu.SemaphoreType.DMA
    traj, whole = pl.pallas_call(
        newton,
        out_shape=(out(count, hidden), out(tiles, 8, hidden)),
        in_specs=[HBM] * 8,
        out_specs=[VM, VM],
        scratch_shapes=[
            vmem(count, features), vmem(count, hidden), vmem(hidden, hidden), vmem(1, hidden),
            vmem(features, hidden), vmem(1, hidden), vmem(4, hidden), pltpu.SMEM((seqs, 2), jnp.int32), dma((8,)),
            vmem(seqs, 8, hidden), vmem(extra, hidden), vmem(extra, hidden), vmem(lanes + 16, hidden),
            vmem(lanes + 4, hidden, hidden), vmem(chunks // 2, AUG, hidden), vmem(seqs, AUG, hidden),
            vmem(lanes, AUG, hidden), vmem(lanes, hidden, hidden), pltpu.VMEM((lanes, 2 * hidden, 2 * hidden), BF16),
            vmem(2, AUG, hidden), vmem(4, AUG, hidden), vmem(2, 2, AUG, hidden), vmem(nz, AUG, hidden),
            vmem(nz, hidden, hidden), vmem(nx, AUG, hidden), vmem(nx * nz, 2, hidden),
            vmem(2, 8, hidden), vmem(2, seqs, 8, hidden),
            vmem(lanes, hidden), vmem(lanes, hidden), vmem(lanes, hidden), vmem(count, hidden), vmem(count, hidden),
            vmem(tiles, 8, hidden), vmem(plane, share, 8, hidden), vmem(column, share, 8, hidden),
            dma((2,)), dma((2,)), dma((4,)), dma((4,)), dma((nz - 1,)), dma((nz - 1,)), dma((2,)), dma((2,)), dma((nx - 1,)), dma((nx - 1,)),
            dma((nx * nz - 1,)), dma((nx * nz - 1,)),
            dma((plane - 1,)), dma((plane - 1,)), dma((column - 1,)), dma((column - 1,)), dma((plane - 1,)),
            dma((plane - 1,)),
        ],
        compiler_params=pltpu.CompilerParams(
            collective_id=0, has_side_effects=True, vmem_limit_bytes=40 * 1024 * 1024
        ),
        name="newton",
    )(
        *(pltpu.with_memory_space_constraint(value, pltpu.HBM) for value in (
            inputs.reshape(count, features), guess_path.reshape(count, hidden), recur_weight, damping.reshape(1, hidden),
            in_weight, bias_term.reshape(1, hidden), targets.reshape(-1, hidden), target_steps,
        ))
    )
    any_space = pl.BlockSpec(memory_space=pl.ANY)
    traj, grad_recur, grad_in = pl.pallas_call(
        deliver,
        out_shape=(out(count, hidden), out(hidden, hidden), out(features, hidden)),
        in_specs=[VM, VM],
        out_specs=[any_space] * 3,
        scratch_shapes=[dma((3,))],
        compiler_params=pltpu.CompilerParams(vmem_limit_bytes=4 * 1024 * 1024),
        name="deliver",
    )(traj, whole.reshape(3 * hidden, hidden))
    return traj.reshape(guess_path.shape), grad_recur, grad_in


def solution(mesh):
    torus = Mesh(mesh.devices.reshape(4, 8, 2, mesh.shape["batch"]), (*SEQ, "batch"))
    return jax.shard_map(
        on_device,
        mesh=torus,
        in_specs=(
            P("batch", SEQ, None), P("batch", SEQ, None), P(), P(), P(), P(), P("batch", SEQ, None), P("batch", SEQ),
        ),
        out_specs=(P("batch", SEQ, None), P(), P()),
        check_vma=False,
    )
```

```python
import jax
import jax.numpy as jnp
from jax import lax
from jax.experimental import pallas as pl
from jax.experimental.pallas import tpu as pltpu
from jax.sharding import Mesh
from jax.sharding import PartitionSpec as P

H = 128
LEN = 16
TBLK = 128
AUG = 144
SENT = 136
DEPTH = 5
SEQ = ("x", "z", "core")
EULER = 0.02
F32 = jnp.float32
BF16 = jnp.bfloat16
MESH = pl.DeviceIdType.MESH
VM = pl.BlockSpec(memory_space=pltpu.VMEM)
HBM = pl.BlockSpec(memory_space=pltpu.HBM)


def split(value):
    high = value.astype(BF16)
    return high, (value - high.astype(F32)).astype(BF16)


def wide(value):
    return jnp.concatenate(split(value), axis=1)


def weights(matrix):
    row = wide(matrix)
    return jnp.concatenate([row, row], axis=0)


def times(rows, packed):
    both = jnp.dot(wide(rows), packed, preferred_element_type=F32)
    return both[:, :H] + both[:, H:]


def unit():
    line = lax.broadcasted_iota(jnp.int32, (H, H), 0)
    return jnp.where(line == lax.broadcasted_iota(jnp.int32, (H, H), 1), 1.0, 0.0).astype(F32)


def rate_matrix(weight, damping):
    return weight.T - weight - unit() * damping


def shift_down(block, first):
    line = lax.broadcasted_iota(jnp.int32, block.shape, 0)
    return jnp.where(line == 0, first, pltpu.roll(block, 1, 0))


def tail_of(rows):
    return jnp.concatenate([rows, jnp.zeros((8, H), F32)], axis=0)


def then(earlier, later, offset, eye):
    moved = earlier + times(earlier, weights(later - eye))
    return jnp.concatenate([moved[:H], moved[H:] + offset], axis=0)


def remote(src, dst, sends, recvs, target):
    return pltpu.make_async_remote_copy(
        src_ref=src, dst_ref=dst, send_sem=sends, recv_sem=recvs,
        device_id=target, device_id_type=MESH,
    )


def swap_copies(buf, axis, sends, recvs, rows):
    n = lax.axis_size(axis)
    me = lax.axis_index(axis)
    part = buf.at[me, pl.ds(0, rows)]
    farthest_first = sorted(range(1, n), key=lambda d: -min(d, n - d))
    return [
        (d, remote(part, part, sends.at[d - 1], recvs.at[d - 1], {axis: lax.rem(me + d, n)})) for d in farthest_first
    ]


def lane_sum(matrix):
    ones = jnp.ones((16, 2 * H), BF16)
    return lax.dot_general(ones, wide(matrix), (((1,), (1,)), ((), ())), preferred_element_type=F32)


def newton(
    x_hbm, guess_hbm, w_hbm, damp_hbm, u_hbm, bias_hbm, target_hbm, steps_hbm,
    traj_ref, whole,
    x_ref, guess_ref, w_ref, damp_ref, u_ref, bias_ref, target_ref, steps_ref, load_sem,
    edge, gain_ref, resid_ref, offs_ref, maps_ref, tree, totals, prefix, suffix, turned,
    pair, hit_ref, hits, zbuf, ubuf, xbuf, pulls, tiles, ends,
    start_ref, carry_ref, push_ref, source_ref, pre_ref,
    grads, parts, shares,
    edge_send, edge_recv, core_send, core_recv, zs, zr, relay_send, relay_recv, xs, xr, pull_send, pull_recv,
    send1, recv1, send2, recv2, send3, recv3,
):
    x, y, z, c = (lax.axis_index(name) for name in ("x", "batch", "z", "core"))
    nx, ny, nz, nc = (lax.axis_size(name) for name in ("x", "batch", "z", "core"))
    count = guess_ref.shape[0]
    steps = count // 2
    chunks = steps // LEN
    lanes = 2 * chunks
    blocks = TBLK // LEN

    loads = [
        pltpu.make_async_copy(src, dst, load_sem.at[i])
        for i, (src, dst) in enumerate((
            (w_hbm, w_ref), (damp_hbm, damp_ref), (guess_hbm, guess_ref), (u_hbm, u_ref), (x_hbm, x_ref),
            (bias_hbm, bias_ref), (target_hbm, target_ref), (steps_hbm, steps_ref),
        ))
    ]
    for load in loads:
        load.start()

    other = 1 - c
    sibling = {"core": other}
    plane, column = nx * ny, nz * nc
    p = x * ny + y
    q = z * nc + c

    def mates(axes):
        (one, here, first), (two, there, second) = axes
        offsets = [(i, j) for i in range(first) for j in range(second) if i or j]
        offsets.sort(key=lambda o: -min(o[0], first - o[0]) - (0 if two == "core" else min(o[1], second - o[1])))
        return [{one: lax.rem(here + i, first), two: lax.rem(there + j, second)} for i, j in offsets]

    plane_ids = mates((("x", x, nx), ("batch", y, ny)))
    planes = [mate["x"] * ny + mate["batch"] for mate in plane_ids]
    place = x * column + q

    def along(where):
        return {"x": where // column, "z": lax.rem(where // nc, nz), "core": lax.rem(where, nc)}

    following = along(lax.rem(place + 1, nx * column))
    preceding = along(lax.rem(place + nx * column - 1, nx * column))
    barrier = pltpu.get_barrier_semaphore()
    chips = nx * nz
    chip = x * nz + z
    z_ids = [{"z": lax.rem(z + d, nz)} for d in range(1, nz)]
    greeted = plane_ids + z_ids + [sibling, following, preceding]

    eye = unit()
    loads[0].wait()
    loads[1].wait()
    rate_t = rate_matrix(w_ref[...], damp_ref[...])
    packed = weights(rate_t)
    for load in loads[2:]:
        load.wait()
    for target in greeted:
        pl.semaphore_signal(barrier, inc=1, device_id=target, device_id_type=MESH)
    guess = guess_ref[...]

    def prev_rows(firsts):
        return jnp.concatenate(
            [shift_down(guess_ref[s * steps:(s + 1) * steps, :], firsts[s]) for s in range(2)], axis=0
        )

    zero_row = jnp.zeros((1, H), F32)
    u_pair = wide(u_ref[...])
    x_high, x_low = split(x_ref[...])
    drive = jnp.dot(x_high, u_pair, preferred_element_type=F32)
    drive = drive + jnp.dot(x_low, u_pair, preferred_element_type=F32)
    prev = prev_rows([zero_row, zero_row])
    preact = times(prev, packed) + drive[:, :H] + drive[:, H:] + bias_ref[...]
    activation = jnp.tanh(preact)
    gain_ref[0:count, :] = EULER * (1.0 - activation * activation)
    resid_ref[0:count, :] = prev + EULER * activation - guess
    early_preact = [preact[s * steps:s * steps + 1] for s in range(2)]

    edge_copies = [
        remote(guess_ref.at[pl.ds((s + 1) * steps - 8, 8)], edge.at[s], edge_send.at[s], edge_recv.at[s], following)
        for s in range(2)
    ]
    chunk_line = lax.broadcasted_iota(jnp.int32, (LEN, H), 0)

    def begin(s):
        gains = jnp.where(chunk_line == 0, 0.0, gain_ref[pl.ds(s * steps, chunks, stride=LEN), :])
        for k in range(chunks):
            maps_ref[s * chunks + k] = eye + rate_t * gains[k:k + 1]
        offs_ref[s * chunks:(s + 1) * chunks, :] = jnp.where(
            chunk_line == 0, 0.0, resid_ref[pl.ds(s * steps, chunks, stride=LEN), :]
        )

    def step_maps(base, size, gains, resid):
        for first in range(0, size, 4):
            state = maps_ref[base + first:base + first + 4].reshape(4 * H, H)
            if first + 4 == size:
                state = jnp.concatenate([state, offs_ref[base:base + 16, :]], axis=0)
            moved = times(state, packed)
            for i in range(4):
                here = slice(i * H, (i + 1) * H)
                maps_ref[base + first + i] = state[here] + gains[first + i:first + i + 1] * moved[here]
            if first + 4 == size:
                offs_ref[base:base + 16, :] = state[4 * H:] + gains * moved[4 * H:] + resid

    def compose(s, begin_at, end_at):
        def body(i, carry):
            for u in range(DEPTH):
                j = 1 + DEPTH * i + u
                rows = pl.ds(s * steps + j, chunks, stride=LEN)
                step_maps(s * chunks, chunks, gain_ref[rows, :], resid_ref[rows, :])
            return carry

        lax.fori_loop(begin_at, end_at, body, 0)

    first_row = chunk_line == 0

    def offset_of(lane):
        return jnp.where(first_row, offs_ref[pl.ds(lane, 1), :], 0.0)

    def lane_rows(lane):
        return jnp.concatenate([maps_ref[lane], offset_of(lane)], axis=0)

    def finish(s):
        lane = s * chunks
        gain = gain_ref[s * steps:s * steps + 1, :]
        resid = jnp.where(first_row, resid_ref[s * steps:s * steps + 1, :], 0.0)
        step = jnp.concatenate([eye + rate_t * gain, resid], axis=0)
        whole_chunk = then(step, maps_ref[lane], offset_of(lane), eye)
        maps_ref[lane] = whole_chunk[:H]
        offs_ref[lane:lane + 1, :] = whole_chunk[H:H + 1]
        for k in range(chunks // 2):
            tree[k] = then(lane_rows(lane + 2 * k), maps_ref[lane + 2 * k + 1], offset_of(lane + 2 * k + 1), eye)
        size = chunks // 2
        while size > 1:
            for k in range(size // 2):
                joined = then(tree[2 * k], tree[2 * k + 1, :H, :], tree[2 * k + 1, H:, :], eye)
                if size == 2:
                    totals[s] = joined
                else:
                    tree[k] = joined
            size //= 2

    core_copy = remote(
        totals.at[other, pl.ds(0, SENT)], pair.at[c, pl.ds(0, SENT)], core_send.at[0], core_recv.at[0], sibling
    )
    quarter = nz // 4
    pieces = (pl.ds(0, 72), pl.ds(72, SENT - 72))
    relays = []
    for i, (toward, piece) in enumerate(zip((quarter, nz - quarter), pieces)):
        part = zbuf.at[lax.rem(z + nz - toward, nz), piece]
        relays.append(remote(part, part, relay_send.at[i], relay_recv.at[i], {"z": lax.rem(z + toward, nz)}))
    first_legs = [copy for d, copy in swap_copies(zbuf, "z", zs, zr, SENT) if d in (quarter, nz - quarter)]
    other_legs = [copy for d, copy in swap_copies(zbuf, "z", zs, zr, SENT) if d not in (quarter, nz // 2, nz - quarter)]

    def pass_on():
        for copy in first_legs:
            copy.wait_recv()
        for copy in relays:
            copy.start()

    def leave():
        core_copy.wait_recv()
        pair[c] = totals[c]
        zbuf[z] = then(
            jnp.concatenate([pair[0, :H, :], tail_of(pair[0, H:SENT, :])], axis=0),
            pair[1, :H, :], tail_of(pair[1, H:SENT, :]), eye,
        )
        for copy in first_legs + other_legs:
            copy.start()

    begin(0)
    compose(0, 0, 2)
    pl.semaphore_wait(barrier, len(greeted))
    for copy in edge_copies:
        copy.start()
    compose(0, 2, (LEN - 1) // DEPTH)
    begin(1)
    for copy in edge_copies:
        copy.wait_recv()
    at_start = jnp.where(place > 0, 1.0, 0.0)
    firsts = [edge[s, 7:8, :] * at_start for s in range(2)]
    added = times(jnp.concatenate(firsts + [jnp.zeros((14, H), F32)], axis=0), packed)
    for s in range(2):
        row = slice(s * steps, s * steps + 1)
        activation = jnp.tanh(early_preact[s] + added[s:s + 1])
        gain_ref[row, :] = EULER * (1.0 - activation * activation)
        resid_ref[row, :] = firsts[s] + EULER * activation - guess_ref[row, :]
    finish(0)

    @pl.when(c == 1)
    def _():
        core_copy.start()

    compose(1, 0, 1)

    @pl.when(c == 0)
    def _():
        leave()

    compose(1, 1, (LEN - 1) // DEPTH)
    finish(1)

    @pl.when(c == 0)
    def _():
        core_copy.start()
        pass_on()

    for s in range(2):
        for h in range(2):
            n = 2 * s + h
            step = steps_ref[s, h]
            kept = chunk_line <= lax.rem(step, LEN)
            to = slice(count + n * LEN, count + (n + 1) * LEN)
            for ref in (gain_ref, resid_ref):
                rows = jnp.zeros((LEN, H), F32)
                for k in range(blocks):
                    base = s * steps + h * TBLK + k * LEN
                    rows = jnp.where(chunk_line * 0 + step // LEN == k, ref[base:base + LEN, :], rows)
                ref[to, :] = jnp.where(kept, rows, 0.0)
    hit_pad = jnp.zeros((12, H), F32)

    def hit_rows(ref, j):
        return jnp.concatenate([ref[pl.ds(count + j, 4, stride=LEN), :], hit_pad], axis=0)

    gains = hit_rows(gain_ref, 0)
    for n in range(4):
        maps_ref[lanes + n] = eye + rate_t * gains[n:n + 1]
    offs_ref[lanes:lanes + 16, :] = hit_rows(resid_ref, 0)

    def compose_hits(begin_at, end_at):
        def body(i, carry):
            for u in range(DEPTH):
                j = 1 + DEPTH * i + u
                step_maps(lanes, 4, hit_rows(gain_ref, j), hit_rows(resid_ref, j))
            return carry

        lax.fori_loop(begin_at, end_at, body, 0)

    compose_hits(0, 1)

    @pl.when(c == 1)
    def _():
        leave()

    compose_hits(1, (LEN - 1) // DEPTH)

    start = jnp.concatenate([eye, jnp.zeros((16, H), F32)], axis=0)

    def chain(k, carry):
        out = []
        for s in range(2):
            lane = s * chunks + k
            prefix[lane] = carry[s]
            out.append(then(carry[s], maps_ref[lane], offset_of(lane), eye))
        return tuple(out)

    lax.fori_loop(0, chunks, chain, (start, start))

    @pl.when(c == 1)
    def _():
        pass_on()

    block_line = lax.broadcasted_iota(jnp.int32, (TBLK, H), 0)
    map_line = jnp.zeros((AUG, H), jnp.int32)
    for s in range(2):
        for h in range(2):
            n = 2 * s + h
            step = steps_ref[s, h]
            run = jnp.zeros((AUG, H), F32)
            for k in range(blocks):
                run = jnp.where(map_line + step // LEN == k, prefix[s * chunks + h * blocks + k], run)
            base = s * steps + h * TBLK
            here = jnp.where(block_line == step, guess_ref[base:base + TBLK, :], 0.0)
            miss = offs_ref[lanes + n:lanes + n + 1, :] + jnp.sum(here, axis=0, keepdims=True)
            miss = miss - target_ref[n:n + 1, :]
            hit_ref[n] = then(run, maps_ref[lanes + n], jnp.where(first_row, miss, 0.0), eye)
    hit_copy = remote(
        hit_ref.at[pl.ds(2 * other, 2)], hits.at[c], core_send.at[1], core_recv.at[1], sibling
    )
    hit_copy.start()
    hits[c] = hit_ref[pl.ds(2 * c, 2)]

    def back_chain(i, carry):
        k = chunks - 1 - i
        out = []
        for s in range(2):
            lane = s * chunks + k
            suffix[lane] = carry[s]
            turn = weights((maps_ref[lane] - eye).T)
            turned[lane] = turn
            out.append(carry[s] + times(carry[s], turn))
        return tuple(out)

    halfway = lax.fori_loop(0, chunks // 2, back_chain, (eye, eye))

    for copy in other_legs + relays:
        copy.wait_recv()
    size = nz
    while size > 1:
        for k in range(size // 2):
            table = zbuf if size == nz else tree
            ends_at = [tail_of(table[2 * k + i, H:SENT, :]) for i in range(2)]
            left = jnp.concatenate([table[2 * k, :H, :], ends_at[0]], axis=0)
            joined = then(left, table[2 * k + 1, :H, :], ends_at[1], eye)
            if size == 2:
                xbuf[x] = joined
            else:
                tree[k] = joined
        size //= 2
    inner = jnp.logical_and(x > 0, x < nx - 1)

    def x_copy(slot, full, d):
        part = xbuf.at[slot, pl.ds(0, SENT) if full else pl.ds(H, 8)]
        return remote(part, part, xs.at[d - 1], xr.at[d - 1], {"x": lax.rem(x + d, nx)})

    def x_copies(slot, full):
        return [x_copy(slot, full, d) for d in range(1, nx)]

    @pl.when(inner)
    def _():
        for copy in x_copies(x, True):
            copy.start()

    @pl.when(jnp.logical_not(inner))
    def _():
        for copy in x_copies(x, False):
            copy.start()

    run = jnp.concatenate([zbuf[0, :H, :], tail_of(zbuf[0, H:SENT, :])], axis=0)
    ahead = start
    after = eye
    for k in range(1, nz):
        ahead = jnp.where(k == z, run, ahead)
        ubuf[k] = after
        moved = times(jnp.concatenate([run, after], axis=0), weights(zbuf[k, :H, :] - eye))
        offset = tail_of(zbuf[k, H:SENT, :])
        run = run + moved[:AUG] + jnp.concatenate([jnp.zeros((H, H), F32), offset], axis=0)
        after = jnp.where(k > z, after + moved[AUG:], after)
    hit_copy.wait_recv()
    first_map = jnp.concatenate([pair[0, :H, :], tail_of(pair[0, H:SENT, :])], axis=0)
    late = [then(first_map, hits[1, h, :H, :], hits[1, h, H:, :], eye) for h in range(2)]
    w_ahead = weights(ahead[:H] - eye)
    w_first = weights(pair[0, :H, :] - eye)
    w_hits = [weights(hits[0, h, :H, :] - eye) for h in range(2)] + [weights(late[h][:H] - eye) for h in range(2)]
    t_hits = [weights(hits[0, h, :H, :].T) for h in range(2)] + [weights(late[h][:H].T) for h in range(2)]
    t_late = [weights(hits[1, h, :H, :].T) for h in range(2)]
    t_ahead = weights(ahead[:H].T)
    miss_rows = [hits[0, h, H:, :] for h in range(2)] + [late[h][H:] for h in range(2)]

    lax.fori_loop(chunks // 2, chunks, back_chain, halfway)
    for d in range(1, nx):
        source = lax.rem(x + nx - d, nx)
        source_inner = jnp.logical_and(source > 0, source < nx - 1)

        @pl.when(source_inner)
        def _():
            x_copy(source, True, d).wait_recv()

        @pl.when(jnp.logical_not(source_inner))
        def _():
            x_copy(source, False, d).wait_recv()

    v = jnp.where(x > 0, tail_of(xbuf[0, H:SENT, :]), 0.0)
    for k in range(1, nx - 1):
        moved = v + times(v, weights(xbuf[k, :H, :] - eye)) + tail_of(xbuf[k, H:SENT, :])
        v = jnp.where(k < x, moved, v)
    v = v + times(v, w_ahead) + ahead[H:]
    scale = 0.125
    misses = [(v + times(v, w_hits[i]) + miss_rows[i]) * scale for i in range(4)]
    pull = jnp.zeros((16, H), F32)
    for i in range(4):
        pull = pull + times(misses[i], t_hits[i])
    far = times(pull, t_ahead)
    line = lax.broadcasted_iota(jnp.int32, (8, H), 0)
    pulls[chip] = jnp.concatenate([pull[0:1], far[0:1]], axis=0)
    chip_ids = mates((("x", x, nx), ("z", z, nz)))
    pull_copies = [
        remote(pulls.at[chip], pulls.at[chip], pull_send.at[i], pull_recv.at[i], chip_ids[i]) for i in range(chips - 1)
    ]
    for copy in pull_copies:
        copy.start()
    v_late = v + times(v, w_first) + tail_of(pair[0, H:SENT, :])
    ends[0, c] = jnp.where(c == 0, v[:8], v_late[:8])
    tiles[0] = jnp.where(c == 0, v_late[:8], v[:8])
    delta_copy = remote(tiles.at[0], ends.at[0, c], core_send.at[2], core_recv.at[2], sibling)
    delta_copy.start()
    pull_late = times(misses[2], t_late[0]) + times(misses[3], t_late[1])
    delta_copy.wait_recv()

    lane_line = lax.broadcasted_iota(jnp.int32, (lanes, H), 0)
    pushes = jnp.zeros((lanes, H), F32)
    columns_d = [jnp.broadcast_to(ends[0, s, 0:1, :], (H, H)).T for s in range(2)]
    for s in range(2):
        for h in range(2):
            n = 2 * s + h
            step = steps_ref[s, h]
            miss = jnp.sum(hit_ref[n, :H, :] * columns_d[s], axis=0, keepdims=True) + hit_ref[n, H:H + 1, :]
            miss = miss * scale
            source_ref[s * steps + h * TBLK:s * steps + (h + 1) * TBLK, :] = jnp.where(block_line == step, miss, 0.0)
            pushed = times(jnp.broadcast_to(miss, (16, H)), weights(maps_ref[lanes + n].T))
            pushes = pushes + jnp.where(lane_line == s * chunks + h * blocks + step // LEN, pushed[0:1], 0.0)
    push_ref[...] = pushes

    def spread(table, columns, k, s):
        lane = s * chunks + k
        return jnp.sum(table[lane, :H, :] * columns[s], axis=0, keepdims=True)

    def local_back(j, carry):
        k = chunks - 1 - j
        out = []
        for s, t in enumerate(carry):
            lane = s * chunks + k
            carry_ref[pl.ds(lane, 1), :] = t[0:1]
            out.append(t + times(t, turned[lane]) + push_ref[pl.ds(lane, 1), :])
        return tuple(out)

    nothing = jnp.zeros((16, H), F32)
    lax.fori_loop(0, chunks, local_back, (nothing, nothing), unroll=True)
    t_first = weights((pair[1, :H, :] - eye).T)
    t_after = weights((after - eye).T)
    t_rows = {k: weights((xbuf[k, :H, :] - eye).T) for k in range(1, nx - 1)}

    for copy in pull_copies:
        copy.wait_recv()
    total = jnp.zeros((H, H), F32)
    for k in range(1, nz):
        total = total + jnp.where(k > z, ubuf[k] * pulls[x * nz + k, 0:1, :], 0.0)
    near = lane_sum(total)
    row_pulls = []
    for k in range(nx):
        row = pulls[k * nz]
        for i in range(1, nz):
            row = row + pulls[k * nz + i]
        row_pulls.append(row)
    t = jnp.where(nx - 1 > x, jnp.broadcast_to(row_pulls[nx - 1][1:2], (16, H)), 0.0)
    for k in range(nx - 2, 0, -1):
        t = jnp.where(k > x, t + times(t, t_rows[k]) + row_pulls[k][1:2], t)
    lam_late = near + t + times(t, t_after)
    lam = lam_late + times(lam_late, t_first) + pull_late
    ends[1, c] = jnp.where(c == 0, lam[:8], lam_late[:8])
    tiles[1] = jnp.where(c == 0, lam_late[:8], lam[:8])
    lam_copy = remote(tiles.at[1], ends.at[1, c], core_send.at[3], core_recv.at[3], sibling)
    lam_copy.start()
    packed_t = weights(rate_t.T)

    def add_carries(s):
        spread_row = jnp.broadcast_to(ends[1, s, 0:1, :], (H, H)).T

        def body(i, carry):
            for u in range(4):
                lane = s * chunks + 4 * i + u
                rows = pl.ds(lane, 1)
                moved = jnp.sum(suffix[lane] * spread_row, axis=0, keepdims=True)
                carry_ref[rows, :] = carry_ref[rows, :] + moved
            return carry

        lax.fori_loop(0, chunks // 4, body, 0)

    add_carries(c)
    lam_copy.wait_recv()
    add_carries(other)
    def backward(j, adjoint):
        rows = pl.ds(LEN - 1 - j, lanes, stride=LEN)
        adjoint = adjoint + source_ref[rows, :]
        scaled = gain_ref[rows, :] * adjoint
        pre_ref[rows, :] = scaled
        return adjoint + times(scaled, packed_t)

    lax.fori_loop(0, LEN, backward, carry_ref[...], unroll=True)
    left_high, left_low = split(jnp.concatenate([prev_rows([edge[s, 7:8, :] * at_start for s in range(2)]), x_ref[...]], axis=1))
    right = wide(pre_ref[...])
    dims = (((0,), (0,)), ((), ()))
    both = lax.dot_general(left_high, right, dims, preferred_element_type=F32)
    both = both + lax.dot_general(left_low, right, dims, preferred_element_type=F32)
    sums = both[:, :H] + both[:, H:]
    grads[0:H // 8] = (sums[:H].T - sums[:H]).reshape(H // 8, 8, H)
    grads[H // 8:] = sums[H:].reshape(2 * H // 8, 8, H)

    share = grads.shape[0] // plane
    done = []
    for i in range(plane - 1):
        done.append(remote(
            grads.at[pl.ds(planes[i] * share, share)], parts.at[p], send1.at[i], recv1.at[i], plane_ids[i]
        ))
        done[-1].start()
    parts[p] = grads[pl.ds(p * share, share)]

    def starts(k, carry):
        for s in range(2):
            lane = s * chunks + k
            start_ref[pl.ds(lane, 1), :] = spread(prefix, columns_d, k, s) + prefix[lane, H:H + 1, :]
        return carry

    def forward(j, state):
        rows = pl.ds(j, lanes, stride=LEN)
        state = state + gain_ref[rows, :] * times(state, packed) + resid_ref[rows, :]
        traj_ref[rows, :] = state + guess_ref[rows, :]
        return state

    lax.fori_loop(0, chunks, starts, 0)
    lax.fori_loop(0, LEN, forward, start_ref[...], unroll=True)
    for copy in done:
        copy.wait_recv()
    shares[q] = jnp.sum(parts[...], axis=0)
    column_ids = mates((("z", z, nz), ("core", c, nc)))
    exchange = [
        remote(shares.at[q], shares.at[q], send2.at[i], recv2.at[i], column_ids[i]) for i in range(column - 1)
    ]
    for copy in exchange:
        copy.start()
    for copy in exchange:
        copy.wait_recv()
    mine = pl.ds(p * share, share)
    whole[mine] = jnp.sum(shares[...], axis=0)
    last = [
        remote(whole.at[mine], whole.at[mine], send3.at[i], recv3.at[i], plane_ids[i]) for i in range(plane - 1)
    ]
    for copy in last:
        copy.start()

    @pl.when(inner)
    def _():
        for copy in x_copies(x, True):
            copy.wait_send()

    @pl.when(jnp.logical_not(inner))
    def _():
        for copy in x_copies(x, False):
            copy.wait_send()

    early = edge_copies + [core_copy, hit_copy, delta_copy, lam_copy] + first_legs + other_legs + relays + pull_copies
    for copy in early + done + exchange:
        copy.wait_send()
    for copy in last:
        copy.wait_recv()
    for copy in last:
        copy.wait_send()


def deliver(traj_ref, whole_ref, traj_hbm, recur_hbm, gin_hbm, sems):
    rows = recur_hbm.shape[0]
    copies = [
        pltpu.make_async_copy(src, dst, sems.at[i])
        for i, (src, dst) in enumerate((
            (traj_ref, traj_hbm), (whole_ref.at[pl.ds(0, rows)], recur_hbm),
            (whole_ref.at[pl.ds(rows, gin_hbm.shape[0])], gin_hbm),
        ))
    ]
    for copy in copies:
        copy.start()
    for copy in copies:
        copy.wait()


def vmem(*dims):
    return pltpu.VMEM(dims, F32)


def out(*dims):
    return jax.ShapeDtypeStruct(dims, F32)


def on_device(inputs, guess_path, recur_weight, damping, in_weight, bias_term, targets, target_steps):
    seqs, steps, hidden = guess_path.shape
    features = inputs.shape[2]
    count = seqs * steps
    chunks = steps // LEN
    lanes = seqs * chunks
    nx, nz, nc, ny = (lax.axis_size(name) for name in ("x", "z", "core", "batch"))
    plane, column = nx * ny, nz * nc
    tiles = 3 * hidden // 8
    share = tiles // plane
    extra = count + 4 * LEN
    dma = pltpu.SemaphoreType.DMA
    traj, whole = pl.pallas_call(
        newton,
        out_shape=(out(count, hidden), out(tiles, 8, hidden)),
        in_specs=[HBM] * 8,
        out_specs=[VM, VM],
        scratch_shapes=[
            vmem(count, features), vmem(count, hidden), vmem(hidden, hidden), vmem(1, hidden),
            vmem(features, hidden), vmem(1, hidden), vmem(4, hidden), pltpu.SMEM((seqs, 2), jnp.int32), dma((8,)),
            vmem(seqs, 8, hidden), vmem(extra, hidden), vmem(extra, hidden), vmem(lanes + 16, hidden),
            vmem(lanes + 4, hidden, hidden), vmem(chunks // 2, AUG, hidden), vmem(seqs, AUG, hidden),
            vmem(lanes, AUG, hidden), vmem(lanes, hidden, hidden), pltpu.VMEM((lanes, 2 * hidden, 2 * hidden), BF16),
            vmem(2, AUG, hidden), vmem(4, AUG, hidden), vmem(2, 2, AUG, hidden), vmem(nz, AUG, hidden),
            vmem(nz, hidden, hidden), vmem(nx, AUG, hidden), vmem(nx * nz, 2, hidden),
            vmem(2, 8, hidden), vmem(2, seqs, 8, hidden),
            vmem(lanes, hidden), vmem(lanes, hidden), vmem(lanes, hidden), vmem(count, hidden), vmem(count, hidden),
            vmem(tiles, 8, hidden), vmem(plane, share, 8, hidden), vmem(column, share, 8, hidden),
            dma((2,)), dma((2,)), dma((4,)), dma((4,)), dma((nz - 1,)), dma((nz - 1,)), dma((2,)), dma((2,)), dma((nx - 1,)), dma((nx - 1,)),
            dma((nx * nz - 1,)), dma((nx * nz - 1,)),
            dma((plane - 1,)), dma((plane - 1,)), dma((column - 1,)), dma((column - 1,)), dma((plane - 1,)),
            dma((plane - 1,)),
        ],
        compiler_params=pltpu.CompilerParams(
            collective_id=0, has_side_effects=True, vmem_limit_bytes=40 * 1024 * 1024
        ),
        name="newton",
    )(
        *(pltpu.with_memory_space_constraint(value, pltpu.HBM) for value in (
            inputs.reshape(count, features), guess_path.reshape(count, hidden), recur_weight, damping.reshape(1, hidden),
            in_weight, bias_term.reshape(1, hidden), targets.reshape(-1, hidden), target_steps,
        ))
    )
    any_space = pl.BlockSpec(memory_space=pl.ANY)
    traj, grad_recur, grad_in = pl.pallas_call(
        deliver,
        out_shape=(out(count, hidden), out(hidden, hidden), out(features, hidden)),
        in_specs=[VM, VM],
        out_specs=[any_space] * 3,
        scratch_shapes=[dma((3,))],
        compiler_params=pltpu.CompilerParams(vmem_limit_bytes=4 * 1024 * 1024),
        name="deliver",
    )(traj, whole.reshape(3 * hidden, hidden))
    return traj.reshape(guess_path.shape), grad_recur, grad_in


def solution(mesh):
    torus = Mesh(mesh.devices.reshape(4, 8, 2, mesh.shape["batch"]), (*SEQ, "batch"))
    return jax.shard_map(
        on_device,
        mesh=torus,
        in_specs=(
            P("batch", SEQ, None), P("batch", SEQ, None), P(), P(), P(), P(), P("batch", SEQ, None), P("batch", SEQ),
        ),
        out_specs=(P("batch", SEQ, None), P(), P()),
        check_vma=False,
    )
```

```python
import jax
import jax.numpy as jnp
from jax import lax
from jax.experimental import pallas as pl
from jax.experimental.pallas import tpu as pltpu
from jax.sharding import Mesh
from jax.sharding import PartitionSpec as P

H = 128
LEN = 16
TBLK = 128
AUG = 144
SENT = 136
DEPTH = 5
SEQ = ("x", "z", "core")
EULER = 0.02
F32 = jnp.float32
BF16 = jnp.bfloat16
MESH = pl.DeviceIdType.MESH
VM = pl.BlockSpec(memory_space=pltpu.VMEM)
HBM = pl.BlockSpec(memory_space=pltpu.HBM)


def split(value):
    high = value.astype(BF16)
    return high, (value - high.astype(F32)).astype(BF16)


def wide(value):
    return jnp.concatenate(split(value), axis=1)


def weights(matrix):
    row = wide(matrix)
    return jnp.concatenate([row, row], axis=0)


def times(rows, packed):
    both = jnp.dot(wide(rows), packed, preferred_element_type=F32)
    return both[:, :H] + both[:, H:]


def unit():
    line = lax.broadcasted_iota(jnp.int32, (H, H), 0)
    return jnp.where(line == lax.broadcasted_iota(jnp.int32, (H, H), 1), 1.0, 0.0).astype(F32)


def rate_matrix(weight, damping):
    return weight.T - weight - unit() * damping


def shift_down(block, first):
    line = lax.broadcasted_iota(jnp.int32, block.shape, 0)
    return jnp.where(line == 0, first, pltpu.roll(block, 1, 0))


def tail_of(rows):
    return jnp.concatenate([rows, jnp.zeros((8, H), F32)], axis=0)


def then(earlier, later, offset, eye):
    moved = earlier + times(earlier, weights(later - eye))
    return jnp.concatenate([moved[:H], moved[H:] + offset], axis=0)


def remote(src, dst, sends, recvs, target):
    return pltpu.make_async_remote_copy(
        src_ref=src, dst_ref=dst, send_sem=sends, recv_sem=recvs,
        device_id=target, device_id_type=MESH,
    )


def swap_copies(buf, axis, sends, recvs, rows):
    n = lax.axis_size(axis)
    me = lax.axis_index(axis)
    part = buf.at[me, pl.ds(0, rows)]
    farthest_first = sorted(range(1, n), key=lambda d: -min(d, n - d))
    return [
        (d, remote(part, part, sends.at[d - 1], recvs.at[d - 1], {axis: lax.rem(me + d, n)})) for d in farthest_first
    ]


def lane_sum(matrix):
    ones = jnp.ones((16, 2 * H), BF16)
    return lax.dot_general(ones, wide(matrix), (((1,), (1,)), ((), ())), preferred_element_type=F32)


def newton(
    x_hbm, guess_hbm, w_hbm, damp_hbm, u_hbm, bias_hbm, target_hbm, steps_hbm,
    traj_ref, whole,
    x_ref, guess_ref, w_ref, damp_ref, u_ref, bias_ref, target_ref, steps_ref, load_sem,
    edge, gain_ref, resid_ref, offs_ref, maps_ref, tree, totals, prefix, suffix, turned,
    pair, hit_ref, hits, zbuf, ubuf, xbuf, pulls, tiles, ends,
    start_ref, carry_ref, push_ref, source_ref, pre_ref,
    grads, parts, shares,
    edge_send, edge_recv, core_send, core_recv, zs, zr, relay_send, relay_recv, xs, xr, pull_send, pull_recv,
    send1, recv1, send2, recv2, send3, recv3,
):
    x, y, z, c = (lax.axis_index(name) for name in ("x", "batch", "z", "core"))
    nx, ny, nz, nc = (lax.axis_size(name) for name in ("x", "batch", "z", "core"))
    count = guess_ref.shape[0]
    steps = count // 2
    chunks = steps // LEN
    lanes = 2 * chunks
    blocks = TBLK // LEN

    loads = [
        pltpu.make_async_copy(src, dst, load_sem.at[i])
        for i, (src, dst) in enumerate((
            (w_hbm, w_ref), (damp_hbm, damp_ref), (guess_hbm, guess_ref), (u_hbm, u_ref), (x_hbm, x_ref),
            (bias_hbm, bias_ref), (target_hbm, target_ref), (steps_hbm, steps_ref),
        ))
    ]
    for load in loads:
        load.start()

    other = 1 - c
    sibling = {"core": other}
    plane, column = nx * ny, nz * nc
    p = x * ny + y
    q = z * nc + c

    def mates(axes):
        (one, here, first), (two, there, second) = axes
        offsets = [(i, j) for i in range(first) for j in range(second) if i or j]
        offsets.sort(key=lambda o: -min(o[0], first - o[0]) - (0 if two == "core" else min(o[1], second - o[1])))
        return [{one: lax.rem(here + i, first), two: lax.rem(there + j, second)} for i, j in offsets]

    plane_ids = mates((("x", x, nx), ("batch", y, ny)))
    planes = [mate["x"] * ny + mate["batch"] for mate in plane_ids]
    place = x * column + q

    def along(where):
        return {"x": where // column, "z": lax.rem(where // nc, nz), "core": lax.rem(where, nc)}

    following = along(lax.rem(place + 1, nx * column))
    preceding = along(lax.rem(place + nx * column - 1, nx * column))
    barrier = pltpu.get_barrier_semaphore()
    chips = nx * nz
    chip = x * nz + z
    z_ids = [{"z": lax.rem(z + d, nz)} for d in range(1, nz)]
    greeted = plane_ids + z_ids + [sibling, following, preceding]

    eye = unit()
    loads[0].wait()
    loads[1].wait()
    rate_t = rate_matrix(w_ref[...], damp_ref[...])
    packed = weights(rate_t)
    for load in loads[2:]:
        load.wait()
    for target in greeted:
        pl.semaphore_signal(barrier, inc=1, device_id=target, device_id_type=MESH)
    guess = guess_ref[...]

    def prev_rows(firsts):
        return jnp.concatenate(
            [shift_down(guess_ref[s * steps:(s + 1) * steps, :], firsts[s]) for s in range(2)], axis=0
        )

    zero_row = jnp.zeros((1, H), F32)
    u_pair = wide(u_ref[...])
    x_high, x_low = split(x_ref[...])
    drive = jnp.dot(x_high, u_pair, preferred_element_type=F32)
    drive = drive + jnp.dot(x_low, u_pair, preferred_element_type=F32)
    prev = prev_rows([zero_row, zero_row])
    preact = times(prev, packed) + drive[:, :H] + drive[:, H:] + bias_ref[...]
    activation = jnp.tanh(preact)
    gain_ref[0:count, :] = EULER * (1.0 - activation * activation)
    resid_ref[0:count, :] = prev + EULER * activation - guess
    early_preact = [preact[s * steps:s * steps + 1] for s in range(2)]

    edge_copies = [
        remote(guess_ref.at[pl.ds((s + 1) * steps - 8, 8)], edge.at[s], edge_send.at[s], edge_recv.at[s], following)
        for s in range(2)
    ]
    chunk_line = lax.broadcasted_iota(jnp.int32, (LEN, H), 0)

    def begin(s):
        gains = jnp.where(chunk_line == 0, 0.0, gain_ref[pl.ds(s * steps, chunks, stride=LEN), :])
        for k in range(chunks):
            maps_ref[s * chunks + k] = eye + rate_t * gains[k:k + 1]
        offs_ref[s * chunks:(s + 1) * chunks, :] = jnp.where(
            chunk_line == 0, 0.0, resid_ref[pl.ds(s * steps, chunks, stride=LEN), :]
        )

    def step_maps(base, size, gains, resid):
        for first in range(0, size, 4):
            state = maps_ref[base + first:base + first + 4].reshape(4 * H, H)
            if first + 4 == size:
                state = jnp.concatenate([state, offs_ref[base:base + 16, :]], axis=0)
            moved = times(state, packed)
            for i in range(4):
                here = slice(i * H, (i + 1) * H)
                maps_ref[base + first + i] = state[here] + gains[first + i:first + i + 1] * moved[here]
            if first + 4 == size:
                offs_ref[base:base + 16, :] = state[4 * H:] + gains * moved[4 * H:] + resid

    def compose(s, begin_at, end_at):
        def body(i, carry):
            for u in range(DEPTH):
                j = 1 + DEPTH * i + u
                rows = pl.ds(s * steps + j, chunks, stride=LEN)
                step_maps(s * chunks, chunks, gain_ref[rows, :], resid_ref[rows, :])
            return carry

        lax.fori_loop(begin_at, end_at, body, 0)

    first_row = chunk_line == 0

    def offset_of(lane):
        return jnp.where(first_row, offs_ref[pl.ds(lane, 1), :], 0.0)

    def lane_rows(lane):
        return jnp.concatenate([maps_ref[lane], offset_of(lane)], axis=0)

    def finish(s):
        lane = s * chunks
        gain = gain_ref[s * steps:s * steps + 1, :]
        resid = jnp.where(first_row, resid_ref[s * steps:s * steps + 1, :], 0.0)
        step = jnp.concatenate([eye + rate_t * gain, resid], axis=0)
        whole_chunk = then(step, maps_ref[lane], offset_of(lane), eye)
        maps_ref[lane] = whole_chunk[:H]
        offs_ref[lane:lane + 1, :] = whole_chunk[H:H + 1]
        for k in range(chunks // 2):
            tree[k] = then(lane_rows(lane + 2 * k), maps_ref[lane + 2 * k + 1], offset_of(lane + 2 * k + 1), eye)
        size = chunks // 2
        while size > 1:
            for k in range(size // 2):
                joined = then(tree[2 * k], tree[2 * k + 1, :H, :], tree[2 * k + 1, H:, :], eye)
                if size == 2:
                    totals[s] = joined
                else:
                    tree[k] = joined
            size //= 2

    core_copy = remote(
        totals.at[other, pl.ds(0, SENT)], pair.at[c, pl.ds(0, SENT)], core_send.at[0], core_recv.at[0], sibling
    )
    quarter = nz // 4
    pieces = (pl.ds(0, 72), pl.ds(72, SENT - 72))
    relays = []
    for i, (toward, piece) in enumerate(zip((quarter, nz - quarter), pieces)):
        part = zbuf.at[lax.rem(z + nz - toward, nz), piece]
        relays.append(remote(part, part, relay_send.at[i], relay_recv.at[i], {"z": lax.rem(z + toward, nz)}))
    first_legs = [copy for d, copy in swap_copies(zbuf, "z", zs, zr, SENT) if d in (quarter, nz - quarter)]
    other_legs = [copy for d, copy in swap_copies(zbuf, "z", zs, zr, SENT) if d not in (quarter, nz // 2, nz - quarter)]

    def pass_on():
        for copy in first_legs:
            copy.wait_recv()
        for copy in relays:
            copy.start()

    def leave():
        core_copy.wait_recv()
        pair[c] = totals[c]
        zbuf[z] = then(
            jnp.concatenate([pair[0, :H, :], tail_of(pair[0, H:SENT, :])], axis=0),
            pair[1, :H, :], tail_of(pair[1, H:SENT, :]), eye,
        )
        for copy in first_legs + other_legs:
            copy.start()

    begin(0)
    compose(0, 0, 2)
    pl.semaphore_wait(barrier, len(greeted))
    for copy in edge_copies:
        copy.start()
    compose(0, 2, (LEN - 1) // DEPTH)
    begin(1)
    for copy in edge_copies:
        copy.wait_recv()
    at_start = jnp.where(place > 0, 1.0, 0.0)
    firsts = [edge[s, 7:8, :] * at_start for s in range(2)]
    added = times(jnp.concatenate(firsts + [jnp.zeros((14, H), F32)], axis=0), packed)
    for s in range(2):
        row = slice(s * steps, s * steps + 1)
        activation = jnp.tanh(early_preact[s] + added[s:s + 1])
        gain_ref[row, :] = EULER * (1.0 - activation * activation)
        resid_ref[row, :] = firsts[s] + EULER * activation - guess_ref[row, :]
    finish(0)

    @pl.when(c == 1)
    def _():
        core_copy.start()

    compose(1, 0, 1)

    @pl.when(c == 0)
    def _():
        leave()

    compose(1, 1, (LEN - 1) // DEPTH)
    finish(1)

    @pl.when(c == 0)
    def _():
        core_copy.start()
        pass_on()

    for s in range(2):
        for h in range(2):
            n = 2 * s + h
            step = steps_ref[s, h]
            kept = chunk_line <= lax.rem(step, LEN)
            to = slice(count + n * LEN, count + (n + 1) * LEN)
            for ref in (gain_ref, resid_ref):
                rows = jnp.zeros((LEN, H), F32)
                for k in range(blocks):
                    base = s * steps + h * TBLK + k * LEN
                    rows = jnp.where(chunk_line * 0 + step // LEN == k, ref[base:base + LEN, :], rows)
                ref[to, :] = jnp.where(kept, rows, 0.0)
    hit_pad = jnp.zeros((12, H), F32)

    def hit_rows(ref, j):
        return jnp.concatenate([ref[pl.ds(count + j, 4, stride=LEN), :], hit_pad], axis=0)

    gains = hit_rows(gain_ref, 0)
    for n in range(4):
        maps_ref[lanes + n] = eye + rate_t * gains[n:n + 1]
    offs_ref[lanes:lanes + 16, :] = hit_rows(resid_ref, 0)

    def compose_hits(begin_at, end_at):
        def body(i, carry):
            for u in range(DEPTH):
                j = 1 + DEPTH * i + u
                step_maps(lanes, 4, hit_rows(gain_ref, j), hit_rows(resid_ref, j))
            return carry

        lax.fori_loop(begin_at, end_at, body, 0)

    compose_hits(0, 1)

    @pl.when(c == 1)
    def _():
        leave()

    compose_hits(1, (LEN - 1) // DEPTH)

    start = jnp.concatenate([eye, jnp.zeros((16, H), F32)], axis=0)

    def chain(k, carry):
        out = []
        for s in range(2):
            lane = s * chunks + k
            prefix[lane] = carry[s]
            out.append(then(carry[s], maps_ref[lane], offset_of(lane), eye))
        return tuple(out)

    middle = lax.fori_loop(0, chunks // 2, chain, (start, start))

    @pl.when(c == 1)
    def _():
        pass_on()

    lax.fori_loop(chunks // 2, chunks, chain, middle)

    block_line = lax.broadcasted_iota(jnp.int32, (TBLK, H), 0)
    map_line = jnp.zeros((AUG, H), jnp.int32)
    for s in range(2):
        for h in range(2):
            n = 2 * s + h
            step = steps_ref[s, h]
            run = jnp.zeros((AUG, H), F32)
            for k in range(blocks):
                run = jnp.where(map_line + step // LEN == k, prefix[s * chunks + h * blocks + k], run)
            base = s * steps + h * TBLK
            here = jnp.where(block_line == step, guess_ref[base:base + TBLK, :], 0.0)
            miss = offs_ref[lanes + n:lanes + n + 1, :] + jnp.sum(here, axis=0, keepdims=True)
            miss = miss - target_ref[n:n + 1, :]
            hit_ref[n] = then(run, maps_ref[lanes + n], jnp.where(first_row, miss, 0.0), eye)
    hit_copy = remote(
        hit_ref.at[pl.ds(2 * other, 2)], hits.at[c], core_send.at[1], core_recv.at[1], sibling
    )
    hit_copy.start()
    hits[c] = hit_ref[pl.ds(2 * c, 2)]

    def back_chain(i, carry):
        k = chunks - 1 - i
        out = []
        for s in range(2):
            lane = s * chunks + k
            suffix[lane] = carry[s]
            turn = weights((maps_ref[lane] - eye).T)
            turned[lane] = turn
            out.append(carry[s] + times(carry[s], turn))
        return tuple(out)

    partway = lax.fori_loop(0, 3 * chunks // 8, back_chain, (eye, eye))

    for copy in other_legs + relays:
        copy.wait_recv()
    size = nz
    while size > 1:
        for k in range(size // 2):
            table = zbuf if size == nz else tree
            ends_at = [tail_of(table[2 * k + i, H:SENT, :]) for i in range(2)]
            left = jnp.concatenate([table[2 * k, :H, :], ends_at[0]], axis=0)
            joined = then(left, table[2 * k + 1, :H, :], ends_at[1], eye)
            if size == 2:
                xbuf[x] = joined
            else:
                tree[k] = joined
        size //= 2
    inner = jnp.logical_and(x > 0, x < nx - 1)

    def x_copy(slot, full, d):
        part = xbuf.at[slot, pl.ds(0, SENT) if full else pl.ds(H, 8)]
        return remote(part, part, xs.at[d - 1], xr.at[d - 1], {"x": lax.rem(x + d, nx)})

    def x_copies(slot, full):
        return [x_copy(slot, full, d) for d in range(1, nx)]

    @pl.when(inner)
    def _():
        for copy in x_copies(x, True):
            copy.start()

    @pl.when(jnp.logical_not(inner))
    def _():
        for copy in x_copies(x, False):
            copy.start()

    run = jnp.concatenate([zbuf[0, :H, :], tail_of(zbuf[0, H:SENT, :])], axis=0)
    ahead = start
    after = eye
    for k in range(1, nz):
        ahead = jnp.where(k == z, run, ahead)
        ubuf[k] = after
        moved = times(jnp.concatenate([run, after], axis=0), weights(zbuf[k, :H, :] - eye))
        offset = tail_of(zbuf[k, H:SENT, :])
        run = run + moved[:AUG] + jnp.concatenate([jnp.zeros((H, H), F32), offset], axis=0)
        after = jnp.where(k > z, after + moved[AUG:], after)
    hit_copy.wait_recv()
    first_map = jnp.concatenate([pair[0, :H, :], tail_of(pair[0, H:SENT, :])], axis=0)
    late = [then(first_map, hits[1, h, :H, :], hits[1, h, H:, :], eye) for h in range(2)]
    w_ahead = weights(ahead[:H] - eye)
    w_first = weights(pair[0, :H, :] - eye)
    w_hits = [weights(hits[0, h, :H, :] - eye) for h in range(2)] + [weights(late[h][:H] - eye) for h in range(2)]
    t_hits = [weights(hits[0, h, :H, :].T) for h in range(2)] + [weights(late[h][:H].T) for h in range(2)]
    t_late = [weights(hits[1, h, :H, :].T) for h in range(2)]
    t_ahead = weights(ahead[:H].T)
    miss_rows = [hits[0, h, H:, :] for h in range(2)] + [late[h][H:] for h in range(2)]

    lax.fori_loop(3 * chunks // 8, chunks, back_chain, partway)
    for d in range(1, nx):
        source = lax.rem(x + nx - d, nx)
        source_inner = jnp.logical_and(source > 0, source < nx - 1)

        @pl.when(source_inner)
        def _():
            x_copy(source, True, d).wait_recv()

        @pl.when(jnp.logical_not(source_inner))
        def _():
            x_copy(source, False, d).wait_recv()

    v = jnp.where(x > 0, tail_of(xbuf[0, H:SENT, :]), 0.0)
    for k in range(1, nx - 1):
        moved = v + times(v, weights(xbuf[k, :H, :] - eye)) + tail_of(xbuf[k, H:SENT, :])
        v = jnp.where(k < x, moved, v)
    v = v + times(v, w_ahead) + ahead[H:]
    scale = 0.125
    misses = [(v + times(v, w_hits[i]) + miss_rows[i]) * scale for i in range(4)]
    pull = jnp.zeros((16, H), F32)
    for i in range(4):
        pull = pull + times(misses[i], t_hits[i])
    far = times(pull, t_ahead)
    line = lax.broadcasted_iota(jnp.int32, (8, H), 0)
    pulls[chip] = jnp.concatenate([pull[0:1], far[0:1]], axis=0)
    chip_ids = mates((("x", x, nx), ("z", z, nz)))
    pull_copies = [
        remote(pulls.at[chip], pulls.at[chip], pull_send.at[i], pull_recv.at[i], chip_ids[i]) for i in range(chips - 1)
    ]
    for copy in pull_copies:
        copy.start()
    v_late = v + times(v, w_first) + tail_of(pair[0, H:SENT, :])
    ends[0, c] = jnp.where(c == 0, v[:8], v_late[:8])
    tiles[0] = jnp.where(c == 0, v_late[:8], v[:8])
    delta_copy = remote(tiles.at[0], ends.at[0, c], core_send.at[2], core_recv.at[2], sibling)
    delta_copy.start()
    pull_late = times(misses[2], t_late[0]) + times(misses[3], t_late[1])
    delta_copy.wait_recv()

    lane_line = lax.broadcasted_iota(jnp.int32, (lanes, H), 0)
    pushes = jnp.zeros((lanes, H), F32)
    columns_d = [jnp.broadcast_to(ends[0, s, 0:1, :], (H, H)).T for s in range(2)]
    for s in range(2):
        for h in range(2):
            n = 2 * s + h
            step = steps_ref[s, h]
            miss = jnp.sum(hit_ref[n, :H, :] * columns_d[s], axis=0, keepdims=True) + hit_ref[n, H:H + 1, :]
            miss = miss * scale
            source_ref[s * steps + h * TBLK:s * steps + (h + 1) * TBLK, :] = jnp.where(block_line == step, miss, 0.0)
            pushed = times(jnp.broadcast_to(miss, (16, H)), weights(maps_ref[lanes + n].T))
            pushes = pushes + jnp.where(lane_line == s * chunks + h * blocks + step // LEN, pushed[0:1], 0.0)
    push_ref[...] = pushes

    def spread(table, columns, k, s):
        lane = s * chunks + k
        return jnp.sum(table[lane, :H, :] * columns[s], axis=0, keepdims=True)

    def local_back(j, carry):
        k = chunks - 1 - j
        out = []
        for s, t in enumerate(carry):
            lane = s * chunks + k
            carry_ref[pl.ds(lane, 1), :] = t[0:1]
            out.append(t + times(t, turned[lane]) + push_ref[pl.ds(lane, 1), :])
        return tuple(out)

    nothing = jnp.zeros((16, H), F32)
    lax.fori_loop(0, chunks, local_back, (nothing, nothing), unroll=True)
    t_first = weights((pair[1, :H, :] - eye).T)
    t_after = weights((after - eye).T)
    t_rows = {k: weights((xbuf[k, :H, :] - eye).T) for k in range(1, nx - 1)}

    for copy in pull_copies:
        copy.wait_recv()
    total = jnp.zeros((H, H), F32)
    for k in range(1, nz):
        total = total + jnp.where(k > z, ubuf[k] * pulls[x * nz + k, 0:1, :], 0.0)
    near = lane_sum(total)
    row_pulls = []
    for k in range(nx):
        row = pulls[k * nz]
        for i in range(1, nz):
            row = row + pulls[k * nz + i]
        row_pulls.append(row)
    t = jnp.where(nx - 1 > x, jnp.broadcast_to(row_pulls[nx - 1][1:2], (16, H)), 0.0)
    for k in range(nx - 2, 0, -1):
        t = jnp.where(k > x, t + times(t, t_rows[k]) + row_pulls[k][1:2], t)
    lam_late = near + t + times(t, t_after)
    lam = lam_late + times(lam_late, t_first) + pull_late
    ends[1, c] = jnp.where(c == 0, lam[:8], lam_late[:8])
    tiles[1] = jnp.where(c == 0, lam_late[:8], lam[:8])
    lam_copy = remote(tiles.at[1], ends.at[1, c], core_send.at[3], core_recv.at[3], sibling)
    lam_copy.start()
    packed_t = weights(rate_t.T)

    def add_carries(s):
        spread_row = jnp.broadcast_to(ends[1, s, 0:1, :], (H, H)).T

        def body(i, carry):
            for u in range(4):
                lane = s * chunks + 4 * i + u
                rows = pl.ds(lane, 1)
                moved = jnp.sum(suffix[lane] * spread_row, axis=0, keepdims=True)
                carry_ref[rows, :] = carry_ref[rows, :] + moved
            return carry

        lax.fori_loop(0, chunks // 4, body, 0)

    add_carries(c)
    lam_copy.wait_recv()
    add_carries(other)
    def backward(j, adjoint):
        rows = pl.ds(LEN - 1 - j, lanes, stride=LEN)
        adjoint = adjoint + source_ref[rows, :]
        scaled = gain_ref[rows, :] * adjoint
        pre_ref[rows, :] = scaled
        return adjoint + times(scaled, packed_t)

    lax.fori_loop(0, LEN, backward, carry_ref[...], unroll=True)
    left_high, left_low = split(jnp.concatenate([prev_rows([edge[s, 7:8, :] * at_start for s in range(2)]), x_ref[...]], axis=1))
    right = wide(pre_ref[...])
    dims = (((0,), (0,)), ((), ()))
    both = lax.dot_general(left_high, right, dims, preferred_element_type=F32)
    both = both + lax.dot_general(left_low, right, dims, preferred_element_type=F32)
    sums = both[:, :H] + both[:, H:]
    grads[0:H // 8] = (sums[:H].T - sums[:H]).reshape(H // 8, 8, H)
    grads[H // 8:] = sums[H:].reshape(2 * H // 8, 8, H)

    share = grads.shape[0] // plane
    done = []
    for i in range(plane - 1):
        done.append(remote(
            grads.at[pl.ds(planes[i] * share, share)], parts.at[p], send1.at[i], recv1.at[i], plane_ids[i]
        ))
        done[-1].start()
    parts[p] = grads[pl.ds(p * share, share)]

    def starts(k, carry):
        for s in range(2):
            lane = s * chunks + k
            start_ref[pl.ds(lane, 1), :] = spread(prefix, columns_d, k, s) + prefix[lane, H:H + 1, :]
        return carry

    def forward(j, state):
        rows = pl.ds(j, lanes, stride=LEN)
        state = state + gain_ref[rows, :] * times(state, packed) + resid_ref[rows, :]
        traj_ref[rows, :] = state + guess_ref[rows, :]
        return state

    lax.fori_loop(0, chunks, starts, 0)
    lax.fori_loop(0, LEN, forward, start_ref[...], unroll=True)
    for copy in done:
        copy.wait_recv()
    shares[q] = jnp.sum(parts[...], axis=0)
    column_ids = mates((("z", z, nz), ("core", c, nc)))
    exchange = [
        remote(shares.at[q], shares.at[q], send2.at[i], recv2.at[i], column_ids[i]) for i in range(column - 1)
    ]
    for copy in exchange:
        copy.start()
    for copy in exchange:
        copy.wait_recv()
    mine = pl.ds(p * share, share)
    whole[mine] = jnp.sum(shares[...], axis=0)
    last = [
        remote(whole.at[mine], whole.at[mine], send3.at[i], recv3.at[i], plane_ids[i]) for i in range(plane - 1)
    ]
    for copy in last:
        copy.start()

    @pl.when(inner)
    def _():
        for copy in x_copies(x, True):
            copy.wait_send()

    @pl.when(jnp.logical_not(inner))
    def _():
        for copy in x_copies(x, False):
            copy.wait_send()

    early = edge_copies + [core_copy, hit_copy, delta_copy, lam_copy] + first_legs + other_legs + relays + pull_copies
    for copy in early + done + exchange:
        copy.wait_send()
    for copy in last:
        copy.wait_recv()
    for copy in last:
        copy.wait_send()


def deliver(traj_ref, whole_ref, traj_hbm, recur_hbm, gin_hbm, sems):
    rows = recur_hbm.shape[0]
    copies = [
        pltpu.make_async_copy(src, dst, sems.at[i])
        for i, (src, dst) in enumerate((
            (traj_ref, traj_hbm), (whole_ref.at[pl.ds(0, rows)], recur_hbm),
            (whole_ref.at[pl.ds(rows, gin_hbm.shape[0])], gin_hbm),
        ))
    ]
    for copy in copies:
        copy.start()
    for copy in copies:
        copy.wait()


def vmem(*dims):
    return pltpu.VMEM(dims, F32)


def out(*dims):
    return jax.ShapeDtypeStruct(dims, F32)


def on_device(inputs, guess_path, recur_weight, damping, in_weight, bias_term, targets, target_steps):
    seqs, steps, hidden = guess_path.shape
    features = inputs.shape[2]
    count = seqs * steps
    chunks = steps // LEN
    lanes = seqs * chunks
    nx, nz, nc, ny = (lax.axis_size(name) for name in ("x", "z", "core", "batch"))
    plane, column = nx * ny, nz * nc
    tiles = 3 * hidden // 8
    share = tiles // plane
    extra = count + 4 * LEN
    dma = pltpu.SemaphoreType.DMA
    traj, whole = pl.pallas_call(
        newton,
        out_shape=(out(count, hidden), out(tiles, 8, hidden)),
        in_specs=[HBM] * 8,
        out_specs=[VM, VM],
        scratch_shapes=[
            vmem(count, features), vmem(count, hidden), vmem(hidden, hidden), vmem(1, hidden),
            vmem(features, hidden), vmem(1, hidden), vmem(4, hidden), pltpu.SMEM((seqs, 2), jnp.int32), dma((8,)),
            vmem(seqs, 8, hidden), vmem(extra, hidden), vmem(extra, hidden), vmem(lanes + 16, hidden),
            vmem(lanes + 4, hidden, hidden), vmem(chunks // 2, AUG, hidden), vmem(seqs, AUG, hidden),
            vmem(lanes, AUG, hidden), vmem(lanes, hidden, hidden), pltpu.VMEM((lanes, 2 * hidden, 2 * hidden), BF16),
            vmem(2, AUG, hidden), vmem(4, AUG, hidden), vmem(2, 2, AUG, hidden), vmem(nz, AUG, hidden),
            vmem(nz, hidden, hidden), vmem(nx, AUG, hidden), vmem(nx * nz, 2, hidden),
            vmem(2, 8, hidden), vmem(2, seqs, 8, hidden),
            vmem(lanes, hidden), vmem(lanes, hidden), vmem(lanes, hidden), vmem(count, hidden), vmem(count, hidden),
            vmem(tiles, 8, hidden), vmem(plane, share, 8, hidden), vmem(column, share, 8, hidden),
            dma((2,)), dma((2,)), dma((4,)), dma((4,)), dma((nz - 1,)), dma((nz - 1,)), dma((2,)), dma((2,)), dma((nx - 1,)), dma((nx - 1,)),
            dma((nx * nz - 1,)), dma((nx * nz - 1,)),
            dma((plane - 1,)), dma((plane - 1,)), dma((column - 1,)), dma((column - 1,)), dma((plane - 1,)),
            dma((plane - 1,)),
        ],
        compiler_params=pltpu.CompilerParams(
            collective_id=0, has_side_effects=True, vmem_limit_bytes=40 * 1024 * 1024
        ),
        name="newton",
    )(
        *(pltpu.with_memory_space_constraint(value, pltpu.HBM) for value in (
            inputs.reshape(count, features), guess_path.reshape(count, hidden), recur_weight, damping.reshape(1, hidden),
            in_weight, bias_term.reshape(1, hidden), targets.reshape(-1, hidden), target_steps,
        ))
    )
    any_space = pl.BlockSpec(memory_space=pl.ANY)
    traj, grad_recur, grad_in = pl.pallas_call(
        deliver,
        out_shape=(out(count, hidden), out(hidden, hidden), out(features, hidden)),
        in_specs=[VM, VM],
        out_specs=[any_space] * 3,
        scratch_shapes=[dma((3,))],
        compiler_params=pltpu.CompilerParams(vmem_limit_bytes=4 * 1024 * 1024),
        name="deliver",
    )(traj, whole.reshape(3 * hidden, hidden))
    return traj.reshape(guess_path.shape), grad_recur, grad_in


def solution(mesh):
    torus = Mesh(mesh.devices.reshape(4, 8, 2, mesh.shape["batch"]), (*SEQ, "batch"))
    return jax.shard_map(
        on_device,
        mesh=torus,
        in_specs=(
            P("batch", SEQ, None), P("batch", SEQ, None), P(), P(), P(), P(), P("batch", SEQ, None), P("batch", SEQ),
        ),
        out_specs=(P("batch", SEQ, None), P(), P()),
        check_vma=False,
    )
```
